32 devices in a mesh: dp: 16 (over z, x, core), inner: 2 (over y).
Axes of the slice: x: 2, y: 2, z: 4, core: 2. Of those that a mesh axis runs over, the one named last changes fastest.
Arguments:
- tokens: bfloat16 [65536, 768], P(('dp', 'inner')), may hold values from -6 to 6
- weight_qkv: bfloat16 [768, 2304], P(('dp', 'inner')), may hold values from -0.21875 to 0.21875
- bias_qv: bfloat16 [1536], P(('dp', 'inner')), may hold values from -1.1953125 to 1.1953125
- weight_out: bfloat16 [768, 768], P(('dp', 'inner')), may hold values from -1 to 1
- bias_out: bfloat16 [768], P(('dp', 'inner')), may hold values from -1.1953125 to 1.1953125
- gain_one: bfloat16 [768], P(('dp', 'inner')), may hold values from 0.5 to 1.5
- shift_one: bfloat16 [768], P(('dp', 'inner')), may hold values from -1.1953125 to 1.1953125
- weight_in: bfloat16 [768, 3072], P(('dp', 'inner')), may hold values from -0.21875 to 0.21875
- bias_in: bfloat16 [3072], P(('dp', 'inner')), may hold values from -1.1953125 to 1.1953125
- weight_fin: bfloat16 [3072, 768], P(('dp', 'inner')), may hold values from -0.109375 to 0.109375
- bias_fin: bfloat16 [768], P(('dp', 'inner')), may hold values from -1.1953125 to 1.1953125
- gain_two: bfloat16 [768], P(('dp', 'inner')), may hold values from 0.5 to 1.5
- shift_two: bfloat16 [768], P(('dp', 'inner')), may hold values from -1.1953125 to 1.1953125
- segments: int32 [128, 512], P(('dp', 'inner')), may hold values from 0 to 7, never falling along the last dimension, each value on 1 to 128 neighbouring positions
- cotangent: bfloat16 [65536, 768], P(('dp', 'inner')), may hold values from -6 to 6
Outputs:
- output: bfloat16 [65536, 768], P(('dp', 'inner'))
- grad_tokens: float32 [65536, 768], P(('dp', 'inner'))
- grad_weight_qkv: float32 [768, 2304], P(('dp', 'inner'))
- grad_bias_qv: float32 [1536], P(('dp', 'inner'))
- grad_weight_out: float32 [768, 768], P(('dp', 'inner'))
- grad_bias_out: float32 [768], P(('dp', 'inner'))
- grad_gain_one: float32 [768], P(('dp', 'inner'))
- grad_shift_one: float32 [768], P(('dp', 'inner'))
- grad_weight_in: float32 [768, 3072], P(('dp', 'inner'))
- grad_bias_in: float32 [3072], P(('dp', 'inner'))
- grad_weight_fin: float32 [3072, 768], P(('dp', 'inner'))
- grad_bias_fin: float32 [768], P(('dp', 'inner'))
- grad_gain_two: float32 [768], P(('dp', 'inner'))
- grad_shift_two: float32 [768], P(('dp', 'inner'))
The draws below stay inside these ranges and needn't reach their ends.
Inputs may be any that keep to these rules, and one draw needn't show every extreme that they name: `segments`: along each row the pair number never falls; each of the 8 pairs has 1 to 128 tokens, and some pair has exactly 128.
All inputs are finite; a program needn't handle non-finite values.
Results may differ from the reference program's by a relative error of at most 0.013.
Values may be sent and summed in bfloat16 or wider, within the bound.
A program may use at most 256 MiB of HBM per device.

```python
import math
import jax
import jax.numpy as jnp
import numpy as np
from jax import lax

D = 768
HEADS = 12
HEAD_DIM = 64
FF = 3072
SEQ_LEN = 512
PAIRS = 8
MOST_SEG = 128
SEQS = 128
TOKENS = 65536


def strengthened(entries, own_key, source, target, shards_of, factor):
    def block_of(position):
        return (jnp.arange(entries.shape[position]) // (entries.shape[position] // shards_of)).reshape((-1,) + (1,) * (entries.ndim - 1 - position))

    one_side = jax.random.permutation(own_key, shards_of)[block_of(target)]
    far = (block_of(target) + shards_of // 2) % shards_of
    return jnp.where((block_of(source) == one_side) | (block_of(source) == far), factor * entries, entries)


def block_levels(stream_key, shape, shards, smallest, largest):
    factor_of = 1.0
    for position, parts in shards:
        steps = jax.random.uniform(jax.random.fold_in(jax.random.fold_in(stream_key, 6), position), (parts,), jnp.float32, smallest / len(shards), largest / len(shards))
        factor_of = factor_of * jnp.repeat(jnp.exp(steps), shape[position] // parts).reshape((-1,) + (1,) * (len(shape) - 1 - position))
    return factor_of


def profile(amount, total, reach, slope):
    loads = [(1 << 20) // math.isqrt(grade ** slope) + 1 for grade in range(2, amount + 1)]
    rest, given = total - reach - (amount - 1), [1] * (amount - 1)
    while rest > 0:
        free = [i for i in range(amount - 1) if given[i] < reach]
        mass, remaining = sum([loads[i] for i in free]), rest
        for i in free:
            more = min(reach - given[i], max(1, remaining * loads[i] // mass), rest)
            given[i] = given[i] + more
            rest = rest - more
    return np.array([reach] + given)


def ragged(key, amount, total, limit, lean):
    if amount == 2:
        one = jax.random.randint(key, (), max(1, total - limit), min(limit, total - 1) + 1)
        return jnp.stack([one, total - one])
    lengths = jnp.asarray(profile(amount, total, limit, lean), jnp.int32)
    pairs = (amount - 1) // 2
    donor, taker = lengths[1:1 + 2 * pairs:2], lengths[2:2 + 2 * pairs:2]
    room = jnp.minimum(donor - 1, limit - taker)
    moved = jax.random.randint(jax.random.fold_in(key, 1), (pairs,), 0, 1 << 20) % (room + 1)
    lengths = lengths.at[1:1 + 2 * pairs:2].set(donor - moved).at[2:2 + 2 * pairs:2].set(taker + moved)
    return lengths[jax.random.permutation(jax.random.fold_in(key, 2), amount)]


def gaussian(own_key, extent, spread, reach, shards=(), kind=jnp.bfloat16):
    drawn = jax.random.normal(own_key, extent, jnp.float32) * spread
    if len(shards) > 0:
        drawn = block_levels(own_key, extent, shards, -0.22, 0.18) * drawn
    return jnp.clip(drawn, min=-reach, max=reach).astype(kind)


def bell_draw_with(key, dims, width, bound, pieces, heavy, held_as=jnp.bfloat16):
    values = width * jax.random.normal(key, dims, jnp.float32)
    if pieces:
        values = values * block_levels(key, dims, pieces, -0.22, 0.18)
    return jnp.clip(strengthened(values, jax.random.fold_in(key, 3), *heavy), -bound, bound).astype(held_as)


def setup_inputs(seed: int = 0) -> dict:
    seeds = jax.random.split(jax.random.key(seed), 16)
    return {
        "tokens": gaussian(seeds[0], (TOKENS, D), 1.0, 6.0, ((0, 32),)),
        "weight_qkv": gaussian(seeds[1], (D, 3 * D), D ** -0.5, 0.21875, ((0, 32),)),
        "bias_qv": gaussian(seeds[2], (2 * D,), 0.2, 1.1953125, ((0, 32),)),
        "weight_out": gaussian(seeds[3], (D, D), (D // 24) ** -0.5, 1.0, ((0, 32),)),
        "bias_out": gaussian(seeds[4], (D,), 0.2, 1.1953125, ((0, 32),)),
        "gain_one": jnp.clip(1.0 + 0.1 * jax.random.normal(seeds[5], (D,), jnp.float32), 0.5, 1.5).astype(jnp.bfloat16),
        "shift_one": gaussian(seeds[6], (D,), 0.2, 1.1953125, ((0, 32),)),
        "weight_in": gaussian(seeds[7], (D, FF), D ** -0.5, 0.21875, ((0, 32),)),
        "bias_in": gaussian(seeds[8], (FF,), 0.2, 1.1953125, ((0, 32),)),
        "weight_fin": gaussian(seeds[9], (FF, D), FF ** -0.5, 0.109375, ((0, 32),)),
        "bias_fin": gaussian(seeds[10], (D,), 0.2, 1.1953125, ((0, 32),)),
        "gain_two": jnp.clip(1.0 + 0.1 * jax.random.normal(seeds[11], (D,), jnp.float32), 0.5, 1.5).astype(jnp.bfloat16),
        "shift_two": gaussian(seeds[12], (D,), 0.2, 1.1953125, ((0, 32),)),
        "segments": jax.vmap(lambda own: jnp.searchsorted(jnp.cumsum(ragged(own, PAIRS, SEQ_LEN, MOST_SEG, 0)), jnp.arange(SEQ_LEN), side="right"))(jax.random.split(seeds[13], SEQS)).reshape((SEQS, SEQ_LEN)).astype(jnp.int32),
        "cotangent": bell_draw_with(seeds[14], (TOKENS, D), 1.0, 6.0, ((0, 32),), (0, 1, 32, 2.75)),
    }


EPSILON = 1e-06
NEG_FILL = -1e+30

@jax.custom_vjp
def low(v):
    return lax.optimization_barrier(v.astype(jnp.bfloat16)).astype(jnp.float32)

@jax.custom_vjp
def low_back(v):
    return v

def low_keep(v):
    return (low(v), None)

def low_pass(kept, grad):
    return (grad,)

def back_keep(v):
    return (v, None)

def back_low(kept, grad):
    return (low(grad),)
low.defvjp(low_keep, low_pass)
low_back.defvjp(back_keep, back_low)

def product(left, right):
    return jnp.dot(left, right, precision=lax.Precision.HIGHEST)

def layer_norm(summed, gain, shift):
    center = summed - lax.optimization_barrier(jnp.mean(summed, axis=-1, keepdims=True))
    inverse = lax.rsqrt(lax.optimization_barrier(jnp.mean(center * center, axis=-1, keepdims=True)) + EPSILON)
    return center * inverse * gain + shift

def layer_group(rows, segment_group, params):
    weight_qkv, bias_qv, weight_out, bias_out, gain_one, shift_one, weight_in, bias_in, weight_fin, bias_fin, gain_two, shift_two = params
    joined = product(rows, weight_qkv)
    queries = low(low_back(joined[:, :D] + bias_qv[:D]))
    key_rows = low(low_back(joined[:, D:2 * D]))
    values = low(low_back(joined[:, 2 * D:] + bias_qv[D:]))
    group_count = segment_group.shape[0]
    shape_heads = (group_count, SEQ_LEN, HEADS, HEAD_DIM)
    scores = jnp.einsum('gqhd,gkhd->ghqk', queries.reshape(shape_heads), key_rows.reshape(shape_heads), precision=lax.Precision.HIGHEST) * HEAD_DIM ** (-0.5)
    scores = low_back(scores)
    same_pair = segment_group[:, :, None] == segment_group[:, None, :]
    scores = jnp.where(same_pair[:, None], scores, NEG_FILL)
    maxima = lax.optimization_barrier(jnp.max(scores, axis=-1, keepdims=True))
    exponent = jnp.exp(scores - maxima)
    attn_probs = exponent / lax.optimization_barrier(jnp.sum(exponent, axis=-1, keepdims=True))
    context = jnp.einsum('ghqk,gkhd->gqhd', low(attn_probs), values.reshape(shape_heads), precision=lax.Precision.HIGHEST)
    context = low(low_back(context.reshape(rows.shape)))
    attn_branch = low_back(product(context, weight_out) + bias_out)
    hidden = layer_norm(rows + attn_branch, gain_one, shift_one)
    pre_act = low_back(product(low(hidden), weight_in) + bias_in)
    activated = low(jax.nn.gelu(pre_act, approximate=False))
    ffn_branch = low_back(product(activated, weight_fin) + bias_fin)
    return layer_norm(hidden + ffn_branch, gain_two, shift_two)

def forward(rows_all, params, segments):
    group_count = 8
    blocks = rows_all.reshape(SEQS // group_count, group_count * SEQ_LEN, D)
    segment_blocks = segments.reshape(SEQS // group_count, group_count, SEQ_LEN)

    def one_block(block_pair):
        return layer_group(block_pair[0], block_pair[1], params)
    mapped = lax.map(jax.checkpoint(one_block), (blocks, segment_blocks))
    return mapped.reshape(TOKENS, D)

def reference(tokens, weight_qkv, bias_qv, weight_out, bias_out, gain_one, shift_one, weight_in, bias_in, weight_fin, bias_fin, gain_two, shift_two, segments, cotangent):
    params = tuple((member.astype(jnp.float32) for member in (weight_qkv, bias_qv, weight_out, bias_out, gain_one, shift_one, weight_in, bias_in, weight_fin, bias_fin, gain_two, shift_two)))

    def wrapped(rows_all, weights):
        return forward(rows_all, weights, segments)
    result, pullback = jax.vjp(wrapped, tokens.astype(jnp.float32), params)
    grad_tokens, gradients = pullback(cotangent.astype(jnp.float32))
    return (result.astype(jnp.bfloat16), grad_tokens, gradients[0], gradients[1], gradients[2], gradients[3], gradients[4], gradients[5], gradients[6], gradients[7], gradients[8], gradients[9], gradients[10], gradients[11])
```

```python
import functools

import jax
import jax.numpy as jnp
from jax import lax
from jax.experimental import pallas as pl
from jax.experimental.pallas import tpu as pltpu
from jax.sharding import PartitionSpec as P

HEAD_DIM = 64
BLOCK = 128
EPSILON = 1e-06
NEG_FILL = -1e30
F32 = jnp.float32
BF16 = jnp.bfloat16
VMEM_LIMIT = 60 << 20


def dot(left, right, dims):
    return lax.dot_general(left, right, ((dims[:1], dims[1:]), ((), ())), preferred_element_type=F32)


def dot_nn(left, right):
    return dot(left, right, (1, 0))


def dot_nt(left, right):
    return dot(left, right, (1, 1))


def dot_tn(left, right):
    return dot(left, right, (0, 0))


def windows(length):
    return [
        (max(0, start - BLOCK), min(length, start + 2 * BLOCK))
        for start in range(0, length, BLOCK)
    ]


def mask_offsets(length):
    offsets, total = [], 0
    for low, high in windows(length):
        offsets.append(total)
        total += high - low
    return offsets, total


def fill_masks(mask_ref, seq, segment_row):
    length = segment_row.shape[1]
    columns = jnp.transpose(jnp.broadcast_to(segment_row, (BLOCK, length)))
    offsets, _ = mask_offsets(length)
    for block, (low, high) in enumerate(windows(length)):
        rows = jnp.broadcast_to(
            segment_row[:, block * BLOCK : (block + 1) * BLOCK], (high - low, BLOCK)
        )
        mask_ref[seq, pl.ds(offsets[block], high - low), :] = jnp.where(
            columns[low:high] == rows, 0.0, NEG_FILL
        )


def stacked(pair):
    lane = lax.broadcasted_iota(jnp.int32, pair.shape, 1)
    zero = jnp.zeros_like(pair)
    return jnp.concatenate(
        [jnp.where(lane < HEAD_DIM, pair, zero), jnp.where(lane < HEAD_DIM, zero, pair)], axis=0
    )


def unstacked_t(joined):
    row = lax.broadcasted_iota(jnp.int32, (2 * HEAD_DIM, BLOCK), 0)
    return jnp.transpose(jnp.where(row < HEAD_DIM, joined[:, :BLOCK], joined[:, BLOCK:]))


def twice(mask):
    return jnp.concatenate([mask, mask], axis=1)


def normalize(summed):
    center = summed - jnp.mean(summed, axis=-1, keepdims=True)
    inverse = lax.rsqrt(jnp.mean(center * center, axis=-1, keepdims=True) + EPSILON)
    return (center * inverse, inverse)


def normalize_back(grad_normed, normed, inverse):
    mean_grad = jnp.mean(grad_normed, axis=-1, keepdims=True)
    mean_cross = jnp.mean(grad_normed * normed, axis=-1, keepdims=True)
    return inverse * (grad_normed - mean_grad - normed * mean_cross)


def column_sum(rows):
    return jnp.sum(rows, axis=0, keepdims=True)


def gelu_parts(pre):
    size = jnp.abs(pre)
    t = 1.0 / (1.0 + 0.3275911 * 0.7071067811865476 * size)
    bell = jnp.exp(-0.5 * pre * pre)
    series = t * (
        0.127414796
        + t * (-0.142248368 + t * (0.7107068705 + t * (-0.7265760135 + t * 0.5307027145)))
    )
    tail = series * bell
    cdf = jnp.where(pre >= 0.0, 1.0 - tail, tail)
    return (pre * cdf, cdf + pre * (bell * 0.3989422804014327))


def attention_kernel(
    tokens_ref, segment_ref, wqkv_ref, wout_ref, bqkv_ref, bout_ref,
    qkv_ref, context_ref, lse_ref, normed_ref, inverse_ref, mask_ref,
):
    length, width = tokens_ref.shape
    fill_masks(mask_ref, 0, segment_ref[0])
    offsets, _ = mask_offsets(length)
    for part in range(3):
        cols = slice(part * width, (part + 1) * width)
        joined = dot_nn(tokens_ref[...], wqkv_ref[:, cols]) + bqkv_ref[:, cols]
        if part == 0:
            joined = joined * HEAD_DIM ** (-0.5)
        qkv_ref[:, cols] = joined.astype(BF16)

    def one_pair(pair, _):
        def cols(part):
            return pl.ds(pl.multiple_of(part * width + pair * BLOCK, BLOCK), BLOCK)

        for block, (low, high) in enumerate(windows(length)):
            here = slice(block * BLOCK, (block + 1) * BLOCK)
            query = stacked(qkv_ref[here, cols(0)])
            scores = dot_nt(qkv_ref[low:high, cols(1)], query)
            scores = scores + twice(mask_ref[0, pl.ds(offsets[block], high - low), :])
            maxima = jnp.max(scores, axis=0, keepdims=True)
            exponent = jnp.exp(scores - maxima)
            totals = jnp.sum(exponent, axis=0, keepdims=True)
            context = dot_tn(qkv_ref[low:high, cols(2)], exponent.astype(BF16)) * (1.0 / totals)
            context_ref[here, cols(0)] = unstacked_t(context).astype(BF16)
            lse_ref[0, pl.ds(pair * (length // BLOCK) + block, 1), :] = maxima + jnp.log(totals)
        return 0

    lax.fori_loop(0, width // BLOCK, one_pair, 0)
    branch = dot_nn(context_ref[...], wout_ref[...]) + bout_ref[...]
    normed, inverse = normalize(tokens_ref[...].astype(F32) + branch)
    normed_ref[...] = normed
    inverse_ref[...] = jnp.broadcast_to(inverse, inverse_ref.shape)


def whole(shape):
    return pl.BlockSpec(shape, lambda *_: (0,) * len(shape), pipeline_mode=pl.Buffered(1))


def attention_forward(tokens, segments, wqkv, wout, bqkv, bout):
    count, length = segments.shape[0], segments.shape[2]
    width = tokens.shape[1]
    rows = pl.BlockSpec((length, width), lambda i: (i, 0))
    lse_rows = (width // BLOCK) * (length // BLOCK)
    return pl.pallas_call(
        attention_kernel,
        grid=(count,),
        in_specs=[
            rows,
            pl.BlockSpec((1, 1, length), lambda i: (i, 0, 0)),
            whole(wqkv.shape),
            whole(wout.shape),
            whole(bqkv.shape),
            whole(bout.shape),
        ],
        out_specs=[
            pl.BlockSpec((length, 3 * width), lambda i: (i, 0)),
            rows,
            pl.BlockSpec((1, lse_rows, 2 * BLOCK), lambda i: (i, 0, 0)),
            rows,
            pl.BlockSpec((length, BLOCK), lambda i: (i, 0)),
        ],
        out_shape=[
            jax.ShapeDtypeStruct((count * length, 3 * width), BF16),
            jax.ShapeDtypeStruct((count * length, width), BF16),
            jax.ShapeDtypeStruct((count, lse_rows, 2 * BLOCK), F32),
            jax.ShapeDtypeStruct((count * length, width), F32),
            jax.ShapeDtypeStruct((count * length, BLOCK), F32),
        ],
        scratch_shapes=[pltpu.VMEM((1, mask_offsets(length)[1], BLOCK), F32)],
        compiler_params=pltpu.CompilerParams(vmem_limit_bytes=VMEM_LIMIT),
        name="attention_forward",
    )(tokens, segments, wqkv, wout, bqkv, bout)


def feed_kernel(
    normed_ref, cot_ref, win_ref, wfin_ref, vec_ref, bin_ref,
    out_ref, act_ref, slope_ref, gsum_ref, gffn_ref, low_ref, gvec_ref,
    hidden_ref,
):
    hidden = normed_ref[...] * vec_ref[0:1] + vec_ref[1:2]
    hidden_ref[...] = hidden
    low_ref[...] = hidden.astype(BF16)
    width = win_ref.shape[0]

    def one_chunk(chunk, _):
        cols = pl.ds(pl.multiple_of(chunk * width, width), width)
        pre = dot_nn(low_ref[...], win_ref[:, cols]) + bin_ref[:, cols]
        active, slope = gelu_parts(pre)
        act_ref[:, cols] = active.astype(BF16)
        slope_ref[:, cols] = slope.astype(BF16)
        return 0

    lax.fori_loop(0, win_ref.shape[1] // width, one_chunk, 0)
    branch = dot_nn(act_ref[...], wfin_ref[...]) + vec_ref[2:3]
    normed, inverse = normalize(hidden_ref[...] + branch)
    gain = vec_ref[3:4]
    out_ref[...] = (normed * gain + vec_ref[4:5]).astype(BF16)
    cot = cot_ref[...].astype(F32)
    gsum = normalize_back(cot * gain, normed, inverse)
    gsum_ref[...] = gsum
    gffn = gsum.astype(BF16)
    gffn_ref[...] = gffn

    @pl.when(pl.program_id(0) == 0)
    def _():
        gvec_ref[...] = jnp.zeros_like(gvec_ref)

    gvec_ref[0:1] += column_sum(cot * normed)
    gvec_ref[1:2] += column_sum(cot)
    gvec_ref[2:3] += column_sum(gffn.astype(F32))


def feed_forward(normed, cotangent, win, wfin, vectors, bin_, tile):
    tokens, width = normed.shape
    hidden = win.shape[1]
    rows = pl.BlockSpec((tile, width), lambda i: (i, 0))
    wide = pl.BlockSpec((tile, hidden), lambda i: (i, 0))
    return pl.pallas_call(
        feed_kernel,
        grid=(tokens // tile,),
        in_specs=[rows, rows, whole(win.shape), whole(wfin.shape), whole(vectors.shape), whole(bin_.shape)],
        out_specs=[rows, wide, wide, rows, rows, rows, pl.BlockSpec((8, width), lambda i: (0, 0))],
        out_shape=[
            jax.ShapeDtypeStruct((tokens, width), BF16),
            jax.ShapeDtypeStruct((tokens, hidden), BF16),
            jax.ShapeDtypeStruct((tokens, hidden), BF16),
            jax.ShapeDtypeStruct((tokens, width), F32),
            jax.ShapeDtypeStruct((tokens, width), BF16),
            jax.ShapeDtypeStruct((tokens, width), BF16),
            jax.ShapeDtypeStruct((8, width), F32),
        ],
        scratch_shapes=[pltpu.VMEM((tile, width), F32)],
        compiler_params=pltpu.CompilerParams(vmem_limit_bytes=VMEM_LIMIT),
        name="feed_forward",
    )(normed, cotangent, win, wfin, vectors, bin_)


def feed_back_kernel(
    gffn_ref, low_ref, gsum_hbm, act_ref, slope_ref, win_ref, wfin_ref,
    dwin_ref, dwfin_ref, gbin_ref, ghid_hbm,
    low_t_ref, acc_ref, gpre_ref, sem,
):
    step = pl.program_id(0)
    tokens = gffn_ref.shape[0]
    tile = 512

    @pl.when(step == 0)
    def _():
        copy = pltpu.make_async_copy(gsum_hbm, acc_ref, sem)
        copy.start()
        low_t_ref[...] = jnp.transpose(low_ref[...])
        copy.wait()

    gbin_ref[...] = jnp.zeros_like(gbin_ref)
    for start in range(0, tokens, tile):
        here = slice(start, start + tile)
        gpre = (dot_nt(gffn_ref[here], wfin_ref[...]) * slope_ref[here].astype(F32)).astype(BF16)
        gpre_ref[here] = gpre
        gbin_ref[0:1] += column_sum(gpre.astype(F32))
        acc_ref[here] += dot_nt(gpre, win_ref[...])
    dwin_ref[...] = dot_nn(low_t_ref[...], gpre_ref[...]).astype(BF16)
    dwfin_ref[...] = dot_tn(act_ref[...], gffn_ref[...]).astype(BF16)

    @pl.when(step == pl.num_programs(0) - 1)
    def _():
        pltpu.sync_copy(acc_ref, ghid_hbm)


def feed_backward(gffn, low, gsum, act, slope, win, wfin, chunk):
    tokens, width = low.shape
    hidden = win.shape[1]
    any_ = pl.BlockSpec(memory_space=pl.ANY)
    return pl.pallas_call(
        feed_back_kernel,
        grid=(hidden // chunk,),
        in_specs=[
            whole(gffn.shape), whole(low.shape), any_,
            pl.BlockSpec((tokens, chunk), lambda i: (0, i)),
            pl.BlockSpec((tokens, chunk), lambda i: (0, i)),
            pl.BlockSpec((width, chunk), lambda i: (0, i)),
            pl.BlockSpec((chunk, width), lambda i: (i, 0)),
        ],
        out_specs=[
            pl.BlockSpec((width, chunk), lambda i: (0, i)),
            pl.BlockSpec((chunk, width), lambda i: (i, 0)),
            pl.BlockSpec((8, chunk), lambda i: (0, i)),
            any_,
        ],
        out_shape=[
            jax.ShapeDtypeStruct((width, hidden), BF16),
            jax.ShapeDtypeStruct((hidden, width), BF16),
            jax.ShapeDtypeStruct((8, hidden), F32),
            jax.ShapeDtypeStruct((tokens, width), F32),
        ],
        scratch_shapes=[
            pltpu.VMEM((width, tokens), BF16),
            pltpu.VMEM((tokens, width), F32),
            pltpu.VMEM((tokens, chunk), BF16),
            pltpu.SemaphoreType.DMA,
        ],
        compiler_params=pltpu.CompilerParams(vmem_limit_bytes=VMEM_LIMIT),
        name="feed_backward",
    )(gffn, low, gsum, act, slope, win, wfin)


def project_back_kernel(
    ghid_ref, normed_ref, inverse_ref, context_ref, wout_ref, gain_ref,
    gsum_ref, gcon_ref, dwout_ref, gvec_ref, acc_ref,
):
    step = pl.program_id(0)

    @pl.when(step == 0)
    def _():
        gvec_ref[...] = jnp.zeros_like(gvec_ref)
        acc_ref[...] = jnp.zeros_like(acc_ref)

    ghid = ghid_ref[...]
    normed = normed_ref[...]
    gvec_ref[0:1] += column_sum(ghid * normed)
    gvec_ref[1:2] += column_sum(ghid)
    gsum = normalize_back(ghid * gain_ref[...], normed, inverse_ref[:, 0:1])
    gsum_ref[...] = gsum
    gattn = gsum.astype(BF16)
    gvec_ref[2:3] += column_sum(gattn.astype(F32))
    gcon_ref[...] = dot_nt(gattn, wout_ref[...]).astype(BF16)
    acc_ref[...] += dot_tn(context_ref[...], gattn)

    @pl.when(step == pl.num_programs(0) - 1)
    def _():
        dwout_ref[...] = acc_ref[...].astype(BF16)


def project_backward(ghid, normed, inverse, context, wout, gain, tile):
    tokens, width = ghid.shape
    rows = pl.BlockSpec((tile, width), lambda i: (i, 0))
    return pl.pallas_call(
        project_back_kernel,
        grid=(tokens // tile,),
        in_specs=[
            rows, rows, pl.BlockSpec((tile, BLOCK), lambda i: (i, 0)), rows,
            whole(wout.shape), whole(gain.shape),
        ],
        out_specs=[rows, rows, whole((width, width)), pl.BlockSpec((8, width), lambda i: (0, 0))],
        out_shape=[
            jax.ShapeDtypeStruct((tokens, width), F32),
            jax.ShapeDtypeStruct((tokens, width), BF16),
            jax.ShapeDtypeStruct((width, width), BF16),
            jax.ShapeDtypeStruct((8, width), F32),
        ],
        scratch_shapes=[pltpu.VMEM((width, width), F32)],
        compiler_params=pltpu.CompilerParams(vmem_limit_bytes=VMEM_LIMIT),
        name="project_backward",
    )(ghid, normed, inverse, context, wout, gain)


def attention_back_kernel(
    q_ref, k_ref, v_ref, gcon_ref, lse_ref, segment_ref, tokens_ref, wq_ref, wk_ref, wv_ref, gsum_hbm,
    dw_ref, gvec_ref, gtok_hbm,
    tokens_t_ref, acc_ref, mask_ref, grad_ref, dk_ref, dv_ref, sem,
):
    pair = pl.program_id(0)
    count, length = segment_ref.shape[0], segment_ref.shape[2]
    blocks = length // BLOCK
    offsets, _ = mask_offsets(length)
    tile = 512

    @pl.when(pair == 0)
    def _():
        copy = pltpu.make_async_copy(gsum_hbm, acc_ref, sem)
        copy.start()
        tokens_t_ref[...] = jnp.transpose(tokens_ref[...])
        for seq in range(count):
            fill_masks(mask_ref, seq, segment_ref[seq])
        copy.wait()

    def one_seq(seq, _):
        base = pl.multiple_of(seq * length, length)
        dk_ref[...] = jnp.zeros_like(dk_ref)
        dv_ref[...] = jnp.zeros_like(dv_ref)
        for block, (low, high) in enumerate(windows(length)):
            here = pl.ds(base + block * BLOCK, BLOCK)
            reach = pl.ds(base + low, high - low)
            query = stacked(q_ref[here])
            grad = stacked(gcon_ref[here])
            keys = k_ref[reach]
            scores = dot_nt(keys, query) + twice(mask_ref[seq, pl.ds(offsets[block], high - low), :])
            probs = jnp.exp(scores - lse_ref[seq, pl.ds(pair * blocks + block, 1), :])
            gprobs = dot_nt(v_ref[reach], grad)
            dots = jnp.sum(probs * gprobs, axis=0, keepdims=True)
            gscores = (probs * (gprobs - dots)).astype(BF16)
            dv_ref[low:high] += dot_nn(probs.astype(BF16), grad)
            dk_ref[low:high] += dot_nn(gscores, query)
            gquery = unstacked_t(dot_tn(keys, gscores)) * HEAD_DIM ** (-0.5)
            grad_ref[here, 0:BLOCK] = gquery.astype(BF16)
        rows = pl.ds(base, length)
        grad_ref[rows, BLOCK : 2 * BLOCK] = dk_ref[...].astype(BF16)
        grad_ref[rows, 2 * BLOCK :] = dv_ref[...].astype(BF16)
        return 0

    lax.fori_loop(0, count, one_seq, 0)
    gvec_ref[...] = jnp.zeros_like(gvec_ref)
    gvec_ref[0:1] = column_sum(grad_ref[:, :BLOCK].astype(F32))
    gvec_ref[1:2] = column_sum(grad_ref[:, 2 * BLOCK :].astype(F32))
    weights = jnp.concatenate([wq_ref[...], wk_ref[...], wv_ref[...]], axis=1)
    for start in range(0, acc_ref.shape[0], tile):
        here = slice(start, start + tile)
        acc_ref[here] += dot_nt(grad_ref[here], weights)
    dw = dot_nn(tokens_t_ref[...], grad_ref[...]).astype(BF16)
    for part in range(3):
        dw_ref[part] = dw[:, part * BLOCK : (part + 1) * BLOCK]

    @pl.when(pair == pl.num_programs(0) - 1)
    def _():
        pltpu.sync_copy(acc_ref, gtok_hbm)


def attention_backward(qkv, gcon, lse, segments, tokens, wqkv, gsum):
    count, length = segments.shape[0], segments.shape[2]
    total, width = tokens.shape
    pairs = width // BLOCK
    any_ = pl.BlockSpec(memory_space=pl.ANY)

    def part(rows, index):
        return pl.BlockSpec((rows, BLOCK), lambda i: (0, index * pairs + i))

    return pl.pallas_call(
        attention_back_kernel,
        grid=(pairs,),
        in_specs=[
            part(total, 0), part(total, 1), part(total, 2), part(total, 0),
            whole(lse.shape), whole(segments.shape), whole(tokens.shape),
            part(width, 0), part(width, 1), part(width, 2), any_,
        ],
        out_specs=[
            pl.BlockSpec((3, width, BLOCK), lambda i: (0, 0, i)),
            pl.BlockSpec((8, BLOCK), lambda i: (0, i)),
            any_,
        ],
        out_shape=[
            jax.ShapeDtypeStruct((3, width, width), BF16),
            jax.ShapeDtypeStruct((8, width), F32),
            jax.ShapeDtypeStruct((total, width), F32),
        ],
        scratch_shapes=[
            pltpu.VMEM((width, total), BF16),
            pltpu.VMEM((total, width), F32),
            pltpu.VMEM((count, mask_offsets(length)[1], BLOCK), F32),
            pltpu.VMEM((total, 3 * BLOCK), BF16),
            pltpu.VMEM((length, BLOCK), F32),
            pltpu.VMEM((length, BLOCK), F32),
            pltpu.SemaphoreType.DMA,
        ],
        compiler_params=pltpu.CompilerParams(vmem_limit_bytes=VMEM_LIMIT),
        name="attention_backward",
    )(qkv, qkv, qkv, gcon, lse, segments, tokens, wqkv, wqkv, wqkv, gsum)


def layer(
    tokens, wqkv, bqv, wout, bout, gain_one, shift_one,
    win, bin_, wfin, bfin, gain_two, shift_two, segments, cotangent,
):
    width = tokens.shape[1]
    length = segments.shape[1]
    segments = segments.reshape(segments.shape[0], 1, length)
    bqkv = jnp.concatenate([bqv[:, :width], jnp.zeros_like(bout), bqv[:, width:]], axis=1)
    qkv, context, lse, normed, inverse = attention_forward(tokens, segments, wqkv, wout, bqkv, bout)
    zero = jnp.zeros_like(bfin)
    vectors = jnp.concatenate([gain_one, shift_one, bfin, gain_two, shift_two, zero, zero, zero], axis=0)
    output, act, slope, gsum_two, gffn, low, gvec_two = feed_forward(
        normed, cotangent, win, wfin, vectors, bin_, min(512, tokens.shape[0])
    )
    dwin, dwfin, gbin, ghid = feed_backward(gffn, low, gsum_two, act, slope, win, wfin, 512)
    gsum_one, gcon, dwout, gvec_one = project_backward(
        ghid, normed, inverse, context, wout, gain_one, min(512, tokens.shape[0])
    )
    dwqkv, gvec_qv, gtok = attention_backward(qkv, gcon, lse, segments, tokens, wqkv, gsum_one)
    return (
        output, gtok, dwqkv, gvec_qv[0:2].reshape(1, -1), dwout, gvec_one[2:3], gvec_one[0:1], gvec_one[1:2],
        dwin, gbin[0:1], dwfin, gvec_two[2:3], gvec_two[0:1], gvec_two[1:2],
    )


AXES = ("dp", "inner")


def shards(
    tokens, weight_qkv, bias_qv, weight_out, bias_out, gain_one, shift_one,
    weight_in, bias_in, weight_fin, bias_fin, gain_two, shift_two, segments, cotangent,
):
    vectors = (bias_qv, bias_out, gain_one, shift_one, bias_in, bias_fin, gain_two, shift_two)
    sizes = [v.shape[0] for v in vectors]
    joined = jnp.concatenate(vectors).reshape(1, -1)
    joined = lax.all_gather(joined, AXES, axis=0, tiled=True).astype(F32)
    rows, start = [], 0
    for size in sizes:
        rows.append(joined[:, start : start + size].reshape(1, -1))
        start += size
    full = [lax.all_gather(w, AXES, axis=0, tiled=True) for w in (weight_qkv, weight_out, weight_in, weight_fin)]
    out = layer(
        tokens, full[0], rows[0], full[1], rows[1], rows[2], rows[3],
        full[2], rows[4], full[3], rows[5], rows[6], rows[7], segments, cotangent,
    )
    def scatter(grad, axis=0):
        return lax.psum_scatter(grad, AXES, scatter_dimension=axis, tiled=True).astype(F32)

    count = joined.shape[0]
    order = (3, 5, 6, 7, 9, 11, 12, 13)
    small = jnp.concatenate([out[i].reshape(count, -1) for i in order], axis=1)
    small = lax.psum_scatter(small, AXES, scatter_dimension=0, tiled=True).reshape(-1)
    parts, start = {}, 0
    for index, size in zip(order, sizes):
        parts[index] = small[start : start + size]
        start += size
    dwqkv = scatter(out[2], 1)
    dwqkv = jnp.concatenate([dwqkv[0], dwqkv[1], dwqkv[2]], axis=1)
    return (
        out[0], out[1], dwqkv, parts[3], scatter(out[4]), parts[5], parts[6], parts[7],
        scatter(out[8]), parts[9], scatter(out[10]), parts[11], parts[12], parts[13],
    )


def solution(mesh):
    row, vec = P(AXES, None), P(AXES)
    in_specs = (row, row, vec, row, vec, vec, vec, row, vec, row, vec, vec, vec, row, row)
    out_specs = (row, row, row, vec, row, vec, vec, vec, row, vec, row, vec, vec, vec)
    return jax.shard_map(shards, mesh=mesh, in_specs=in_specs, out_specs=out_specs, check_vma=False)
```

```python
import functools

import jax
import jax.numpy as jnp
from jax import lax
from jax.experimental import pallas as pl
from jax.experimental.pallas import tpu as pltpu
from jax.sharding import PartitionSpec as P

HEAD_DIM = 64
BLOCK = 128
EPSILON = 1e-06
NEG_FILL = -1e30
F32 = jnp.float32
BF16 = jnp.bfloat16
VMEM_LIMIT = 60 << 20


def dot(left, right, dims):
    return lax.dot_general(left, right, ((dims[:1], dims[1:]), ((), ())), preferred_element_type=F32)


def dot_nn(left, right):
    return dot(left, right, (1, 0))


def dot_nt(left, right):
    return dot(left, right, (1, 1))


def dot_tn(left, right):
    return dot(left, right, (0, 0))


def windows(length):
    return [
        (max(0, start - BLOCK), min(length, start + 2 * BLOCK))
        for start in range(0, length, BLOCK)
    ]


def mask_offsets(length):
    offsets, total = [], 0
    for low, high in windows(length):
        offsets.append(total)
        total += high - low
    return offsets, total


def fill_masks(mask_ref, seq, segment_row):
    length = segment_row.shape[1]
    columns = jnp.transpose(jnp.broadcast_to(segment_row, (BLOCK, length)))
    offsets, _ = mask_offsets(length)
    for block, (low, high) in enumerate(windows(length)):
        rows = jnp.broadcast_to(
            segment_row[:, block * BLOCK : (block + 1) * BLOCK], (high - low, BLOCK)
        )
        mask_ref[seq, pl.ds(offsets[block], high - low), :] = jnp.where(
            columns[low:high] == rows, 0.0, NEG_FILL
        )


def stacked(pair):
    lane = lax.broadcasted_iota(jnp.int32, pair.shape, 1)
    zero = jnp.zeros_like(pair)
    return jnp.concatenate(
        [jnp.where(lane < HEAD_DIM, pair, zero), jnp.where(lane < HEAD_DIM, zero, pair)], axis=0
    )


def unstacked_t(joined):
    row = lax.broadcasted_iota(jnp.int32, (2 * HEAD_DIM, BLOCK), 0)
    return jnp.transpose(jnp.where(row < HEAD_DIM, joined[:, :BLOCK], joined[:, BLOCK:]))


def twice(mask):
    return jnp.concatenate([mask, mask], axis=1)


def normalize(summed):
    center = summed - jnp.mean(summed, axis=-1, keepdims=True)
    inverse = lax.rsqrt(jnp.mean(center * center, axis=-1, keepdims=True) + EPSILON)
    return (center * inverse, inverse)


def normalize_back(grad_normed, normed, inverse):
    mean_grad = jnp.mean(grad_normed, axis=-1, keepdims=True)
    mean_cross = jnp.mean(grad_normed * normed, axis=-1, keepdims=True)
    return inverse * (grad_normed - mean_grad - normed * mean_cross)


def column_sum(rows):
    return jnp.sum(rows, axis=0, keepdims=True)


def gelu_parts(pre):
    size = jnp.abs(pre)
    t = 1.0 / (1.0 + 0.3275911 * 0.7071067811865476 * size)
    bell = jnp.exp(-0.5 * pre * pre)
    series = t * (
        0.127414796
        + t * (-0.142248368 + t * (0.7107068705 + t * (-0.7265760135 + t * 0.5307027145)))
    )
    tail = series * bell
    cdf = jnp.where(pre >= 0.0, 1.0 - tail, tail)
    return (pre * cdf, cdf + pre * (bell * 0.3989422804014327))


def attention_kernel(
    tokens_ref, segment_ref, wqkv_ref, wout_ref, bqkv_ref, bout_ref,
    qkv_ref, context_ref, lse_ref, normed_ref, inverse_ref, mask_ref,
):
    length, width = tokens_ref.shape
    fill_masks(mask_ref, 0, segment_ref[0])
    offsets, _ = mask_offsets(length)
    for part in range(3):
        cols = slice(part * width, (part + 1) * width)
        joined = dot_nn(tokens_ref[...], wqkv_ref[:, cols]) + bqkv_ref[:, cols]
        if part == 0:
            joined = joined * HEAD_DIM ** (-0.5)
        qkv_ref[:, cols] = joined.astype(BF16)

    def one_pair(pair, _):
        def cols(part):
            return pl.ds(pl.multiple_of(part * width + pair * BLOCK, BLOCK), BLOCK)

        for block, (low, high) in enumerate(windows(length)):
            here = slice(block * BLOCK, (block + 1) * BLOCK)
            query = stacked(qkv_ref[here, cols(0)])
            scores = dot_nt(qkv_ref[low:high, cols(1)], query)
            scores = scores + twice(mask_ref[0, pl.ds(offsets[block], high - low), :])
            maxima = jnp.max(scores, axis=0, keepdims=True)
            exponent = jnp.exp(scores - maxima)
            totals = jnp.sum(exponent, axis=0, keepdims=True)
            context = dot_tn(qkv_ref[low:high, cols(2)], exponent.astype(BF16)) * (1.0 / totals)
            context_ref[here, cols(0)] = unstacked_t(context).astype(BF16)
            lse_ref[0, pl.ds(pair * (length // BLOCK) + block, 1), :] = maxima + jnp.log(totals)
        return 0

    lax.fori_loop(0, width // BLOCK, one_pair, 0)
    branch = dot_nn(context_ref[...], wout_ref[...]) + bout_ref[...]
    normed, inverse = normalize(tokens_ref[...].astype(F32) + branch)
    normed_ref[...] = normed
    inverse_ref[...] = jnp.broadcast_to(inverse, inverse_ref.shape)


def whole(shape):
    return pl.BlockSpec(shape, lambda *_: (0,) * len(shape), pipeline_mode=pl.Buffered(1))


def attention_forward(tokens, segments, wqkv, wout, bqkv, bout):
    count, length = segments.shape[0], segments.shape[2]
    width = tokens.shape[1]
    rows = pl.BlockSpec((length, width), lambda i: (i, 0))
    lse_rows = (width // BLOCK) * (length // BLOCK)
    return pl.pallas_call(
        attention_kernel,
        grid=(count,),
        in_specs=[
            rows,
            pl.BlockSpec((1, 1, length), lambda i: (i, 0, 0)),
            whole(wqkv.shape),
            whole(wout.shape),
            whole(bqkv.shape),
            whole(bout.shape),
        ],
        out_specs=[
            pl.BlockSpec((length, 3 * width), lambda i: (i, 0)),
            rows,
            pl.BlockSpec((1, lse_rows, 2 * BLOCK), lambda i: (i, 0, 0)),
            rows,
            pl.BlockSpec((length, BLOCK), lambda i: (i, 0)),
        ],
        out_shape=[
            jax.ShapeDtypeStruct((count * length, 3 * width), BF16),
            jax.ShapeDtypeStruct((count * length, width), BF16),
            jax.ShapeDtypeStruct((count, lse_rows, 2 * BLOCK), F32),
            jax.ShapeDtypeStruct((count * length, width), F32),
            jax.ShapeDtypeStruct((count * length, BLOCK), F32),
        ],
        scratch_shapes=[pltpu.VMEM((1, mask_offsets(length)[1], BLOCK), F32)],
        compiler_params=pltpu.CompilerParams(vmem_limit_bytes=VMEM_LIMIT),
        name="attention_forward",
    )(tokens, segments, wqkv, wout, bqkv, bout)


def feed_kernel(
    normed_ref, cot_ref, win_ref, wfin_ref, vec_ref, bin_ref,
    out_ref, act_ref, slope_ref, gsum_ref, gffn_ref, low_ref, gvec_ref,
    hidden_ref,
):
    hidden = normed_ref[...] * vec_ref[0:1] + vec_ref[1:2]
    hidden_ref[...] = hidden
    low_ref[...] = hidden.astype(BF16)
    width = win_ref.shape[0]

    def one_chunk(chunk, _):
        cols = pl.ds(pl.multiple_of(chunk * width, width), width)
        pre = dot_nn(low_ref[...], win_ref[:, cols]) + bin_ref[:, cols]
        active, slope = gelu_parts(pre)
        act_ref[:, cols] = active.astype(BF16)
        slope_ref[:, cols] = slope.astype(BF16)
        return 0

    lax.fori_loop(0, win_ref.shape[1] // width, one_chunk, 0)
    branch = dot_nn(act_ref[...], wfin_ref[...]) + vec_ref[2:3]
    normed, inverse = normalize(hidden_ref[...] + branch)
    gain = vec_ref[3:4]
    out_ref[...] = (normed * gain + vec_ref[4:5]).astype(BF16)
    cot = cot_ref[...].astype(F32)
    gsum = normalize_back(cot * gain, normed, inverse)
    gsum_ref[...] = gsum
    gffn = gsum.astype(BF16)
    gffn_ref[...] = gffn

    @pl.when(pl.program_id(0) == 0)
    def _():
        gvec_ref[...] = jnp.zeros_like(gvec_ref)

    gvec_ref[0:1] += column_sum(cot * normed)
    gvec_ref[1:2] += column_sum(cot)
    gvec_ref[2:3] += column_sum(gffn.astype(F32))


def feed_forward(normed, cotangent, win, wfin, vectors, bin_, tile):
    tokens, width = normed.shape
    hidden = win.shape[1]
    rows = pl.BlockSpec((tile, width), lambda i: (i, 0))
    wide = pl.BlockSpec((tile, hidden), lambda i: (i, 0))
    return pl.pallas_call(
        feed_kernel,
        grid=(tokens // tile,),
        in_specs=[rows, rows, whole(win.shape), whole(wfin.shape), whole(vectors.shape), whole(bin_.shape)],
        out_specs=[rows, wide, wide, rows, rows, rows, pl.BlockSpec((8, width), lambda i: (0, 0))],
        out_shape=[
            jax.ShapeDtypeStruct((tokens, width), BF16),
            jax.ShapeDtypeStruct((tokens, hidden), BF16),
            jax.ShapeDtypeStruct((tokens, hidden), BF16),
            jax.ShapeDtypeStruct((tokens, width), F32),
            jax.ShapeDtypeStruct((tokens, width), BF16),
            jax.ShapeDtypeStruct((tokens, width), BF16),
            jax.ShapeDtypeStruct((8, width), F32),
        ],
        scratch_shapes=[pltpu.VMEM((tile, width), F32)],
        compiler_params=pltpu.CompilerParams(vmem_limit_bytes=VMEM_LIMIT),
        name="feed_forward",
    )(normed, cotangent, win, wfin, vectors, bin_)


def feed_back_kernel(
    gffn_ref, low_ref, gsum_hbm, act_ref, slope_ref, win_ref, wfin_ref,
    dwin_ref, dwfin_ref, gbin_ref, ghid_hbm,
    low_t_ref, acc_ref, gpre_ref, sem,
):
    step = pl.program_id(0)
    tokens = gffn_ref.shape[0]
    tile = 512

    @pl.when(step == 0)
    def _():
        copy = pltpu.make_async_copy(gsum_hbm, acc_ref, sem)
        copy.start()
        low_t_ref[...] = jnp.transpose(low_ref[...])
        copy.wait()

    gbin_ref[...] = jnp.zeros_like(gbin_ref)
    for start in range(0, tokens, tile):
        here = slice(start, start + tile)
        gpre = (dot_nt(gffn_ref[here], wfin_ref[...]) * slope_ref[here].astype(F32)).astype(BF16)
        gpre_ref[here] = gpre
        gbin_ref[0:1] += column_sum(gpre.astype(F32))
        acc_ref[here] += dot_nt(gpre, win_ref[...])
    dwin_ref[...] = dot_nn(low_t_ref[...], gpre_ref[...]).astype(BF16)
    dwfin_ref[...] = dot_tn(act_ref[...], gffn_ref[...]).astype(BF16)

    @pl.when(step == pl.num_programs(0) - 1)
    def _():
        pltpu.sync_copy(acc_ref, ghid_hbm)


def feed_backward(gffn, low, gsum, act, slope, win, wfin, chunk):
    tokens, width = low.shape
    hidden = win.shape[1]
    any_ = pl.BlockSpec(memory_space=pl.ANY)
    return pl.pallas_call(
        feed_back_kernel,
        grid=(hidden // chunk,),
        in_specs=[
            whole(gffn.shape), whole(low.shape), any_,
            pl.BlockSpec((tokens, chunk), lambda i: (0, i)),
            pl.BlockSpec((tokens, chunk), lambda i: (0, i)),
            pl.BlockSpec((width, chunk), lambda i: (0, i)),
            pl.BlockSpec((chunk, width), lambda i: (i, 0)),
        ],
        out_specs=[
            pl.BlockSpec((width, chunk), lambda i: (0, i)),
            pl.BlockSpec((chunk, width), lambda i: (i, 0)),
            pl.BlockSpec((8, chunk), lambda i: (0, i)),
            any_,
        ],
        out_shape=[
            jax.ShapeDtypeStruct((width, hidden), BF16),
            jax.ShapeDtypeStruct((hidden, width), BF16),
            jax.ShapeDtypeStruct((8, hidden), F32),
            jax.ShapeDtypeStruct((tokens, width), F32),
        ],
        scratch_shapes=[
            pltpu.VMEM((width, tokens), BF16),
            pltpu.VMEM((tokens, width), F32),
            pltpu.VMEM((tokens, chunk), BF16),
            pltpu.SemaphoreType.DMA,
        ],
        compiler_params=pltpu.CompilerParams(vmem_limit_bytes=VMEM_LIMIT),
        name="feed_backward",
    )(gffn, low, gsum, act, slope, win, wfin)


def project_back_kernel(
    ghid_ref, normed_ref, inverse_ref, context_ref, wout_ref, gain_ref,
    gsum_ref, gcon_ref, dwout_ref, gvec_ref, acc_ref,
):
    step = pl.program_id(0)

    @pl.when(step == 0)
    def _():
        gvec_ref[...] = jnp.zeros_like(gvec_ref)
        acc_ref[...] = jnp.zeros_like(acc_ref)

    ghid = ghid_ref[...]
    normed = normed_ref[...]
    gvec_ref[0:1] += column_sum(ghid * normed)
    gvec_ref[1:2] += column_sum(ghid)
    gsum = normalize_back(ghid * gain_ref[...], normed, inverse_ref[:, 0:1])
    gsum_ref[...] = gsum
    gattn = gsum.astype(BF16)
    gvec_ref[2:3] += column_sum(gattn.astype(F32))
    gcon_ref[...] = dot_nt(gattn, wout_ref[...]).astype(BF16)
    acc_ref[...] += dot_tn(context_ref[...], gattn)

    @pl.when(step == pl.num_programs(0) - 1)
    def _():
        dwout_ref[...] = acc_ref[...].astype(BF16)


def project_backward(ghid, normed, inverse, context, wout, gain, tile):
    tokens, width = ghid.shape
    rows = pl.BlockSpec((tile, width), lambda i: (i, 0))
    return pl.pallas_call(
        project_back_kernel,
        grid=(tokens // tile,),
        in_specs=[
            rows, rows, pl.BlockSpec((tile, BLOCK), lambda i: (i, 0)), rows,
            whole(wout.shape), whole(gain.shape),
        ],
        out_specs=[rows, rows, whole((width, width)), pl.BlockSpec((8, width), lambda i: (0, 0))],
        out_shape=[
            jax.ShapeDtypeStruct((tokens, width), F32),
            jax.ShapeDtypeStruct((tokens, width), BF16),
            jax.ShapeDtypeStruct((width, width), BF16),
            jax.ShapeDtypeStruct((8, width), F32),
        ],
        scratch_shapes=[pltpu.VMEM((width, width), F32)],
        compiler_params=pltpu.CompilerParams(vmem_limit_bytes=VMEM_LIMIT),
        name="project_backward",
    )(ghid, normed, inverse, context, wout, gain)


def attention_back_kernel(
    q_ref, k_ref, v_ref, gcon_ref, lse_ref, segment_ref, tokens_ref, wq_ref, wk_ref, wv_ref, gsum_hbm,
    dw_ref, gvec_ref, gtok_hbm,
    tokens_t_ref, acc_ref, mask_ref, grad_ref, dk_ref, dv_ref, sem,
):
    pair = pl.program_id(0)
    count, length = segment_ref.shape[0], segment_ref.shape[2]
    blocks = length // BLOCK
    offsets, _ = mask_offsets(length)
    tile = 512

    @pl.when(pair == 0)
    def _():
        copy = pltpu.make_async_copy(gsum_hbm, acc_ref, sem)
        copy.start()
        tokens_t_ref[...] = jnp.transpose(tokens_ref[...])
        for seq in range(count):
            fill_masks(mask_ref, seq, segment_ref[seq])
        copy.wait()

    def one_seq(seq, _):
        base = pl.multiple_of(seq * length, length)
        dk_ref[...] = jnp.zeros_like(dk_ref)
        dv_ref[...] = jnp.zeros_like(dv_ref)
        for block, (low, high) in enumerate(windows(length)):
            here = pl.ds(base + block * BLOCK, BLOCK)
            reach = pl.ds(base + low, high - low)
            query = stacked(q_ref[here])
            grad = stacked(gcon_ref[here])
            keys = k_ref[reach]
            scores = dot_nt(keys, query) + twice(mask_ref[seq, pl.ds(offsets[block], high - low), :])
            probs = jnp.exp(scores - lse_ref[seq, pl.ds(pair * blocks + block, 1), :])
            gprobs = dot_nt(v_ref[reach], grad)
            dots = jnp.sum(probs * gprobs, axis=0, keepdims=True)
            gscores = (probs * (gprobs - dots)).astype(BF16)
            dv_ref[low:high] += dot_nn(probs.astype(BF16), grad)
            dk_ref[low:high] += dot_nn(gscores, query)
            gquery = unstacked_t(dot_tn(keys, gscores)) * HEAD_DIM ** (-0.5)
            grad_ref[here, 0:BLOCK] = gquery.astype(BF16)
        rows = pl.ds(base, length)
        grad_ref[rows, BLOCK : 2 * BLOCK] = dk_ref[...].astype(BF16)
        grad_ref[rows, 2 * BLOCK :] = dv_ref[...].astype(BF16)
        return 0

    lax.fori_loop(0, count, one_seq, 0)
    gvec_ref[...] = jnp.zeros_like(gvec_ref)
    gvec_ref[0:1] = column_sum(grad_ref[:, :BLOCK].astype(F32))
    gvec_ref[1:2] = column_sum(grad_ref[:, 2 * BLOCK :].astype(F32))
    weights = jnp.concatenate([wq_ref[...], wk_ref[...], wv_ref[...]], axis=1)
    for start in range(0, acc_ref.shape[0], tile):
        here = slice(start, start + tile)
        acc_ref[here] += dot_nt(grad_ref[here], weights)
    dw_ref[...] = dot_nn(tokens_t_ref[...], grad_ref[...]).astype(BF16)

    @pl.when(pair == pl.num_programs(0) - 1)
    def _():
        pltpu.sync_copy(acc_ref, gtok_hbm)


def attention_backward(qkv, gcon, lse, segments, tokens, wqkv, gsum):
    count, length = segments.shape[0], segments.shape[2]
    total, width = tokens.shape
    pairs = width // BLOCK
    any_ = pl.BlockSpec(memory_space=pl.ANY)

    def part(rows, index):
        return pl.BlockSpec((rows, BLOCK), lambda i: (0, index * pairs + i))

    return pl.pallas_call(
        attention_back_kernel,
        grid=(pairs,),
        in_specs=[
            part(total, 0), part(total, 1), part(total, 2), part(total, 0),
            whole(lse.shape), whole(segments.shape), whole(tokens.shape),
            part(width, 0), part(width, 1), part(width, 2), any_,
        ],
        out_specs=[
            pl.BlockSpec((width, 3 * BLOCK), lambda i: (0, i)),
            pl.BlockSpec((8, BLOCK), lambda i: (0, i)),
            any_,
        ],
        out_shape=[
            jax.ShapeDtypeStruct((width, 3 * width), BF16),
            jax.ShapeDtypeStruct((8, width), F32),
            jax.ShapeDtypeStruct((total, width), F32),
        ],
        scratch_shapes=[
            pltpu.VMEM((width, total), BF16),
            pltpu.VMEM((total, width), F32),
            pltpu.VMEM((count, mask_offsets(length)[1], BLOCK), F32),
            pltpu.VMEM((total, 3 * BLOCK), BF16),
            pltpu.VMEM((length, BLOCK), F32),
            pltpu.VMEM((length, BLOCK), F32),
            pltpu.SemaphoreType.DMA,
        ],
        compiler_params=pltpu.CompilerParams(vmem_limit_bytes=VMEM_LIMIT),
        name="attention_backward",
    )(qkv, qkv, qkv, gcon, lse, segments, tokens, wqkv, wqkv, wqkv, gsum)


def layer(
    tokens, wqkv, bqv, wout, bout, gain_one, shift_one,
    win, bin_, wfin, bfin, gain_two, shift_two, segments, cotangent,
):
    width = tokens.shape[1]
    length = segments.shape[1]
    segments = segments.reshape(segments.shape[0], 1, length)
    bqkv = jnp.concatenate([bqv[:, :width], jnp.zeros_like(bout), bqv[:, width:]], axis=1)
    qkv, context, lse, normed, inverse = attention_forward(tokens, segments, wqkv, wout, bqkv, bout)
    zero = jnp.zeros_like(bfin)
    vectors = jnp.concatenate([gain_one, shift_one, bfin, gain_two, shift_two, zero, zero, zero], axis=0)
    output, act, slope, gsum_two, gffn, low, gvec_two = feed_forward(
        normed, cotangent, win, wfin, vectors, bin_, min(512, tokens.shape[0])
    )
    dwin, dwfin, gbin, ghid = feed_backward(gffn, low, gsum_two, act, slope, win, wfin, 512)
    gsum_one, gcon, dwout, gvec_one = project_backward(
        ghid, normed, inverse, context, wout, gain_one, min(512, tokens.shape[0])
    )
    dwqkv, gvec_qv, gtok = attention_backward(qkv, gcon, lse, segments, tokens, wqkv, gsum_one)
    return (
        output, gtok, dwqkv, gvec_qv[0:2].reshape(1, -1), dwout, gvec_one[2:3], gvec_one[0:1], gvec_one[1:2],
        dwin, gbin[0:1], dwfin, gvec_two[2:3], gvec_two[0:1], gvec_two[1:2],
    )


MESH = pl.DeviceIdType.MESH


def when(condition, body):
    if condition is True:
        body()
    else:
        pl.when(condition)(body)


class Place:
    def __init__(self, planes):
        along = lax.axis_index("dp")
        self.planes = planes
        self.y = lax.axis_index("inner")
        self.c = lax.rem(along, 2)
        self.x = lax.rem(lax.div(along, 2), 2)
        self.z = lax.div(along, 4)

    def device(self, z=None, x=None, c=None, y=None):
        z = self.z if z is None else z
        x = self.x if x is None else x
        c = self.c if c is None else c
        return ((z * 2 + x) * 2 + c, self.y if y is None else y)

    @property
    def above(self):
        return self.device(z=lax.rem(self.z + 1, self.planes))

    @property
    def below(self):
        return self.device(z=lax.rem(self.z + self.planes - 1, self.planes))

    @property
    def across(self):
        return self.device(x=1 - self.x)

    @property
    def beside(self):
        return self.device(y=1 - self.y)

    @property
    def partner(self):
        return self.device(c=1 - self.c)

    @property
    def has_above(self):
        return self.z < self.planes - 1

    @property
    def has_below(self):
        return self.z > 0

    def enter(self):
        barrier = pltpu.get_barrier_semaphore()

        def greet(device):
            pl.semaphore_signal(barrier, inc=1, device_id=device, device_id_type=MESH)

        for device in (self.across, self.beside, self.partner):
            greet(device)
        when(self.has_above, lambda: greet(self.above))
        when(self.has_below, lambda: greet(self.below))
        pl.semaphore_wait(
            barrier, 3 + self.has_above.astype(jnp.int32) + self.has_below.astype(jnp.int32)
        )


def half_of(ref, half):
    if half == 2:
        return ref
    width = ref.shape[-1] // 2
    lead = (slice(None),) * (len(ref.shape) - 1)
    return ref.at[lead + (slice(half * width, (half + 1) * width),)]


SENDS = 48


class Gather:
    def __init__(self, place, index, shard, full, send, recv, local):
        self.place, self.index, self.shard, self.full = place, index, shard, full
        self.send, self.recv, self.local = send, recv, local
        self.halves = (0, 1) if full.shape[-1] % (2 * BLOCK) == 0 else (2, None)
        self.slot = 0
        self.ends = []

    def push(self, condition, item, half, device, source=None):
        slot = self.slot
        self.slot += 1

        def make():
            return pltpu.make_async_remote_copy(
                src_ref=half_of(self.full.at[item] if source is None else source, half),
                dst_ref=half_of(self.full.at[item], half),
                send_sem=self.send.at[self.index, slot],
                recv_sem=self.recv.at[(self.index,) + item + (min(half, 1),)],
                device_id=device,
                device_id_type=MESH,
            )

        when(condition, lambda: make().start())
        self.ends.append((condition, make))

    def await_item(self, item, half):
        ref = half_of(self.full.at[item], half)
        pltpu.make_async_remote_copy(
            src_ref=ref, dst_ref=ref, send_sem=self.send.at[self.index, 0],
            recv_sem=self.recv.at[(self.index,) + item + (min(half, 1),)],
            device_id=self.place.partner, device_id_type=MESH,
        ).wait_recv()

    def own_copy(self):
        p = self.place
        return pltpu.make_async_copy(
            self.shard, self.full.at[p.z, p.x, p.c, p.y], self.local.at[self.index]
        )

    def first(self):
        p = self.place
        item = (p.z, p.x, p.c, p.y)
        self.push(p.has_above, item, 2, p.above, self.shard)
        self.push(p.has_below, item, 2, p.below, self.shard)
        self.push(True, item, 2, p.across, self.shard)
        self.push(True, item, 2, p.beside, self.shard)
        self.push(True, item, 2, p.partner, self.shard)
        self.own_copy().start()

    def planes_at(self, distance):
        p = self.place
        if distance == 0:
            return [(True, p.z, None, None)]
        return [
            (p.z >= distance, p.z - distance, p.has_above, p.above),
            (p.z + distance < p.planes, p.z + distance, p.has_below, p.below),
        ]

    def along_z(self, distance):
        p = self.place
        for there, z, more, onward in self.planes_at(distance):
            item = (jnp.clip(z, 0, p.planes - 1), p.x, p.c, p.y)
            when(there, lambda: self.await_item(item, 2))
            self.push(jnp.logical_and(there, more), item, 2, onward)
            for device in (p.across, p.beside, p.partner):
                self.push(there, item, 2, device)

    def across_xy(self, distance):
        p = self.place
        for there, z, _, _ in self.planes_at(distance):
            z = jnp.clip(z, 0, p.planes - 1)
            for half, item, onward in (
                (self.halves[0], (z, 1 - p.x, p.c, p.y), p.beside),
                (self.halves[1], (z, p.x, p.c, 1 - p.y), p.across),
            ):
                when(there, lambda: self.await_item(item, 2))
                if half is not None:
                    self.push(there, item, half, onward)
                self.push(there, item, 2, p.partner)

    def diagonal(self, distance):
        p = self.place
        for there, z, _, _ in self.planes_at(distance):
            item = (jnp.clip(z, 0, p.planes - 1), 1 - p.x, p.c, 1 - p.y)

            def arrive():
                for half in self.halves:
                    if half is not None:
                        self.await_item(item, half)

            when(there, arrive)
            self.push(there, item, 2, p.partner)

    def finish(self):
        p = self.place
        for z in range(p.planes):
            for x in range(2):
                for y in range(2):
                    self.await_item((z, x, 1 - p.c, y), 2)
        for condition, make in self.ends:
            when(condition, lambda: make().wait_send())
        self.own_copy().wait()


def gather_kernel(planes, count, *refs):
    shards, fulls = refs[:count], refs[count : 2 * count]
    send, recv, local = refs[2 * count :]
    place = Place(planes)
    place.enter()
    gathers = [
        Gather(place, i, shards[i], fulls[i], send, recv, local) for i in range(count)
    ]
    for gather in gathers:
        gather.first()
    for distance in range(1, planes + 2):
        for gather in gathers:
            if distance < planes:
                gather.along_z(distance)
            if distance - 1 < planes:
                gather.across_xy(distance - 1)
            if distance >= 2:
                gather.diagonal(distance - 2)
    for gather in gathers:
        gather.finish()


def gather_all(planes, shards):
    count = len(shards)
    any_ = pl.BlockSpec(memory_space=pl.ANY)
    fulls = pl.pallas_call(
        functools.partial(gather_kernel, planes, count),
        in_specs=[any_] * count,
        out_specs=[any_] * count,
        out_shape=[jax.ShapeDtypeStruct((planes, 2, 2, 2) + s.shape, s.dtype) for s in shards],
        scratch_shapes=[
            pltpu.SemaphoreType.DMA((count, SENDS)),
            pltpu.SemaphoreType.DMA((count, planes, 2, 2, 2, 2)),
            pltpu.SemaphoreType.DMA((count,)),
        ],
        compiler_params=pltpu.CompilerParams(collective_id=0, has_side_effects=True, vmem_limit_bytes=VMEM_LIMIT),
        name="gather_weights",
    )(*shards)
    return [f.reshape((-1,) + f.shape[5:]) for f in fulls]


class Scatter:
    def __init__(self, place, index, source, out, bufs, send, recv, local):
        self.place, self.index, self.source, self.out = place, index, source, out
        self.held, self.from_partner, self.from_diag, self.from_side, self.from_z, self.spare = bufs
        self.send, self.recv, self.local = send, recv, local
        self.split = source.shape[-1] % (2 * BLOCK) == 0

    def copy(self, slot, src, dst, device):
        return pltpu.make_async_remote_copy(
            src_ref=src, dst_ref=dst, send_sem=self.send.at[self.index, slot],
            recv_sem=self.recv.at[self.index, slot], device_id=device, device_id_type=MESH,
        )

    def own_copy(self):
        p = self.place
        return pltpu.make_async_copy(self.source.at[:, :, p.c], self.held, self.local.at[self.index])

    def partner_copy(self):
        p = self.place
        return self.copy(0, self.source.at[:, :, 1 - p.c], self.from_partner, p.partner)

    def diag_copies(self):
        p = self.place
        ref = self.held.at[:, 1 - p.x, 1 - p.y]
        if not self.split:
            return [self.copy(1, ref, self.from_diag.at[0], p.across)]
        return [
            self.copy(1, half_of(ref, 0), self.from_diag.at[0], p.across),
            self.copy(2, half_of(ref, 1), self.from_diag.at[1], p.beside),
        ]

    def side_copies(self):
        p = self.place
        return [
            self.copy(3, self.held.at[:, 1 - p.x, p.y], self.from_side.at[0], p.across),
            self.copy(4, self.held.at[:, p.x, 1 - p.y], self.from_side.at[1], p.beside),
        ]

    def z_copy(self, up, z):
        p = self.place
        return self.copy(
            5 + up * p.planes + z, self.spare.at[z], self.from_z.at[up, z], p.above if up else p.below
        )

    def start(self):
        self.own_copy().start()
        self.partner_copy().start()

    def add(self, x, y, *others):
        def one(z, _):
            total = self.held[z, x, y].astype(F32)
            for other in others:
                total = total + other(z).astype(F32)
            self.held[z, x, y] = total.astype(self.held.dtype)
            return 0

        lax.fori_loop(0, self.place.planes, one, 0)

    def after_partner(self):
        p = self.place
        self.own_copy().wait()
        self.partner_copy().wait_recv()
        for x, y in ((1 - p.x, 1 - p.y), (1 - p.x, p.y), (p.x, 1 - p.y), (p.x, p.y)):
            self.add(x, y, lambda z: self.from_partner[z, x, y])
            if x is not p.x and y is not p.y:
                for copy in self.diag_copies():
                    copy.start()

    def after_diag(self):
        p = self.place
        width = self.held.shape[-1]
        for copy in self.diag_copies():
            copy.wait_recv()
        parts = ((0, p.x, 1 - p.y, 0, width // 2), (1, 1 - p.x, p.y, width // 2, width))
        if not self.split:
            parts = ((0, p.x, 1 - p.y, 0, width),)

        def one(z, _):
            for index, x, y, low, high in parts:
                total = self.held[z, x, y, :, low:high].astype(F32) + self.from_diag[index, z].astype(F32)
                self.held[z, x, y, :, low:high] = total.astype(self.held.dtype)
            return 0

        lax.fori_loop(0, p.planes, one, 0)
        for copy in self.side_copies():
            copy.start()

    def after_side(self):
        p = self.place
        for copy in self.side_copies():
            copy.wait_recv()

        def one(z, _):
            total = self.held[z, p.x, p.y].astype(F32)
            total = total + self.from_side[0, z].astype(F32) + self.from_side[1, z].astype(F32)
            self.spare[z] = total.astype(self.spare.dtype)
            return 0

        lax.fori_loop(0, p.planes, one, 0)
        for z in range(p.planes):
            when(jnp.logical_and(jnp.logical_not(p.has_below), z > p.z), lambda: self.z_copy(1, z).start())
            when(jnp.logical_and(jnp.logical_not(p.has_above), z < p.z), lambda: self.z_copy(0, z).start())

    def along_z(self):
        p = self.place
        for z in range(p.planes):
            def onward(up, z=z):
                self.z_copy(up, z).wait_recv()
                total = self.spare[z].astype(F32) + self.from_z[up, z].astype(F32)
                self.spare[z] = total.astype(self.spare.dtype)
                self.z_copy(up, z).start()

            when(jnp.logical_and(jnp.logical_and(p.has_below, p.has_above), z > p.z), lambda: onward(1))
            when(jnp.logical_and(jnp.logical_and(p.has_below, p.has_above), z < p.z), lambda: onward(0))

    def finish(self, store):
        p = self.place
        store(self.spare[p.z].astype(F32), False)
        for up, there in ((1, p.has_below), (0, p.has_above)):
            def arrive(up=up):
                self.z_copy(up, p.z).wait_recv()
                store(self.from_z[up, p.z].astype(F32), True)

            when(there, arrive)
        self.partner_copy().wait_send()
        for copy in self.diag_copies() + self.side_copies():
            copy.wait_send()
        for z in range(p.planes):
            when(jnp.logical_and(z > p.z, p.has_above), lambda: self.z_copy(1, z).wait_send())
            when(jnp.logical_and(z < p.z, p.has_below), lambda: self.z_copy(0, z).wait_send())


def scatter_scratch(planes, rows, width, dtype):
    split = width % (2 * BLOCK) == 0
    return [
        pltpu.VMEM((planes, 2, 2, rows, width), dtype),
        pltpu.VMEM((planes, 2, 2, rows, width), dtype),
        pltpu.VMEM((2 if split else 1, planes, rows, width // 2 if split else width), dtype),
        pltpu.VMEM((2, planes, rows, width), dtype),
        pltpu.VMEM((2, planes, rows, width), dtype),
        pltpu.VMEM((planes, rows, width), dtype),
    ]


def scatter_kernel(planes, count, *refs):
    sources, outs, rest = refs[:count], refs[count : 2 * count], refs[2 * count :]
    send, recv, local = rest[:3]
    place = Place(planes)
    place.enter()
    scatters = [
        Scatter(place, i, sources[i], outs[i], rest[3 + 6 * i : 9 + 6 * i], send, recv, local)
        for i in range(count)
    ]
    for s in scatters:
        s.start()
    for stage in ("after_partner", "after_diag", "after_side", "along_z"):
        for s in scatters:
            getattr(s, stage)()
    for s in scatters:
        def store(value, more, out=s.out):
            if more:
                out[...] += value
            else:
                out[...] = value

        s.finish(store)


def scatter_all(planes, sources):
    count = len(sources)
    sources = [s.reshape((planes, 2, 2, 2, -1) + s.shape[1:]) for s in sources]
    shapes = [s.shape[4:] for s in sources]
    scratch = []
    for s in sources:
        scratch += scatter_scratch(planes, *s.shape[4:], s.dtype)
    any_ = pl.BlockSpec(memory_space=pl.ANY)
    vmem = pl.BlockSpec(memory_space=pltpu.VMEM)
    return pl.pallas_call(
        functools.partial(scatter_kernel, planes, count),
        in_specs=[any_] * count,
        out_specs=[vmem] * count,
        out_shape=[jax.ShapeDtypeStruct(s, F32) for s in shapes],
        scratch_shapes=[
            pltpu.SemaphoreType.DMA((count, 5 + 2 * planes)),
            pltpu.SemaphoreType.DMA((count, 5 + 2 * planes)),
            pltpu.SemaphoreType.DMA((count,)),
        ] + scratch,
        compiler_params=pltpu.CompilerParams(collective_id=1, has_side_effects=True, vmem_limit_bytes=VMEM_LIMIT),
        name="scatter_gradients",
    )(*sources)


def spread_masks(devices, piece):
    size = devices * piece
    column = lax.broadcasted_iota(jnp.int32, (devices, size), 1)
    start = lax.broadcasted_iota(jnp.int32, (devices, size), 0) * piece
    owner = jnp.logical_and(column >= start, column < start + piece)
    column = lax.broadcasted_iota(jnp.int32, (BLOCK, size), 1)
    number = jnp.floor((column.astype(F32) + 0.5) * (1.0 / piece)).astype(jnp.int32)
    place = column - number * piece == lax.broadcasted_iota(jnp.int32, (BLOCK, size), 0)
    return owner, place.astype(F32)


def spread_kernel(pieces, gathered_ref, *outs):
    devices = gathered_ref.shape[0]
    masks = {piece: spread_masks(devices, piece) for piece in set(pieces)}
    for index, piece in enumerate(pieces):
        owner, place = masks[piece]
        wide = dot_nn(gathered_ref[:, index, :].astype(F32), place)
        outs[index][...] = jnp.sum(jnp.where(owner, wide, 0.0), axis=0, keepdims=True)


def spread_vectors(gathered, pieces):
    devices = gathered.shape[0]
    return pl.pallas_call(
        functools.partial(spread_kernel, pieces),
        out_shape=[jax.ShapeDtypeStruct((1, devices * piece), F32) for piece in pieces],
        compiler_params=pltpu.CompilerParams(vmem_limit_bytes=VMEM_LIMIT),
        name="spread_vectors",
    )(gathered)


def collect_kernel(pieces, devices, *refs):
    out_ref = refs[-1]
    masks = {piece: spread_masks(devices, piece) for piece in set(pieces)}
    for index, piece in enumerate(pieces):
        owner, place = masks[piece]
        wide = jnp.where(owner, refs[index][...], 0.0)
        out_ref[:, index, :] = lax.dot_general(
            wide, place, (((1,), (1,)), ((), ())),
            precision=lax.Precision.HIGHEST, preferred_element_type=F32,
        )


def collect_vectors(vectors, pieces, devices):
    return pl.pallas_call(
        functools.partial(collect_kernel, pieces, devices),
        out_shape=jax.ShapeDtypeStruct((devices, 8, BLOCK), F32),
        compiler_params=pltpu.CompilerParams(vmem_limit_bytes=VMEM_LIMIT),
        name="collect_vectors",
    )(*vectors)


MESH = pl.DeviceIdType.MESH


def when(condition, body):
    if condition is True:
        body()
    else:
        pl.when(condition)(body)


class Place:
    def __init__(self, planes):
        along = lax.axis_index("dp")
        self.planes = planes
        self.y = lax.axis_index("inner")
        self.c = lax.rem(along, 2)
        self.x = lax.rem(lax.div(along, 2), 2)
        self.z = lax.div(along, 4)

    def device(self, z=None, x=None, c=None, y=None):
        z = self.z if z is None else z
        x = self.x if x is None else x
        c = self.c if c is None else c
        return ((z * 2 + x) * 2 + c, self.y if y is None else y)

    @property
    def above(self):
        return self.device(z=lax.rem(self.z + 1, self.planes))

    @property
    def below(self):
        return self.device(z=lax.rem(self.z + self.planes - 1, self.planes))

    @property
    def across(self):
        return self.device(x=1 - self.x)

    @property
    def beside(self):
        return self.device(y=1 - self.y)

    @property
    def partner(self):
        return self.device(c=1 - self.c)

    @property
    def has_above(self):
        return self.z < self.planes - 1

    @property
    def has_below(self):
        return self.z > 0

    def enter(self):
        barrier = pltpu.get_barrier_semaphore()

        def greet(device):
            pl.semaphore_signal(barrier, inc=1, device_id=device, device_id_type=MESH)

        for device in (self.across, self.beside, self.partner):
            greet(device)
        when(self.has_above, lambda: greet(self.above))
        when(self.has_below, lambda: greet(self.below))
        pl.semaphore_wait(
            barrier, 3 + self.has_above.astype(jnp.int32) + self.has_below.astype(jnp.int32)
        )


def half_of(ref, half):
    if half == 2:
        return ref
    width = ref.shape[-1] // 2
    lead = (slice(None),) * (len(ref.shape) - 1)
    return ref.at[lead + (slice(half * width, (half + 1) * width),)]


SENDS = 48


class Gather:
    def __init__(self, place, index, shard, full, send, recv, local):
        self.place, self.index, self.shard, self.full = place, index, shard, full
        self.send, self.recv, self.local = send, recv, local
        self.halves = (0, 1) if full.shape[-1] % (2 * BLOCK) == 0 else (2, None)
        self.slot = 0
        self.ends = []

    def push(self, condition, item, half, device, source=None):
        slot = self.slot
        self.slot += 1

        def make():
            return pltpu.make_async_remote_copy(
                src_ref=half_of(self.full.at[item] if source is None else source, half),
                dst_ref=half_of(self.full.at[item], half),
                send_sem=self.send.at[self.index, slot],
                recv_sem=self.recv.at[(self.index,) + item + (min(half, 1),)],
                device_id=device,
                device_id_type=MESH,
            )

        when(condition, lambda: make().start())
        self.ends.append((condition, make))

    def await_item(self, item, half):
        ref = half_of(self.full.at[item], half)
        pltpu.make_async_remote_copy(
            src_ref=ref, dst_ref=ref, send_sem=self.send.at[self.index, 0],
            recv_sem=self.recv.at[(self.index,) + item + (min(half, 1),)],
            device_id=self.place.partner, device_id_type=MESH,
        ).wait_recv()

    def own_copy(self):
        p = self.place
        return pltpu.make_async_copy(
            self.shard, self.full.at[p.z, p.x, p.c, p.y], self.local.at[self.index]
        )

    def first(self):
        p = self.place
        item = (p.z, p.x, p.c, p.y)
        self.push(p.has_above, item, 2, p.above, self.shard)
        self.push(p.has_below, item, 2, p.below, self.shard)
        self.push(True, item, 2, p.across, self.shard)
        self.push(True, item, 2, p.beside, self.shard)
        self.push(True, item, 2, p.partner, self.shard)
        self.own_copy().start()

    def planes_at(self, distance):
        p = self.place
        if distance == 0:
            return [(True, p.z, None, None)]
        return [
            (p.z >= distance, p.z - distance, p.has_above, p.above),
            (p.z + distance < p.planes, p.z + distance, p.has_below, p.below),
        ]

    def along_z(self, distance):
        p = self.place
        for there, z, more, onward in self.planes_at(distance):
            item = (jnp.clip(z, 0, p.planes - 1), p.x, p.c, p.y)
            when(there, lambda: self.await_item(item, 2))
            self.push(jnp.logical_and(there, more), item, 2, onward)
            for device in (p.across, p.beside, p.partner):
                self.push(there, item, 2, device)

    def across_xy(self, distance):
        p = self.place
        for there, z, _, _ in self.planes_at(distance):
            z = jnp.clip(z, 0, p.planes - 1)
            for half, item, onward in (
                (self.halves[0], (z, 1 - p.x, p.c, p.y), p.beside),
                (self.halves[1], (z, p.x, p.c, 1 - p.y), p.across),
            ):
                when(there, lambda: self.await_item(item, 2))
                if half is not None:
                    self.push(there, item, half, onward)
                self.push(there, item, 2, p.partner)

    def diagonal(self, distance):
        p = self.place
        for there, z, _, _ in self.planes_at(distance):
            item = (jnp.clip(z, 0, p.planes - 1), 1 - p.x, p.c, 1 - p.y)

            def arrive():
                for half in self.halves:
                    if half is not None:
                        self.await_item(item, half)

            when(there, arrive)
            self.push(there, item, 2, p.partner)

    def finish(self):
        p = self.place
        for z in range(p.planes):
            for x in range(2):
                for y in range(2):
                    self.await_item((z, x, 1 - p.c, y), 2)
        for condition, make in self.ends:
            when(condition, lambda: make().wait_send())
        self.own_copy().wait()


def gather_kernel(planes, count, *refs):
    shards, fulls = refs[:count], refs[count : 2 * count]
    send, recv, local = refs[2 * count :]
    place = Place(planes)
    place.enter()
    gathers = [
        Gather(place, i, shards[i], fulls[i], send, recv, local) for i in range(count)
    ]
    for gather in gathers:
        gather.first()
    for distance in range(1, planes + 2):
        for gather in gathers:
            if distance < planes:
                gather.along_z(distance)
            if distance - 1 < planes:
                gather.across_xy(distance - 1)
            if distance >= 2:
                gather.diagonal(distance - 2)
    for gather in gathers:
        gather.finish()


def gather_all(planes, shards):
    count = len(shards)
    any_ = pl.BlockSpec(memory_space=pl.ANY)
    fulls = pl.pallas_call(
        functools.partial(gather_kernel, planes, count),
        in_specs=[any_] * count,
        out_specs=[any_] * count,
        out_shape=[jax.ShapeDtypeStruct((planes, 2, 2, 2) + s.shape, s.dtype) for s in shards],
        scratch_shapes=[
            pltpu.SemaphoreType.DMA((count, SENDS)),
            pltpu.SemaphoreType.DMA((count, planes, 2, 2, 2, 2)),
            pltpu.SemaphoreType.DMA((count,)),
        ],
        compiler_params=pltpu.CompilerParams(collective_id=0, has_side_effects=True, vmem_limit_bytes=VMEM_LIMIT),
        name="gather_weights",
    )(*shards)
    return [f.reshape((-1,) + f.shape[4:]) for f in fulls]


class Scatter:
    def __init__(self, place, index, source, out, bufs, send, recv, local):
        self.place, self.index, self.source, self.out = place, index, source, out
        self.held, self.from_partner, self.from_diag, self.from_side, self.from_z, self.spare = bufs
        self.send, self.recv, self.local = send, recv, local
        self.split = source.shape[-1] % (2 * BLOCK) == 0

    def copy(self, slot, src, dst, device):
        return pltpu.make_async_remote_copy(
            src_ref=src, dst_ref=dst, send_sem=self.send.at[self.index, slot],
            recv_sem=self.recv.at[self.index, slot], device_id=device, device_id_type=MESH,
        )

    def own_copy(self):
        p = self.place
        return pltpu.make_async_copy(self.source.at[:, :, p.c], self.held, self.local.at[self.index])

    def partner_copy(self):
        p = self.place
        return self.copy(0, self.source.at[:, :, 1 - p.c], self.from_partner, p.partner)

    def diag_copies(self):
        p = self.place
        ref = self.held.at[:, 1 - p.x, 1 - p.y]
        if not self.split:
            return [self.copy(1, ref, self.from_diag.at[0], p.across)]
        return [
            self.copy(1, half_of(ref, 0), self.from_diag.at[0], p.across),
            self.copy(2, half_of(ref, 1), self.from_diag.at[1], p.beside),
        ]

    def side_copies(self):
        p = self.place
        return [
            self.copy(3, self.held.at[:, 1 - p.x, p.y], self.from_side.at[0], p.across),
            self.copy(4, self.held.at[:, p.x, 1 - p.y], self.from_side.at[1], p.beside),
        ]

    def z_copy(self, up, z):
        p = self.place
        return self.copy(
            5 + up * p.planes + z, self.spare.at[z], self.from_z.at[up, z], p.above if up else p.below
        )

    def start(self):
        self.own_copy().start()
        self.partner_copy().start()

    def add(self, x, y, *others):
        def one(z, _):
            total = self.held[z, x, y].astype(F32)
            for other in others:
                total = total + other(z).astype(F32)
            self.held[z, x, y] = total.astype(self.held.dtype)
            return 0

        lax.fori_loop(0, self.place.planes, one, 0)

    def after_partner(self):
        p = self.place
        self.own_copy().wait()
        self.partner_copy().wait_recv()
        for x, y in ((1 - p.x, 1 - p.y), (1 - p.x, p.y), (p.x, 1 - p.y), (p.x, p.y)):
            self.add(x, y, lambda z: self.from_partner[z, x, y])
            if x is not p.x and y is not p.y:
                for copy in self.diag_copies():
                    copy.start()

    def after_diag(self):
        p = self.place
        width = self.held.shape[-1]
        for copy in self.diag_copies():
            copy.wait_recv()
        parts = ((0, p.x, 1 - p.y, 0, width // 2), (1, 1 - p.x, p.y, width // 2, width))
        if not self.split:
            parts = ((0, p.x, 1 - p.y, 0, width),)

        def one(z, _):
            for index, x, y, low, high in parts:
                total = self.held[z, x, y, :, low:high].astype(F32) + self.from_diag[index, z].astype(F32)
                self.held[z, x, y, :, low:high] = total.astype(self.held.dtype)
            return 0

        lax.fori_loop(0, p.planes, one, 0)
        for copy in self.side_copies():
            copy.start()

    def after_side(self):
        p = self.place
        for copy in self.side_copies():
            copy.wait_recv()

        def one(z, _):
            total = self.held[z, p.x, p.y].astype(F32)
            total = total + self.from_side[0, z].astype(F32) + self.from_side[1, z].astype(F32)
            self.spare[z] = total.astype(self.spare.dtype)
            return 0

        lax.fori_loop(0, p.planes, one, 0)
        for z in range(p.planes):
            when(jnp.logical_and(jnp.logical_not(p.has_below), z > p.z), lambda: self.z_copy(1, z).start())
            when(jnp.logical_and(jnp.logical_not(p.has_above), z < p.z), lambda: self.z_copy(0, z).start())

    def along_z(self):
        p = self.place
        for z in range(p.planes):
            def onward(up, z=z):
                self.z_copy(up, z).wait_recv()
                total = self.spare[z].astype(F32) + self.from_z[up, z].astype(F32)
                self.spare[z] = total.astype(self.spare.dtype)
                self.z_copy(up, z).start()

            when(jnp.logical_and(jnp.logical_and(p.has_below, p.has_above), z > p.z), lambda: onward(1))
            when(jnp.logical_and(jnp.logical_and(p.has_below, p.has_above), z < p.z), lambda: onward(0))

    def finish(self, store):
        p = self.place
        store(self.spare[p.z].astype(F32), False)
        for up, there in ((1, p.has_below), (0, p.has_above)):
            def arrive(up=up):
                self.z_copy(up, p.z).wait_recv()
                store(self.from_z[up, p.z].astype(F32), True)

            when(there, arrive)
        self.partner_copy().wait_send()
        for copy in self.diag_copies() + self.side_copies():
            copy.wait_send()
        for z in range(p.planes):
            when(jnp.logical_and(z > p.z, p.has_above), lambda: self.z_copy(1, z).wait_send())
            when(jnp.logical_and(z < p.z, p.has_below), lambda: self.z_copy(0, z).wait_send())


def scatter_scratch(planes, rows, width, dtype):
    split = width % (2 * BLOCK) == 0
    return [
        pltpu.VMEM((planes, 2, 2, rows, width), dtype),
        pltpu.VMEM((planes, 2, 2, rows, width), dtype),
        pltpu.VMEM((2 if split else 1, planes, rows, width // 2 if split else width), dtype),
        pltpu.VMEM((2, planes, rows, width), dtype),
        pltpu.VMEM((2, planes, rows, width), dtype),
        pltpu.VMEM((planes, rows, width), dtype),
    ]


def scatter_kernel(planes, count, *refs):
    sources, outs, rest = refs[:count], refs[count : 2 * count], refs[2 * count :]
    send, recv, local = rest[:3]
    place = Place(planes)
    place.enter()
    scatters = [
        Scatter(place, i, sources[i], outs[i], rest[3 + 6 * i : 9 + 6 * i], send, recv, local)
        for i in range(count)
    ]
    for s in scatters:
        s.start()
    for stage in ("after_partner", "after_diag", "after_side", "along_z"):
        for s in scatters:
            getattr(s, stage)()
    for s in scatters:
        def store(value, more, out=s.out):
            if more:
                out[...] += value
            else:
                out[...] = value

        s.finish(store)


def scatter_all(planes, sources):
    count = len(sources)
    sources = [s.reshape((planes, 2, 2, 2, -1) + s.shape[1:]) for s in sources]
    shapes = [s.shape[4:] for s in sources]
    scratch = []
    for s in sources:
        scratch += scatter_scratch(planes, *s.shape[4:], s.dtype)
    any_ = pl.BlockSpec(memory_space=pl.ANY)
    vmem = pl.BlockSpec(memory_space=pltpu.VMEM)
    return pl.pallas_call(
        functools.partial(scatter_kernel, planes, count),
        in_specs=[any_] * count,
        out_specs=[vmem] * count,
        out_shape=[jax.ShapeDtypeStruct(s, F32) for s in shapes],
        scratch_shapes=[
            pltpu.SemaphoreType.DMA((count, 5 + 2 * planes)),
            pltpu.SemaphoreType.DMA((count, 5 + 2 * planes)),
            pltpu.SemaphoreType.DMA((count,)),
        ] + scratch,
        compiler_params=pltpu.CompilerParams(collective_id=1, has_side_effects=True, vmem_limit_bytes=VMEM_LIMIT),
        name="scatter_gradients",
    )(*sources)


def spread_masks(devices, piece):
    size = devices * piece
    column = lax.broadcasted_iota(jnp.int32, (devices, size), 1)
    start = lax.broadcasted_iota(jnp.int32, (devices, size), 0) * piece
    owner = jnp.logical_and(column >= start, column < start + piece)
    column = lax.broadcasted_iota(jnp.int32, (BLOCK, size), 1)
    number = jnp.floor((column.astype(F32) + 0.5) * (1.0 / piece)).astype(jnp.int32)
    place = column - number * piece == lax.broadcasted_iota(jnp.int32, (BLOCK, size), 0)
    return owner, place.astype(F32)


def spread_kernel(pieces, gathered_ref, *outs):
    devices = gathered_ref.shape[0]
    masks = {piece: spread_masks(devices, piece) for piece in set(pieces)}
    for index, piece in enumerate(pieces):
        owner, place = masks[piece]
        wide = dot_nn(gathered_ref[:, index, :].astype(F32), place)
        outs[index][...] = jnp.sum(jnp.where(owner, wide, 0.0), axis=0, keepdims=True)


def spread_vectors(gathered, pieces):
    devices = gathered.shape[0]
    return pl.pallas_call(
        functools.partial(spread_kernel, pieces),
        out_shape=[jax.ShapeDtypeStruct((1, devices * piece), F32) for piece in pieces],
        compiler_params=pltpu.CompilerParams(vmem_limit_bytes=VMEM_LIMIT),
        name="spread_vectors",
    )(gathered)


def collect_kernel(pieces, devices, *refs):
    out_ref = refs[-1]
    masks = {piece: spread_masks(devices, piece) for piece in set(pieces)}
    for index, piece in enumerate(pieces):
        owner, place = masks[piece]
        wide = jnp.where(owner, refs[index][...], 0.0)
        out_ref[:, index, :] = lax.dot_general(
            wide, place, (((1,), (1,)), ((), ())),
            precision=lax.Precision.HIGHEST, preferred_element_type=F32,
        )


def collect_vectors(vectors, pieces, devices):
    return pl.pallas_call(
        functools.partial(collect_kernel, pieces, devices),
        out_shape=jax.ShapeDtypeStruct((devices, 8, BLOCK), F32),
        compiler_params=pltpu.CompilerParams(vmem_limit_bytes=VMEM_LIMIT),
        name="collect_vectors",
    )(*vectors)


MESH = pl.DeviceIdType.MESH


def when(condition, body):
    if condition is True:
        body()
    else:
        pl.when(condition)(body)


class Place:
    def __init__(self, planes):
        along = lax.axis_index("dp")
        self.planes = planes
        self.y = lax.axis_index("inner")
        self.c = lax.rem(along, 2)
        self.x = lax.rem(lax.div(along, 2), 2)
        self.z = lax.div(along, 4)

    def device(self, z=None, x=None, c=None, y=None):
        z = self.z if z is None else z
        x = self.x if x is None else x
        c = self.c if c is None else c
        return ((z * 2 + x) * 2 + c, self.y if y is None else y)

    @property
    def above(self):
        return self.device(z=lax.rem(self.z + 1, self.planes))

    @property
    def below(self):
        return self.device(z=lax.rem(self.z + self.planes - 1, self.planes))

    @property
    def across(self):
        return self.device(x=1 - self.x)

    @property
    def beside(self):
        return self.device(y=1 - self.y)

    @property
    def partner(self):
        return self.device(c=1 - self.c)

    @property
    def has_above(self):
        return self.z < self.planes - 1

    @property
    def has_below(self):
        return self.z > 0

    def enter(self):
        barrier = pltpu.get_barrier_semaphore()

        def greet(device):
            pl.semaphore_signal(barrier, inc=1, device_id=device, device_id_type=MESH)

        for device in (self.across, self.beside, self.partner):
            greet(device)
        when(self.has_above, lambda: greet(self.above))
        when(self.has_below, lambda: greet(self.below))
        pl.semaphore_wait(
            barrier, 3 + self.has_above.astype(jnp.int32) + self.has_below.astype(jnp.int32)
        )


def half_of(ref, half):
    if half == 2:
        return ref
    width = ref.shape[-1] // 2
    lead = (slice(None),) * (len(ref.shape) - 1)
    return ref.at[lead + (slice(half * width, (half + 1) * width),)]


SENDS = 48


class Gather:
    def __init__(self, place, index, shard, full, send, recv, local):
        self.place, self.index, self.shard, self.full = place, index, shard, full
        self.send, self.recv, self.local = send, recv, local
        self.halves = (0, 1) if full.shape[-1] % (2 * BLOCK) == 0 else (2, None)
        self.slot = 0
        self.ends = []

    def push(self, condition, item, half, device, source=None):
        slot = self.slot
        self.slot += 1

        def make():
            return pltpu.make_async_remote_copy(
                src_ref=half_of(self.full.at[item] if source is None else source, half),
                dst_ref=half_of(self.full.at[item], half),
                send_sem=self.send.at[self.index, slot],
                recv_sem=self.recv.at[(self.index,) + item + (min(half, 1),)],
                device_id=device,
                device_id_type=MESH,
            )

        when(condition, lambda: make().start())
        self.ends.append((condition, make))

    def await_item(self, item, half):
        ref = half_of(self.full.at[item], half)
        pltpu.make_async_remote_copy(
            src_ref=ref, dst_ref=ref, send_sem=self.send.at[self.index, 0],
            recv_sem=self.recv.at[(self.index,) + item + (min(half, 1),)],
            device_id=self.place.partner, device_id_type=MESH,
        ).wait_recv()

    def own_copy(self):
        p = self.place
        return pltpu.make_async_copy(
            self.shard, self.full.at[p.z, p.x, p.c, p.y], self.local.at[self.index]
        )

    def first(self):
        p = self.place
        item = (p.z, p.x, p.c, p.y)
        self.push(p.has_above, item, 2, p.above, self.shard)
        self.push(p.has_below, item, 2, p.below, self.shard)
        self.push(True, item, 2, p.across, self.shard)
        self.push(True, item, 2, p.beside, self.shard)
        self.push(True, item, 2, p.partner, self.shard)
        self.own_copy().start()

    def planes_at(self, distance):
        p = self.place
        if distance == 0:
            return [(True, p.z, None, None)]
        return [
            (p.z >= distance, p.z - distance, p.has_above, p.above),
            (p.z + distance < p.planes, p.z + distance, p.has_below, p.below),
        ]

    def along_z(self, distance):
        p = self.place
        for there, z, more, onward in self.planes_at(distance):
            item = (jnp.clip(z, 0, p.planes - 1), p.x, p.c, p.y)
            when(there, lambda: self.await_item(item, 2))
            self.push(jnp.logical_and(there, more), item, 2, onward)
            for device in (p.across, p.beside, p.partner):
                self.push(there, item, 2, device)

    def across_xy(self, distance):
        p = self.place
        for there, z, _, _ in self.planes_at(distance):
            z = jnp.clip(z, 0, p.planes - 1)
            for half, item, onward in (
                (self.halves[0], (z, 1 - p.x, p.c, p.y), p.beside),
                (self.halves[1], (z, p.x, p.c, 1 - p.y), p.across),
            ):
                when(there, lambda: self.await_item(item, 2))
                if half is not None:
                    self.push(there, item, half, onward)
                self.push(there, item, 2, p.partner)

    def diagonal(self, distance):
        p = self.place
        for there, z, _, _ in self.planes_at(distance):
            item = (jnp.clip(z, 0, p.planes - 1), 1 - p.x, p.c, 1 - p.y)

            def arrive():
                for half in self.halves:
                    if half is not None:
                        self.await_item(item, half)

            when(there, arrive)
            self.push(there, item, 2, p.partner)

    def finish(self):
        p = self.place
        for z in range(p.planes):
            for x in range(2):
                for y in range(2):
                    self.await_item((z, x, 1 - p.c, y), 2)
        for condition, make in self.ends:
            when(condition, lambda: make().wait_send())
        self.own_copy().wait()


def gather_kernel(planes, count, *refs):
    shards, fulls = refs[:count], refs[count : 2 * count]
    send, recv, local = refs[2 * count :]
    place = Place(planes)
    place.enter()
    gathers = [
        Gather(place, i, shards[i], fulls[i], send, recv, local) for i in range(count)
    ]
    for gather in gathers:
        gather.first()
    for distance in range(1, planes + 2):
        for gather in gathers:
            if distance < planes:
                gather.along_z(distance)
            if distance - 1 < planes:
                gather.across_xy(distance - 1)
            if distance >= 2:
                gather.diagonal(distance - 2)
    for gather in gathers:
        gather.finish()


def gather_all(planes, shards):
    count = len(shards)
    any_ = pl.BlockSpec(memory_space=pl.ANY)
    fulls = pl.pallas_call(
        functools.partial(gather_kernel, planes, count),
        in_specs=[any_] * count,
        out_specs=[any_] * count,
        out_shape=[jax.ShapeDtypeStruct((planes, 2, 2, 2) + s.shape, s.dtype) for s in shards],
        scratch_shapes=[
            pltpu.SemaphoreType.DMA((count, SENDS)),
            pltpu.SemaphoreType.DMA((count, planes, 2, 2, 2, 2)),
            pltpu.SemaphoreType.DMA((count,)),
        ],
        compiler_params=pltpu.CompilerParams(collective_id=0, has_side_effects=True, vmem_limit_bytes=VMEM_LIMIT),
        name="gather_weights",
    )(*shards)
    return [f.reshape((-1,) + f.shape[4:]) for f in fulls]


class Scatter:
    def __init__(self, place, index, source, out, bufs, send, recv, local):
        self.place, self.index, self.source, self.out = place, index, source, out
        self.held, self.from_partner, self.from_diag, self.from_side, self.from_z, self.spare = bufs
        self.send, self.recv, self.local = send, recv, local
        self.split = source.shape[-1] % (2 * BLOCK) == 0

    def copy(self, slot, src, dst, device):
        return pltpu.make_async_remote_copy(
            src_ref=src, dst_ref=dst, send_sem=self.send.at[self.index, slot],
            recv_sem=self.recv.at[self.index, slot], device_id=device, device_id_type=MESH,
        )

    def own_copy(self):
        p = self.place
        return pltpu.make_async_copy(self.source.at[:, :, p.c], self.held, self.local.at[self.index])

    def partner_copy(self):
        p = self.place
        return self.copy(0, self.source.at[:, :, 1 - p.c], self.from_partner, p.partner)

    def diag_copies(self):
        p = self.place
        ref = self.held.at[:, 1 - p.x, 1 - p.y]
        if not self.split:
            return [self.copy(1, ref, self.from_diag.at[0], p.across)]
        return [
            self.copy(1, half_of(ref, 0), self.from_diag.at[0], p.across),
            self.copy(2, half_of(ref, 1), self.from_diag.at[1], p.beside),
        ]

    def side_copies(self):
        p = self.place
        return [
            self.copy(3, self.held.at[:, 1 - p.x, p.y], self.from_side.at[0], p.across),
            self.copy(4, self.held.at[:, p.x, 1 - p.y], self.from_side.at[1], p.beside),
        ]

    def z_copy(self, up, z):
        p = self.place
        return self.copy(
            5 + up * p.planes + z, self.spare.at[z], self.from_z.at[up, z], p.above if up else p.below
        )

    def start(self):
        self.own_copy().start()
        self.partner_copy().start()

    def add(self, x, y, *others):
        def one(z, _):
            total = self.held[z, x, y].astype(F32)
            for other in others:
                total = total + other(z).astype(F32)
            self.held[z, x, y] = total.astype(self.held.dtype)
            return 0

        lax.fori_loop(0, self.place.planes, one, 0)

    def after_partner(self):
        p = self.place
        self.own_copy().wait()
        self.partner_copy().wait_recv()
        for x, y in ((1 - p.x, 1 - p.y), (1 - p.x, p.y), (p.x, 1 - p.y), (p.x, p.y)):
            self.add(x, y, lambda z: self.from_partner[z, x, y])
            if x is not p.x and y is not p.y:
                for copy in self.diag_copies():
                    copy.start()

    def after_diag(self):
        p = self.place
        width = self.held.shape[-1]
        for copy in self.diag_copies():
            copy.wait_recv()
        parts = ((0, p.x, 1 - p.y, 0, width // 2), (1, 1 - p.x, p.y, width // 2, width))
        if not self.split:
            parts = ((0, p.x, 1 - p.y, 0, width),)

        def one(z, _):
            for index, x, y, low, high in parts:
                total = self.held[z, x, y, :, low:high].astype(F32) + self.from_diag[index, z].astype(F32)
                self.held[z, x, y, :, low:high] = total.astype(self.held.dtype)
            return 0

        lax.fori_loop(0, p.planes, one, 0)
        for copy in self.side_copies():
            copy.start()

    def after_side(self):
        p = self.place
        for copy in self.side_copies():
            copy.wait_recv()

        def one(z, _):
            total = self.held[z, p.x, p.y].astype(F32)
            total = total + self.from_side[0, z].astype(F32) + self.from_side[1, z].astype(F32)
            self.spare[z] = total.astype(self.spare.dtype)
            return 0

        lax.fori_loop(0, p.planes, one, 0)
        for z in range(p.planes):
            when(jnp.logical_and(jnp.logical_not(p.has_below), z > p.z), lambda: self.z_copy(1, z).start())
            when(jnp.logical_and(jnp.logical_not(p.has_above), z < p.z), lambda: self.z_copy(0, z).start())

    def along_z(self):
        p = self.place
        for z in range(p.planes):
            def onward(up, z=z):
                self.z_copy(up, z).wait_recv()
                total = self.spare[z].astype(F32) + self.from_z[up, z].astype(F32)
                self.spare[z] = total.astype(self.spare.dtype)
                self.z_copy(up, z).start()

            when(jnp.logical_and(jnp.logical_and(p.has_below, p.has_above), z > p.z), lambda: onward(1))
            when(jnp.logical_and(jnp.logical_and(p.has_below, p.has_above), z < p.z), lambda: onward(0))

    def finish(self, store):
        p = self.place
        store(self.spare[p.z].astype(F32), False)
        for up, there in ((1, p.has_below), (0, p.has_above)):
            def arrive(up=up):
                self.z_copy(up, p.z).wait_recv()
                store(self.from_z[up, p.z].astype(F32), True)

            when(there, arrive)
        self.partner_copy().wait_send()
        for copy in self.diag_copies() + self.side_copies():
            copy.wait_send()
        for z in range(p.planes):
            when(jnp.logical_and(z > p.z, p.has_above), lambda: self.z_copy(1, z).wait_send())
            when(jnp.logical_and(z < p.z, p.has_below), lambda: self.z_copy(0, z).wait_send())


def scatter_scratch(planes, rows, width, dtype):
    split = width % (2 * BLOCK) == 0
    return [
        pltpu.VMEM((planes, 2, 2, rows, width), dtype),
        pltpu.VMEM((planes, 2, 2, rows, width), dtype),
        pltpu.VMEM((2 if split else 1, planes, rows, width // 2 if split else width), dtype),
        pltpu.VMEM((2, planes, rows, width), dtype),
        pltpu.VMEM((2, planes, rows, width), dtype),
        pltpu.VMEM((planes, rows, width), dtype),
    ]


def scatter_kernel(planes, count, *refs):
    sources, outs, rest = refs[:count], refs[count : 2 * count], refs[2 * count :]
    send, recv, local = rest[:3]
    place = Place(planes)
    place.enter()
    scatters = [
        Scatter(place, i, sources[i], outs[i], rest[3 + 6 * i : 9 + 6 * i], send, recv, local)
        for i in range(count)
    ]
    for s in scatters:
        s.start()
    for stage in ("after_partner", "after_diag", "after_side", "along_z"):
        for s in scatters:
            getattr(s, stage)()
    for s in scatters:
        def store(value, more, out=s.out):
            if more:
                out[...] += value
            else:
                out[...] = value

        s.finish(store)


def scatter_all(planes, sources):
    count = len(sources)
    sources = [s.reshape((planes, 2, 2, 2) + s.shape[1:]) for s in sources]
    shapes = [s.shape[4:] for s in sources]
    scratch = []
    for s in sources:
        scratch += scatter_scratch(planes, *s.shape[4:], s.dtype)
    any_ = pl.BlockSpec(memory_space=pl.ANY)
    vmem = pl.BlockSpec(memory_space=pltpu.VMEM)
    return pl.pallas_call(
        functools.partial(scatter_kernel, planes, count),
        in_specs=[any_] * count,
        out_specs=[vmem] * count,
        out_shape=[jax.ShapeDtypeStruct(s, F32) for s in shapes],
        scratch_shapes=[
            pltpu.SemaphoreType.DMA((count, 5 + 2 * planes)),
            pltpu.SemaphoreType.DMA((count, 5 + 2 * planes)),
            pltpu.SemaphoreType.DMA((count,)),
        ] + scratch,
        compiler_params=pltpu.CompilerParams(collective_id=1, has_side_effects=True, vmem_limit_bytes=VMEM_LIMIT),
        name="scatter_gradients",
    )(*sources)


def spread_masks(devices, piece):
    size = devices * piece
    column = lax.broadcasted_iota(jnp.int32, (devices, size), 1)
    start = lax.broadcasted_iota(jnp.int32, (devices, size), 0) * piece
    owner = jnp.logical_and(column >= start, column < start + piece)
    column = lax.broadcasted_iota(jnp.int32, (BLOCK, size), 1)
    number = jnp.floor((column.astype(F32) + 0.5) * (1.0 / piece)).astype(jnp.int32)
    place = column - number * piece == lax.broadcasted_iota(jnp.int32, (BLOCK, size), 0)
    return owner, place.astype(F32)


def spread_kernel(pieces, gathered_ref, *outs):
    devices = gathered_ref.shape[0]
    masks = {piece: spread_masks(devices, piece) for piece in set(pieces)}
    for index, piece in enumerate(pieces):
        owner, place = masks[piece]
        wide = dot_nn(gathered_ref[:, index, :].astype(F32), place)
        outs[index][...] = jnp.sum(jnp.where(owner, wide, 0.0), axis=0, keepdims=True)


def spread_vectors(gathered, pieces):
    devices = gathered.shape[0]
    return pl.pallas_call(
        functools.partial(spread_kernel, pieces),
        out_shape=[jax.ShapeDtypeStruct((1, devices * piece), F32) for piece in pieces],
        compiler_params=pltpu.CompilerParams(vmem_limit_bytes=VMEM_LIMIT),
        name="spread_vectors",
    )(gathered)


def collect_kernel(pieces, devices, *refs):
    out_ref = refs[-1]
    masks = {piece: spread_masks(devices, piece) for piece in set(pieces)}
    for index, piece in enumerate(pieces):
        owner, place = masks[piece]
        wide = jnp.where(owner, refs[index][...], 0.0)
        out_ref[:, index, :] = lax.dot_general(
            wide, place, (((1,), (1,)), ((), ())),
            precision=lax.Precision.HIGHEST, preferred_element_type=F32,
        )


def collect_vectors(vectors, pieces, devices):
    return pl.pallas_call(
        functools.partial(collect_kernel, pieces, devices),
        out_shape=jax.ShapeDtypeStruct((devices, 8, BLOCK), F32),
        compiler_params=pltpu.CompilerParams(vmem_limit_bytes=VMEM_LIMIT),
        name="collect_vectors",
    )(*vectors)


MESH = pl.DeviceIdType.MESH


def when(condition, body):
    if condition is True:
        body()
    else:
        pl.when(condition)(body)


class Place:
    def __init__(self, planes):
        along = lax.axis_index("dp")
        self.planes = planes
        self.y = lax.axis_index("inner")
        self.c = lax.rem(along, 2)
        self.x = lax.rem(lax.div(along, 2), 2)
        self.z = lax.div(along, 4)

    def device(self, z=None, x=None, c=None, y=None):
        z = self.z if z is None else z
        x = self.x if x is None else x
        c = self.c if c is None else c
        return ((z * 2 + x) * 2 + c, self.y if y is None else y)

    @property
    def above(self):
        return self.device(z=lax.rem(self.z + 1, self.planes))

    @property
    def below(self):
        return self.device(z=lax.rem(self.z + self.planes - 1, self.planes))

    @property
    def across(self):
        return self.device(x=1 - self.x)

    @property
    def beside(self):
        return self.device(y=1 - self.y)

    @property
    def partner(self):
        return self.device(c=1 - self.c)

    @property
    def has_above(self):
        return self.z < self.planes - 1

    @property
    def has_below(self):
        return self.z > 0

    def enter(self):
        barrier = pltpu.get_barrier_semaphore()

        def greet(device):
            pl.semaphore_signal(barrier, inc=1, device_id=device, device_id_type=MESH)

        for device in (self.across, self.beside, self.partner):
            greet(device)
        when(self.has_above, lambda: greet(self.above))
        when(self.has_below, lambda: greet(self.below))
        pl.semaphore_wait(
            barrier, 3 + self.has_above.astype(jnp.int32) + self.has_below.astype(jnp.int32)
        )


def half_of(ref, half):
    if half == 2:
        return ref
    width = ref.shape[-1] // 2
    lead = (slice(None),) * (len(ref.shape) - 1)
    return ref.at[lead + (slice(half * width, (half + 1) * width),)]


SENDS = 64


class Gather:
    def __init__(self, place, index, shard, full, send, recv, local):
        self.place, self.index, self.shard, self.full = place, index, shard, full
        self.send, self.recv, self.local = send, recv, local
        self.halves = (0, 1) if full.shape[-1] % (2 * BLOCK) == 0 else (2, None)
        self.slot = 0
        self.ends = []

    def push(self, condition, item, half, device, source=None):
        slot = self.slot
        self.slot += 1
        assert slot < SENDS

        def make():
            return pltpu.make_async_remote_copy(
                src_ref=half_of(self.full.at[item] if source is None else source, half),
                dst_ref=half_of(self.full.at[item], half),
                send_sem=self.send.at[self.index, slot],
                recv_sem=self.recv.at[(self.index,) + item + (min(half, 1),)],
                device_id=device,
                device_id_type=MESH,
            )

        when(condition, lambda: make().start())
        self.ends.append((condition, make))

    def await_item(self, item, half):
        ref = half_of(self.full.at[item], half)
        pltpu.make_async_remote_copy(
            src_ref=ref, dst_ref=ref, send_sem=self.send.at[self.index, 0],
            recv_sem=self.recv.at[(self.index,) + item + (min(half, 1),)],
            device_id=self.place.partner, device_id_type=MESH,
        ).wait_recv()

    def own_copy(self):
        p = self.place
        return pltpu.make_async_copy(
            self.shard, self.full.at[p.z, p.x, p.c, p.y], self.local.at[self.index]
        )

    def first(self):
        p = self.place
        item = (p.z, p.x, p.c, p.y)
        self.push(p.has_above, item, 2, p.above, self.shard)
        self.push(p.has_below, item, 2, p.below, self.shard)
        self.push(True, item, 2, p.across, self.shard)
        self.push(True, item, 2, p.beside, self.shard)
        self.push(True, item, 2, p.partner, self.shard)
        self.own_copy().start()

    def planes_at(self, distance):
        p = self.place
        if distance == 0:
            return [(True, p.z, None, None)]
        return [
            (p.z >= distance, p.z - distance, p.has_above, p.above),
            (p.z + distance < p.planes, p.z + distance, p.has_below, p.below),
        ]

    def along_z(self, distance):
        p = self.place
        for there, z, more, onward in self.planes_at(distance):
            item = (jnp.clip(z, 0, p.planes - 1), p.x, p.c, p.y)
            when(there, lambda: self.await_item(item, 2))
            self.push(jnp.logical_and(there, more), item, 2, onward)
            for device in (p.across, p.beside, p.partner):
                self.push(there, item, 2, device)

    def across_xy(self, distance):
        p = self.place
        for there, z, _, _ in self.planes_at(distance):
            z = jnp.clip(z, 0, p.planes - 1)
            for half, item, onward in (
                (self.halves[0], (z, 1 - p.x, p.c, p.y), p.beside),
                (self.halves[1], (z, p.x, p.c, 1 - p.y), p.across),
            ):
                when(there, lambda: self.await_item(item, 2))
                if half is not None:
                    self.push(there, item, half, onward)
                self.push(there, item, 2, p.partner)

    def diagonal(self, distance):
        p = self.place
        for there, z, _, _ in self.planes_at(distance):
            item = (jnp.clip(z, 0, p.planes - 1), 1 - p.x, p.c, 1 - p.y)

            def arrive():
                for half in self.halves:
                    if half is not None:
                        self.await_item(item, half)

            when(there, arrive)
            self.push(there, item, 2, p.partner)

    def finish(self):
        p = self.place
        for z in range(p.planes):
            for x in range(2):
                for y in range(2):
                    self.await_item((z, x, 1 - p.c, y), 2)
        for condition, make in self.ends:
            when(condition, lambda: make().wait_send())
        self.own_copy().wait()


def gather_kernel(planes, count, *refs):
    shards, fulls = refs[:count], refs[count : 2 * count]
    send, recv, local = refs[2 * count :]
    place = Place(planes)
    place.enter()
    gathers = [
        Gather(place, i, shards[i], fulls[i], send, recv, local) for i in range(count)
    ]
    for gather in gathers:
        gather.first()
    for distance in range(1, planes + 2):
        for gather in gathers:
            if distance < planes:
                gather.along_z(distance)
            if distance - 1 < planes:
                gather.across_xy(distance - 1)
            if distance >= 2:
                gather.diagonal(distance - 2)
    for gather in gathers:
        gather.finish()


def gather_all(planes, shards):
    count = len(shards)
    any_ = pl.BlockSpec(memory_space=pl.ANY)
    fulls = pl.pallas_call(
        functools.partial(gather_kernel, planes, count),
        in_specs=[any_] * count,
        out_specs=[any_] * count,
        out_shape=[jax.ShapeDtypeStruct((planes, 2, 2, 2) + s.shape, s.dtype) for s in shards],
        scratch_shapes=[
            pltpu.SemaphoreType.DMA((count, SENDS)),
            pltpu.SemaphoreType.DMA((count, planes, 2, 2, 2, 2)),
            pltpu.SemaphoreType.DMA((count,)),
        ],
        compiler_params=pltpu.CompilerParams(collective_id=0, has_side_effects=True, vmem_limit_bytes=VMEM_LIMIT),
        name="gather_weights",
    )(*shards)
    return [f.reshape((-1,) + f.shape[4:]) for f in fulls]


class Scatter:
    def __init__(self, place, index, source, out, bufs, send, recv, local):
        self.place, self.index, self.source, self.out = place, index, source, out
        self.held, self.from_partner, self.from_diag, self.from_side, self.from_z, self.spare = bufs
        self.send, self.recv, self.local = send, recv, local
        self.split = source.shape[-1] % (2 * BLOCK) == 0

    def copy(self, slot, src, dst, device):
        return pltpu.make_async_remote_copy(
            src_ref=src, dst_ref=dst, send_sem=self.send.at[self.index, slot],
            recv_sem=self.recv.at[self.index, slot], device_id=device, device_id_type=MESH,
        )

    def own_copy(self):
        p = self.place
        return pltpu.make_async_copy(self.source.at[:, :, p.c], self.held, self.local.at[self.index])

    def partner_copy(self):
        p = self.place
        return self.copy(0, self.source.at[:, :, 1 - p.c], self.from_partner, p.partner)

    def diag_copies(self):
        p = self.place
        ref = self.held.at[:, 1 - p.x, 1 - p.y]
        if not self.split:
            return [self.copy(1, ref, self.from_diag.at[0], p.across)]
        return [
            self.copy(1, half_of(ref, 0), self.from_diag.at[0], p.across),
            self.copy(2, half_of(ref, 1), self.from_diag.at[1], p.beside),
        ]

    def side_copies(self):
        p = self.place
        return [
            self.copy(3, self.held.at[:, 1 - p.x, p.y], self.from_side.at[0], p.across),
            self.copy(4, self.held.at[:, p.x, 1 - p.y], self.from_side.at[1], p.beside),
        ]

    def z_copy(self, up, z):
        p = self.place
        return self.copy(
            5 + up * p.planes + z, self.spare.at[z], self.from_z.at[up, z], p.above if up else p.below
        )

    def start(self):
        self.own_copy().start()
        self.partner_copy().start()

    def add(self, x, y, *others):
        def one(z, _):
            total = self.held[z, x, y].astype(F32)
            for other in others:
                total = total + other(z).astype(F32)
            self.held[z, x, y] = total.astype(self.held.dtype)
            return 0

        lax.fori_loop(0, self.place.planes, one, 0)

    def after_partner(self):
        p = self.place
        self.own_copy().wait()
        self.partner_copy().wait_recv()
        for x, y in ((1 - p.x, 1 - p.y), (1 - p.x, p.y), (p.x, 1 - p.y), (p.x, p.y)):
            self.add(x, y, lambda z: self.from_partner[z, x, y])
            if x is not p.x and y is not p.y:
                for copy in self.diag_copies():
                    copy.start()

    def after_diag(self):
        p = self.place
        width = self.held.shape[-1]
        for copy in self.diag_copies():
            copy.wait_recv()
        parts = ((0, p.x, 1 - p.y, 0, width // 2), (1, 1 - p.x, p.y, width // 2, width))
        if not self.split:
            parts = ((0, p.x, 1 - p.y, 0, width),)

        def one(z, _):
            for index, x, y, low, high in parts:
                total = self.held[z, x, y, :, low:high].astype(F32) + self.from_diag[index, z].astype(F32)
                self.held[z, x, y, :, low:high] = total.astype(self.held.dtype)
            return 0

        lax.fori_loop(0, p.planes, one, 0)
        for copy in self.side_copies():
            copy.start()

    def after_side(self):
        p = self.place
        for copy in self.side_copies():
            copy.wait_recv()

        def one(z, _):
            total = self.held[z, p.x, p.y].astype(F32)
            total = total + self.from_side[0, z].astype(F32) + self.from_side[1, z].astype(F32)
            self.spare[z] = total.astype(self.spare.dtype)
            return 0

        lax.fori_loop(0, p.planes, one, 0)
        for z in range(p.planes):
            when(jnp.logical_and(jnp.logical_not(p.has_below), z > p.z), lambda: self.z_copy(1, z).start())
            when(jnp.logical_and(jnp.logical_not(p.has_above), z < p.z), lambda: self.z_copy(0, z).start())

    def along_z(self):
        p = self.place
        for z in range(p.planes):
            def onward(up, z=z):
                self.z_copy(up, z).wait_recv()
                total = self.spare[z].astype(F32) + self.from_z[up, z].astype(F32)
                self.spare[z] = total.astype(self.spare.dtype)
                self.z_copy(up, z).start()

            when(jnp.logical_and(jnp.logical_and(p.has_below, p.has_above), z > p.z), lambda: onward(1))
            when(jnp.logical_and(jnp.logical_and(p.has_below, p.has_above), z < p.z), lambda: onward(0))

    def finish(self, store):
        p = self.place
        store(self.spare[p.z].astype(F32), False)
        for up, there in ((1, p.has_below), (0, p.has_above)):
            def arrive(up=up):
                self.z_copy(up, p.z).wait_recv()
                store(self.from_z[up, p.z].astype(F32), True)

            when(there, arrive)
        self.partner_copy().wait_send()
        for copy in self.diag_copies() + self.side_copies():
            copy.wait_send()
        for z in range(p.planes):
            when(jnp.logical_and(z > p.z, p.has_above), lambda: self.z_copy(1, z).wait_send())
            when(jnp.logical_and(z < p.z, p.has_below), lambda: self.z_copy(0, z).wait_send())


def scatter_scratch(planes, rows, width, dtype):
    split = width % (2 * BLOCK) == 0
    return [
        pltpu.VMEM((planes, 2, 2, rows, width), dtype),
        pltpu.VMEM((planes, 2, 2, rows, width), dtype),
        pltpu.VMEM((2 if split else 1, planes, rows, width // 2 if split else width), dtype),
        pltpu.VMEM((2, planes, rows, width), dtype),
        pltpu.VMEM((2, planes, rows, width), dtype),
        pltpu.VMEM((planes, rows, width), dtype),
    ]


def scatter_kernel(planes, count, *refs):
    sources, outs, rest = refs[:count], refs[count : 2 * count], refs[2 * count :]
    send, recv, local = rest[:3]
    place = Place(planes)
    place.enter()
    scatters = [
        Scatter(place, i, sources[i], outs[i], rest[3 + 6 * i : 9 + 6 * i], send, recv, local)
        for i in range(count)
    ]
    for s in scatters:
        s.start()
    for stage in ("after_partner", "after_diag", "after_side", "along_z"):
        for s in scatters:
            getattr(s, stage)()
    for s in scatters:
        def store(value, more, out=s.out):
            if more:
                out[...] += value
            else:
                out[...] = value

        s.finish(store)


def scatter_all(planes, sources):
    count = len(sources)
    sources = [s.reshape((planes, 2, 2, 2) + s.shape[1:]) for s in sources]
    shapes = [s.shape[4:] for s in sources]
    scratch = []
    for s in sources:
        scratch += scatter_scratch(planes, *s.shape[4:], s.dtype)
    any_ = pl.BlockSpec(memory_space=pl.ANY)
    vmem = pl.BlockSpec(memory_space=pltpu.VMEM)
    return pl.pallas_call(
        functools.partial(scatter_kernel, planes, count),
        in_specs=[any_] * count,
        out_specs=[vmem] * count,
        out_shape=[jax.ShapeDtypeStruct(s, F32) for s in shapes],
        scratch_shapes=[
            pltpu.SemaphoreType.DMA((count, 5 + 2 * planes)),
            pltpu.SemaphoreType.DMA((count, 5 + 2 * planes)),
            pltpu.SemaphoreType.DMA((count,)),
        ] + scratch,
        compiler_params=pltpu.CompilerParams(collective_id=1, has_side_effects=True, vmem_limit_bytes=VMEM_LIMIT),
        name="scatter_gradients",
    )(*sources)


def spread_masks(devices, piece):
    size = devices * piece
    column = lax.broadcasted_iota(jnp.int32, (devices, size), 1)
    start = lax.broadcasted_iota(jnp.int32, (devices, size), 0) * piece
    owner = jnp.logical_and(column >= start, column < start + piece)
    column = lax.broadcasted_iota(jnp.int32, (BLOCK, size), 1)
    number = jnp.floor((column.astype(F32) + 0.5) * (1.0 / piece)).astype(jnp.int32)
    place = column - number * piece == lax.broadcasted_iota(jnp.int32, (BLOCK, size), 0)
    return owner, place.astype(F32)


def spread_kernel(pieces, gathered_ref, *outs):
    devices = gathered_ref.shape[0]
    masks = {piece: spread_masks(devices, piece) for piece in set(pieces)}
    for index, piece in enumerate(pieces):
        owner, place = masks[piece]
        wide = dot_nn(gathered_ref[:, index, :].astype(F32), place)
        outs[index][...] = jnp.sum(jnp.where(owner, wide, 0.0), axis=0, keepdims=True)


def spread_vectors(gathered, pieces):
    devices = gathered.shape[0]
    return pl.pallas_call(
        functools.partial(spread_kernel, pieces),
        out_shape=[jax.ShapeDtypeStruct((1, devices * piece), F32) for piece in pieces],
        compiler_params=pltpu.CompilerParams(vmem_limit_bytes=VMEM_LIMIT),
        name="spread_vectors",
    )(gathered)


def collect_kernel(pieces, devices, *refs):
    out_ref = refs[-1]
    masks = {piece: spread_masks(devices, piece) for piece in set(pieces)}
    for index, piece in enumerate(pieces):
        owner, place = masks[piece]
        wide = jnp.where(owner, refs[index][...], 0.0)
        out_ref[:, index, :] = lax.dot_general(
            wide, place, (((1,), (1,)), ((), ())),
            precision=lax.Precision.HIGHEST, preferred_element_type=F32,
        )


def collect_vectors(vectors, pieces, devices):
    return pl.pallas_call(
        functools.partial(collect_kernel, pieces, devices),
        out_shape=jax.ShapeDtypeStruct((devices, 8, BLOCK), F32),
        compiler_params=pltpu.CompilerParams(vmem_limit_bytes=VMEM_LIMIT),
        name="collect_vectors",
    )(*vectors)


AXES = ("dp", "inner")


def shards(
    planes,
    tokens, weight_qkv, bias_qv, weight_out, bias_out, gain_one, shift_one,
    weight_in, bias_in, weight_fin, bias_fin, gain_two, shift_two, segments, cotangent,
):
    vectors = (bias_qv, bias_out, gain_one, shift_one, bias_in, bias_fin, gain_two, shift_two)
    pieces = tuple(v.shape[0] for v in vectors)
    joined = jnp.stack([jnp.pad(v, (0, BLOCK - v.shape[0])) for v in vectors])
    local = [weight_qkv, weight_out, weight_in, weight_fin, joined]
    if planes:
        full = gather_all(planes, local)
    else:
        full = [lax.all_gather(w, AXES, axis=0) for w in local]
    devices = full[0].shape[0]
    rows = spread_vectors(full[4], pieces)
    full = [f.reshape(-1, f.shape[2]) for f in full[:4]]
    out = layer(
        tokens, full[0], rows[0], full[1], rows[1], rows[2], rows[3],
        full[2], rows[4], full[3], rows[5], rows[6], rows[7], segments, cotangent,
    )
    small = collect_vectors([out[i] for i in (3, 5, 6, 7, 9, 11, 12, 13)], pieces, devices)
    large = [g.reshape(devices, -1, g.shape[1]) for g in (out[2], out[4], out[8], out[10])]
    if planes:
        sums = scatter_all(planes, large + [small])
    else:
        sums = [
            lax.psum_scatter(g, AXES, scatter_dimension=0).astype(F32) for g in large + [small]
        ]
    parts = [sums[4][i, :piece] for i, piece in enumerate(pieces)]
    dwqkv = sums[0].reshape(sums[0].shape[0], -1, 3, BLOCK).swapaxes(1, 2).reshape(sums[0].shape)
    return (
        out[0], out[1], dwqkv, parts[0], sums[1], parts[1], parts[2], parts[3],
        sums[2], parts[4], sums[3], parts[5], parts[6], parts[7],
    )


def solution(mesh):
    row, vec = P(AXES, None), P(AXES)
    in_specs = (row, row, vec, row, vec, vec, vec, row, vec, row, vec, vec, vec, row, row)
    out_specs = (row, row, row, vec, row, vec, vec, vec, row, vec, row, vec, vec, vec)
    planes = mesh.shape["dp"] // 4 if mesh.shape["inner"] == 2 and mesh.shape["dp"] == 16 else 0
    return jax.shard_map(
        functools.partial(shards, planes),
        mesh=mesh, in_specs=in_specs, out_specs=out_specs, check_vma=False,
    )
```

```python
import functools

import jax
import jax.numpy as jnp
from jax import lax
from jax.experimental import pallas as pl
from jax.experimental.pallas import tpu as pltpu
from jax.sharding import PartitionSpec as P

HEAD_DIM = 64
BLOCK = 128
EPSILON = 1e-06
NEG_FILL = -1e30
F32 = jnp.float32
BF16 = jnp.bfloat16
VMEM_LIMIT = 60 << 20


def dot(left, right, dims):
    return lax.dot_general(left, right, ((dims[:1], dims[1:]), ((), ())), preferred_element_type=F32)


def dot_nn(left, right):
    return dot(left, right, (1, 0))


def dot_nt(left, right):
    return dot(left, right, (1, 1))


def dot_tn(left, right):
    return dot(left, right, (0, 0))


def windows(length):
    return [
        (max(0, start - BLOCK), min(length, start + 2 * BLOCK))
        for start in range(0, length, BLOCK)
    ]


def mask_offsets(length):
    offsets, total = [], 0
    for low, high in windows(length):
        offsets.append(total)
        total += high - low
    return offsets, total


def fill_masks(mask_ref, seq, segment_row):
    length = segment_row.shape[1]
    columns = jnp.transpose(jnp.broadcast_to(segment_row, (BLOCK, length)))
    offsets, _ = mask_offsets(length)
    for block, (low, high) in enumerate(windows(length)):
        rows = jnp.broadcast_to(
            segment_row[:, block * BLOCK : (block + 1) * BLOCK], (high - low, BLOCK)
        )
        mask_ref[seq, pl.ds(offsets[block], high - low), :] = jnp.where(
            columns[low:high] == rows, 0.0, NEG_FILL
        )


def stacked(pair):
    lane = lax.broadcasted_iota(jnp.int32, pair.shape, 1)
    zero = jnp.zeros_like(pair)
    return jnp.concatenate(
        [jnp.where(lane < HEAD_DIM, pair, zero), jnp.where(lane < HEAD_DIM, zero, pair)], axis=0
    )


def unstacked_t(joined):
    row = lax.broadcasted_iota(jnp.int32, (2 * HEAD_DIM, BLOCK), 0)
    return jnp.transpose(jnp.where(row < HEAD_DIM, joined[:, :BLOCK], joined[:, BLOCK:]))


def twice(mask):
    return jnp.concatenate([mask, mask], axis=1)


def normalize(summed):
    center = summed - jnp.mean(summed, axis=-1, keepdims=True)
    inverse = lax.rsqrt(jnp.mean(center * center, axis=-1, keepdims=True) + EPSILON)
    return (center * inverse, inverse)


def normalize_back(grad_normed, normed, inverse):
    mean_grad = jnp.mean(grad_normed, axis=-1, keepdims=True)
    mean_cross = jnp.mean(grad_normed * normed, axis=-1, keepdims=True)
    return inverse * (grad_normed - mean_grad - normed * mean_cross)


def column_sum(rows):
    return jnp.sum(rows, axis=0, keepdims=True)


def gelu_parts(pre):
    size = jnp.abs(pre)
    t = 1.0 / (1.0 + 0.3275911 * 0.7071067811865476 * size)
    bell = jnp.exp(-0.5 * pre * pre)
    series = t * (
        0.127414796
        + t * (-0.142248368 + t * (0.7107068705 + t * (-0.7265760135 + t * 0.5307027145)))
    )
    tail = series * bell
    cdf = jnp.where(pre >= 0.0, 1.0 - tail, tail)
    return (pre * cdf, cdf + pre * (bell * 0.3989422804014327))


MESH = pl.DeviceIdType.MESH


def when(condition, body):
    if condition is True:
        body()
    else:
        pl.when(condition)(body)


class Place:
    def __init__(self, planes):
        along = lax.axis_index("dp")
        self.planes = planes
        self.y = lax.axis_index("inner")
        self.c = lax.rem(along, 2)
        self.x = lax.rem(lax.div(along, 2), 2)
        self.z = lax.div(along, 4)

    def device(self, z=None, x=None, c=None, y=None):
        z = self.z if z is None else z
        x = self.x if x is None else x
        c = self.c if c is None else c
        return ((z * 2 + x) * 2 + c, self.y if y is None else y)

    @property
    def above(self):
        return self.device(z=jnp.minimum(self.z + 1, self.planes - 1))

    @property
    def below(self):
        return self.device(z=jnp.maximum(self.z - 1, 0))

    @property
    def across(self):
        return self.device(x=1 - self.x)

    @property
    def beside(self):
        return self.device(y=1 - self.y)

    @property
    def partner(self):
        return self.device(c=1 - self.c)

    @property
    def has_above(self):
        return self.z < self.planes - 1

    @property
    def has_below(self):
        return self.z > 0

    def enter(self):
        barrier = pltpu.get_barrier_semaphore()

        def greet(device):
            pl.semaphore_signal(barrier, inc=1, device_id=device, device_id_type=MESH)

        for device in (self.across, self.beside, self.partner):
            greet(device)
        when(self.has_above, lambda: greet(self.above))
        when(self.has_below, lambda: greet(self.below))
        pl.semaphore_wait(
            barrier, 3 + self.has_above.astype(jnp.int32) + self.has_below.astype(jnp.int32)
        )


def half_of(ref, half):
    if half == 2:
        return ref
    width = ref.shape[-1] // 2
    lead = (slice(None),) * (len(ref.shape) - 1)
    return ref.at[lead + (slice(half * width, (half + 1) * width),)]


SENDS = 64


class Gather:
    def __init__(self, place, index, shard, full, send, recv, local):
        self.place, self.index, self.shard, self.full = place, index, shard, full
        self.send, self.recv, self.local = send, recv, local
        self.rows = shard.shape[0]
        self.halves = (0, 1) if full.shape[-1] % (2 * BLOCK) == 0 else (2, None)
        self.slot = 0
        self.draining = False
        self.log = []

    def entry(self, z, x, c, y):
        device = ((z * 2 + x) * 2 + c) * 2 + y
        return self.full.at[pl.ds(pl.multiple_of(device * self.rows, 8), self.rows)]

    def run(self, name, *args):
        self.log.append((name, args))
        getattr(self, name)(*args)

    def push(self, condition, item, half, device, source=None):
        slot = self.slot
        self.slot += 1
        assert slot < SENDS

        def make():
            return pltpu.make_async_remote_copy(
                src_ref=half_of(self.entry(*item) if source is None else source, half),
                dst_ref=half_of(self.entry(*item), half),
                send_sem=self.send.at[self.index, slot],
                recv_sem=self.recv.at[(self.index,) + item + (min(half, 1),)],
                device_id=device,
                device_id_type=MESH,
            )

        if self.draining:
            when(condition, lambda: make().wait_send())
        else:
            when(condition, lambda: make().start())

    def await_item(self, item, half):
        if self.draining:
            return
        ref = half_of(self.entry(*item), half)
        pltpu.make_async_remote_copy(
            src_ref=ref, dst_ref=ref, send_sem=self.send.at[self.index, 0],
            recv_sem=self.recv.at[(self.index,) + item + (min(half, 1),)],
            device_id=self.place.partner, device_id_type=MESH,
        ).wait_recv()

    def own_copy(self):
        p = self.place
        return pltpu.make_async_copy(
            self.shard, self.entry(p.z, p.x, p.c, p.y), self.local.at[self.index]
        )

    def first_z(self):
        p = self.place
        item = (p.z, p.x, p.c, p.y)
        self.push(p.has_above, item, 2, p.above, self.shard)
        self.push(p.has_below, item, 2, p.below, self.shard)
        if not self.draining:
            self.own_copy().start()

    def first_xy(self):
        p = self.place
        item = (p.z, p.x, p.c, p.y)
        for device in (p.across, p.beside, p.partner):
            self.push(True, item, 2, device, self.shard)

    def planes_at(self, distance):
        p = self.place
        if distance == 0:
            return [(True, p.z, None, None)]
        return [
            (p.z >= distance, p.z - distance, p.has_above, p.above),
            (p.z + distance < p.planes, p.z + distance, p.has_below, p.below),
        ]

    def along_z(self, distance):
        p = self.place
        for there, z, more, onward in self.planes_at(distance):
            item = (jnp.clip(z, 0, p.planes - 1), p.x, p.c, p.y)
            if not self.draining:
                when(there, lambda: self.await_item(item, 2))
            self.push(jnp.logical_and(there, more), item, 2, onward)
            for device in (p.across, p.beside, p.partner):
                self.push(there, item, 2, device)

    def across_xy(self, distance):
        p = self.place
        for there, z, _, _ in self.planes_at(distance):
            z = jnp.clip(z, 0, p.planes - 1)
            for half, item, onward in (
                (self.halves[0], (z, 1 - p.x, p.c, p.y), p.beside),
                (self.halves[1], (z, p.x, p.c, 1 - p.y), p.across),
            ):
                if not self.draining:
                    when(there, lambda: self.await_item(item, 2))
                if half is not None:
                    self.push(there, item, half, onward)
                self.push(there, item, 2, p.partner)

    def diagonal(self, distance):
        p = self.place
        for there, z, _, _ in self.planes_at(distance):
            item = (jnp.clip(z, 0, p.planes - 1), 1 - p.x, p.c, 1 - p.y)

            def arrive():
                for half in self.halves:
                    if half is not None:
                        self.await_item(item, half)

            if not self.draining:
                when(there, arrive)
            self.push(there, item, 2, p.partner)

    def finish(self):
        p = self.place
        for z in range(p.planes):
            for x in range(2):
                for y in range(2):
                    self.await_item((z, x, 1 - p.c, y), 2)
        self.own_copy().wait()
        self.draining, self.slot = True, 0
        for name, args in self.log:
            getattr(self, name)(*args)


class Scatter:
    def __init__(self, place, index, source, held, bufs, sems, store, via=None):
        self.place, self.index, self.source, self.via, self.store = place, index, source, via, store
        self.held = source.at[:, :, place.c] if held is None else held
        self.loads = held is not None
        self.from_partner, self.from_diag, self.from_side, self.from_z, self.spare = bufs
        self.send, self.recv, self.local = sems
        self.dtype = source.dtype

    def copy(self, slot, src, dst, device):
        return pltpu.make_async_remote_copy(
            src_ref=src, dst_ref=dst, send_sem=self.send.at[self.index, slot],
            recv_sem=self.recv.at[self.index, slot], device_id=device, device_id_type=MESH,
        )

    def own_copy(self):
        return pltpu.make_async_copy(
            self.source.at[:, :, self.place.c], self.held, self.local.at[self.index]
        )

    def partner_copy(self):
        p = self.place
        return self.copy(0, self.source.at[:, :, 1 - p.c], self.from_partner, p.partner)

    def diag_copies(self):
        p = self.place
        ref = self.held.at[:, 1 - p.x, 1 - p.y]
        if self.via is not None:
            return [self.copy(1, ref, self.from_diag.at[0], p.beside if self.via else p.across)]
        return [
            self.copy(1, half_of(ref, 0), self.from_diag.at[0], p.across),
            self.copy(2, half_of(ref, 1), self.from_diag.at[1], p.beside),
        ]

    def side_copies(self):
        p = self.place
        return [
            self.copy(3, self.held.at[:, 1 - p.x, p.y], self.from_side.at[0], p.across),
            self.copy(4, self.held.at[:, p.x, 1 - p.y], self.from_side.at[1], p.beside),
        ]

    def z_copy(self, up, z):
        p = self.place
        return self.copy(
            5 + up * p.planes + z, self.spare.at[z], self.from_z.at[up, z], p.above if up else p.below
        )

    def start(self):
        if self.loads:
            self.own_copy().start()
        self.partner_copy().start()

    def after_partner(self):
        p = self.place
        if self.loads:
            self.own_copy().wait()
        self.partner_copy().wait_recv()

        def add(x, y):
            def one(z, _):
                total = self.held[z, x, y].astype(F32) + self.from_partner[z, x, y].astype(F32)
                self.held[z, x, y] = total.astype(self.dtype)
                return 0

            lax.fori_loop(0, p.planes, one, 0)

        add(1 - p.x, 1 - p.y)
        for copy in self.diag_copies():
            copy.start()
        add(1 - p.x, p.y)
        add(p.x, 1 - p.y)
        add(p.x, p.y)

    def after_diag(self):
        p = self.place
        width = self.source.shape[-1]
        for copy in self.diag_copies():
            copy.wait_recv()
        if self.via is None:
            parts = ((0, p.x, 1 - p.y, 0, width // 2), (1, 1 - p.x, p.y, width // 2, width))
        elif self.via:
            parts = ((0, 1 - p.x, p.y, 0, width),)
        else:
            parts = ((0, p.x, 1 - p.y, 0, width),)

        def one(z, _):
            for index, x, y, low, high in parts:
                total = self.held[z, x, y, :, low:high].astype(F32) + self.from_diag[index, z].astype(F32)
                self.held[z, x, y, :, low:high] = total.astype(self.dtype)
            return 0

        lax.fori_loop(0, p.planes, one, 0)
        for copy in self.side_copies():
            copy.start()

    def after_side(self):
        p = self.place
        for copy in self.side_copies():
            copy.wait_recv()

        def one(z, _):
            total = self.held[z, p.x, p.y].astype(F32)
            total = total + self.from_side[0, z].astype(F32) + self.from_side[1, z].astype(F32)
            self.spare[z] = total.astype(self.dtype)
            return 0

        lax.fori_loop(0, p.planes, one, 0)
        for z in range(p.planes):
            when(jnp.logical_and(jnp.logical_not(p.has_below), z > p.z), lambda: self.z_copy(1, z).start())
            when(jnp.logical_and(jnp.logical_not(p.has_above), z < p.z), lambda: self.z_copy(0, z).start())

    def along_z(self):
        p = self.place
        inside = jnp.logical_and(p.has_below, p.has_above)
        for z in range(p.planes):
            def onward(up, z=z):
                self.z_copy(up, z).wait_recv()
                total = self.spare[z].astype(F32) + self.from_z[up, z].astype(F32)
                self.spare[z] = total.astype(self.dtype)
                self.z_copy(up, z).start()

            when(jnp.logical_and(inside, z > p.z), lambda: onward(1))
            when(jnp.logical_and(inside, z < p.z), lambda: onward(0))

    def finish(self):
        p = self.place
        self.store(self.spare[p.z].astype(F32), False)
        for up, there in ((1, p.has_below), (0, p.has_above)):
            def arrive(up=up):
                self.z_copy(up, p.z).wait_recv()
                self.store(self.from_z[up, p.z].astype(F32), True)

            when(there, arrive)
        self.partner_copy().wait_send()
        for copy in self.diag_copies() + self.side_copies():
            copy.wait_send()
        for z in range(p.planes):
            when(jnp.logical_and(z > p.z, p.has_above), lambda: self.z_copy(1, z).wait_send())
            when(jnp.logical_and(z < p.z, p.has_below), lambda: self.z_copy(0, z).wait_send())


STAGES = ("start", "after_partner", "after_diag", "after_side", "along_z", "finish")


def scatter_scratch(planes, rows, width, dtype, held, via):
    return ([pltpu.VMEM((planes, 2, 2, rows, width), dtype)] if held else []) + [
        pltpu.VMEM((planes, 2, 2, rows, width), dtype),
        pltpu.VMEM((2, planes, rows, width // 2) if via is None else (1, planes, rows, width), dtype),
        pltpu.VMEM((2, planes, rows, width), dtype),
        pltpu.VMEM((2, planes, rows, width), dtype),
        pltpu.VMEM((planes, rows, width), dtype),
    ]


def store_to(out, cols=None, rows=None):
    def store(value, more):
        index = (slice(None) if rows is None else rows, slice(None) if cols is None else cols)
        out[index] = out[index] + value if more else value

    return store


def spread_masks(devices, piece):
    size = devices * piece
    column = lax.broadcasted_iota(jnp.int32, (devices, size), 1)
    start = lax.broadcasted_iota(jnp.int32, (devices, size), 0) * piece
    owner = jnp.logical_and(column >= start, column < start + piece)
    column = lax.broadcasted_iota(jnp.int32, (BLOCK, size), 1)
    number = jnp.floor((column.astype(F32) + 0.5) * (1.0 / piece)).astype(jnp.int32)
    place = column - number * piece == lax.broadcasted_iota(jnp.int32, (BLOCK, size), 0)
    return owner, place.astype(F32)


def spread_vectors(gathered, pieces):
    masks = {piece: spread_masks(gathered.shape[0], piece) for piece in set(pieces)}
    rows = []
    for index, piece in enumerate(pieces):
        owner, place = masks[piece]
        wide = dot_nn(gathered[:, index, :], place.astype(BF16))
        rows.append(jnp.sum(jnp.where(owner, wide, 0.0), axis=0, keepdims=True))
    return rows


def collect_vector(row, piece, devices):
    owner, place = spread_masks(devices, piece)
    wide = jnp.where(owner, row, 0.0)
    high = wide.astype(BF16)
    low = (wide - high.astype(F32)).astype(BF16)
    place = place.astype(BF16)
    return dot_nt(high, place) + dot_nt(low, place)


OUT_TICKS = (
    (0, "along_z", 1), (0, "across_xy", 0), (0, "along_z", 2), (1, "across_xy", 1), (1, "diagonal", 0),
    (1, "along_z", 3), (2, "across_xy", 2), (2, "diagonal", 1), (3, "across_xy", 3), (3, "diagonal", 2),
    (4, "diagonal", 3),
)
FEED_TICKS = (
    (0, "first_xy"), (0, "along_z", 1), (2, "along_z", 2), (4, "across_xy", 0), (5, "along_z", 3),
    (8, "diagonal", 0), (9, "across_xy", 1), (13, "diagonal", 1), (14, "across_xy", 2),
    (18, "diagonal", 2), (18, "across_xy", 3), (22, "diagonal", 3),
)


def attention_kernel(planes, pieces, tokens_ref, segment_ref, *refs):
    shards, refs = refs[:5], refs[5:]
    if planes:
        fulls, refs = refs[:5], refs[5:]
    else:
        fulls = shards
    (
        qkv_ref, context_ref, lse_ref, normed_ref, inverse_ref, vectors_ref, bin_ref,
        wqkv_ref, wout_ref, small_ref, bias_ref, mask_ref, load_sem, *sems,
    ) = refs
    length, width = tokens_ref.shape
    count = pl.num_programs(0)
    step = pl.program_id(0)
    pairs = width // BLOCK
    offsets, _ = mask_offsets(length)
    gathers = []
    if planes:
        place = Place(planes)
        gathers = [Gather(place, i, shards[i], fulls[i], *sems) for i in range(5)]
    attn, out, feed = gathers[:2], gathers[2:3], gathers[3:]

    def load(index, ref):
        return pltpu.make_async_copy(fulls[index], ref, load_sem.at[index])

    @pl.when(step == 0)
    def _():
        if planes:
            place.enter()
            for gather in attn + out:
                gather.run("first_z")
                gather.run("first_xy")
            for gather in feed:
                gather.run("first_z")
        for seq in range(segment_ref.shape[0]):
            fill_masks(mask_ref, seq, segment_ref[seq])
        for distance in range(1, planes + 2 if planes else 0):
            for gather in attn:
                if distance < planes:
                    gather.run("along_z", distance)
                if distance - 1 < planes:
                    gather.run("across_xy", distance - 1)
                if distance >= 2:
                    gather.run("diagonal", distance - 2)
        for gather in attn:
            gather.finish()
        load(0, wqkv_ref).start()
        load(1, small_ref).start()
        load(1, small_ref).wait()
        small = small_ref[...].astype(F32).reshape(-1, 8, BLOCK)
        bqv, bout, gain_one, shift_one, bin_, bfin, gain_two, shift_two = spread_vectors(small, pieces)
        bias_ref[:, :width] = bqv[:, :width]
        bias_ref[:, width : 2 * width] = jnp.zeros_like(bout)
        bias_ref[:, 2 * width : 3 * width] = bqv[:, width:]
        bias_ref[:, 3 * width :] = bout
        bin_ref[...] = bin_
        for row, vector in enumerate((gain_one, shift_one, bfin, gain_two, shift_two)):
            vectors_ref[row : row + 1] = vector
        vectors_ref[5:8] = jnp.zeros((3, width), F32)
        load(0, wqkv_ref).wait()

    due = {}
    for group, ticks in ((out, OUT_TICKS), (feed, FEED_TICKS)):
        for number, name, *args in ticks:
            for gather in group:
                due.setdefault(number, []).append(functools.partial(gather.run, name, *args))

    for part in range(3):
        cols = slice(part * width, (part + 1) * width)
        joined = dot_nn(tokens_ref[...], wqkv_ref[:, cols]) + bias_ref[:, cols]
        if part == 0:
            joined = joined * HEAD_DIM ** (-0.5)
        qkv_ref[:, cols] = joined.astype(BF16)

    def one_pair(pair, _):
        for number, acts in due.items():
            @pl.when(step * pairs + pair == number)
            def _():
                for act in acts:
                    act()

        def cols(part):
            return pl.ds(pl.multiple_of(part * width + pair * BLOCK, BLOCK), BLOCK)

        for block, (low, high) in enumerate(windows(length)):
            here = slice(block * BLOCK, (block + 1) * BLOCK)
            query = stacked(qkv_ref[here, cols(0)])
            scores = dot_nt(qkv_ref[low:high, cols(1)], query)
            scores = scores + twice(mask_ref[step, pl.ds(offsets[block], high - low), :])
            maxima = jnp.max(scores, axis=0, keepdims=True)
            exponent = jnp.exp(scores - maxima)
            totals = jnp.sum(exponent, axis=0, keepdims=True)
            context = dot_tn(qkv_ref[low:high, cols(2)], exponent.astype(BF16)) * (1.0 / totals)
            context_ref[here, cols(0)] = unstacked_t(context).astype(BF16)
            lse_ref[0, pl.ds(pair * (length // BLOCK) + block, 1), :] = maxima + jnp.log(totals)
        return 0

    lax.fori_loop(0, pairs, one_pair, 0)

    @pl.when(step == 0)
    def _():
        for gather in out:
            gather.finish()
        load(2, wout_ref).start()
        load(2, wout_ref).wait()

    branch = dot_nn(context_ref[...], wout_ref[...]) + bias_ref[:, 3 * width :]
    normed, inverse = normalize(tokens_ref[...].astype(F32) + branch)
    normed_ref[...] = normed
    inverse_ref[...] = jnp.broadcast_to(inverse, inverse_ref.shape)

    @pl.when(step == count - 1)
    def _():
        for gather in feed:
            gather.finish()


def whole(shape):
    return pl.BlockSpec(shape, lambda *_: (0,) * len(shape), pipeline_mode=pl.Buffered(1))


def attention_forward(planes, tokens, segments, weights, pieces):
    count, length = segments.shape[0], segments.shape[2]
    width = tokens.shape[1]
    rows = pl.BlockSpec((length, width), lambda i: (i, 0))
    any_ = pl.BlockSpec(memory_space=pl.ANY)
    lse_rows = (width // BLOCK) * (length // BLOCK)
    hidden = weights[3].shape[-1]
    devices = planes * 8 if planes else weights[1].shape[0] // 8
    gathered = [(devices * w.shape[0], w.shape[1]) for w in weights] if planes else []
    sems = []
    if planes:
        sems = [
            pltpu.SemaphoreType.DMA((5, SENDS)),
            pltpu.SemaphoreType.DMA((5, planes, 2, 2, 2, 2)),
            pltpu.SemaphoreType.DMA((5,)),
        ]
    out = pl.pallas_call(
        functools.partial(attention_kernel, planes, pieces),
        grid=(count,),
        in_specs=[rows, whole(segments.shape)] + [whole(w.shape) if planes else any_ for w in weights],
        out_specs=[any_] * len(gathered) + [
            pl.BlockSpec((length, 3 * width), lambda i: (i, 0)),
            rows,
            pl.BlockSpec((1, lse_rows, 2 * BLOCK), lambda i: (i, 0, 0)),
            rows,
            pl.BlockSpec((length, BLOCK), lambda i: (i, 0)),
            whole((8, width)),
            whole((1, hidden)),
        ],
        out_shape=[jax.ShapeDtypeStruct(s, w.dtype) for s, w in zip(gathered, weights)] + [
            jax.ShapeDtypeStruct((count * length, 3 * width), BF16),
            jax.ShapeDtypeStruct((count * length, width), BF16),
            jax.ShapeDtypeStruct((count, lse_rows, 2 * BLOCK), F32),
            jax.ShapeDtypeStruct((count * length, width), F32),
            jax.ShapeDtypeStruct((count * length, BLOCK), F32),
            jax.ShapeDtypeStruct((8, width), F32),
            jax.ShapeDtypeStruct((1, hidden), F32),
        ],
        scratch_shapes=[
            pltpu.VMEM((width, 3 * width), BF16),
            pltpu.VMEM((width, width), BF16),
            pltpu.VMEM((devices * 8, BLOCK), BF16),
            pltpu.VMEM((1, 4 * width), F32),
            pltpu.VMEM((count, mask_offsets(length)[1], BLOCK), F32),
            pltpu.SemaphoreType.DMA((3,)),
        ] + sems,
        compiler_params=pltpu.CompilerParams(
            vmem_limit_bytes=VMEM_LIMIT,
            **(dict(collective_id=0, has_side_effects=True) if planes else {}),
        ),
        name="attention_forward",
    )(tokens, segments, *weights)
    fulls = out[: len(gathered)] if planes else weights
    return fulls, out[len(gathered) :]


def feed_kernel(
    normed_ref, cot_ref, win_ref, wfin_ref, vec_ref, bin_ref,
    out_ref, act_ref, slope_ref, gsum_ref, gffn_ref, low_ref, gvec_ref,
    hidden_ref,
):
    hidden = normed_ref[...] * vec_ref[0:1] + vec_ref[1:2]
    hidden_ref[...] = hidden
    low_ref[...] = hidden.astype(BF16)
    width = win_ref.shape[0]

    def one_chunk(chunk, _):
        cols = pl.ds(pl.multiple_of(chunk * width, width), width)
        pre = dot_nn(low_ref[...], win_ref[:, cols]) + bin_ref[:, cols]
        active, slope = gelu_parts(pre)
        act_ref[:, cols] = active.astype(BF16)
        slope_ref[:, cols] = slope.astype(BF16)
        return 0

    lax.fori_loop(0, win_ref.shape[1] // width, one_chunk, 0)
    branch = dot_nn(act_ref[...], wfin_ref[...]) + vec_ref[2:3]
    normed, inverse = normalize(hidden_ref[...] + branch)
    gain = vec_ref[3:4]
    out_ref[...] = (normed * gain + vec_ref[4:5]).astype(BF16)
    cot = cot_ref[...].astype(F32)
    gsum = normalize_back(cot * gain, normed, inverse)
    gsum_ref[...] = gsum
    gffn = gsum.astype(BF16)
    gffn_ref[...] = gffn

    @pl.when(pl.program_id(0) == 0)
    def _():
        gvec_ref[...] = jnp.zeros_like(gvec_ref)

    gvec_ref[0:1] += column_sum(cot * normed)
    gvec_ref[1:2] += column_sum(cot)
    gvec_ref[2:3] += column_sum(gffn.astype(F32))


def feed_forward(normed, cotangent, win, wfin, vectors, bin_, tile):
    tokens, width = normed.shape
    hidden = win.shape[1]
    rows = pl.BlockSpec((tile, width), lambda i: (i, 0))
    wide = pl.BlockSpec((tile, hidden), lambda i: (i, 0))
    return pl.pallas_call(
        feed_kernel,
        grid=(tokens // tile,),
        in_specs=[rows, rows, whole(win.shape), whole(wfin.shape), whole(vectors.shape), whole(bin_.shape)],
        out_specs=[rows, wide, wide, rows, rows, rows, pl.BlockSpec((8, width), lambda i: (0, 0))],
        out_shape=[
            jax.ShapeDtypeStruct((tokens, width), BF16),
            jax.ShapeDtypeStruct((tokens, hidden), BF16),
            jax.ShapeDtypeStruct((tokens, hidden), BF16),
            jax.ShapeDtypeStruct((tokens, width), F32),
            jax.ShapeDtypeStruct((tokens, width), BF16),
            jax.ShapeDtypeStruct((tokens, width), BF16),
            jax.ShapeDtypeStruct((8, width), F32),
        ],
        scratch_shapes=[pltpu.VMEM((tile, width), F32)],
        compiler_params=pltpu.CompilerParams(vmem_limit_bytes=VMEM_LIMIT),
        name="feed_forward",
    )(normed, cotangent, win, wfin, vectors, bin_)


def feed_back_kernel(
    gffn_ref, low_ref, gsum_hbm, act_ref, slope_ref, win_ref, wfin_ref,
    dwin_ref, dwfin_ref, gbin_ref, ghid_hbm,
    low_t_ref, acc_ref, gpre_ref, sem,
):
    step = pl.program_id(0)
    tokens = gffn_ref.shape[0]
    tile = 512

    @pl.when(step == 0)
    def _():
        copy = pltpu.make_async_copy(gsum_hbm, acc_ref, sem)
        copy.start()
        low_t_ref[...] = jnp.transpose(low_ref[...])
        copy.wait()

    gbin_ref[...] = jnp.zeros_like(gbin_ref)
    for start in range(0, tokens, tile):
        here = slice(start, start + tile)
        gpre = (dot_nt(gffn_ref[here], wfin_ref[...]) * slope_ref[here].astype(F32)).astype(BF16)
        gpre_ref[here] = gpre
        gbin_ref[0:1] += column_sum(gpre.astype(F32))
        acc_ref[here] += dot_nt(gpre, win_ref[...])
    dwin_ref[...] = dot_nn(low_t_ref[...], gpre_ref[...]).astype(BF16)
    dwfin_ref[...] = dot_tn(act_ref[...], gffn_ref[...]).astype(BF16)

    @pl.when(step == pl.num_programs(0) - 1)
    def _():
        pltpu.sync_copy(acc_ref, ghid_hbm)


def feed_backward(gffn, low, gsum, act, slope, win, wfin, chunk):
    tokens, width = low.shape
    hidden = win.shape[1]
    any_ = pl.BlockSpec(memory_space=pl.ANY)
    return pl.pallas_call(
        feed_back_kernel,
        grid=(hidden // chunk,),
        in_specs=[
            whole(gffn.shape), whole(low.shape), any_,
            pl.BlockSpec((tokens, chunk), lambda i: (0, i)),
            pl.BlockSpec((tokens, chunk), lambda i: (0, i)),
            pl.BlockSpec((width, chunk), lambda i: (0, i)),
            pl.BlockSpec((chunk, width), lambda i: (i, 0)),
        ],
        out_specs=[
            pl.BlockSpec((width, chunk), lambda i: (0, i)),
            pl.BlockSpec((chunk, width), lambda i: (i, 0)),
            pl.BlockSpec((8, chunk), lambda i: (0, i)),
            any_,
        ],
        out_shape=[
            jax.ShapeDtypeStruct((width, hidden), BF16),
            jax.ShapeDtypeStruct((hidden, width), BF16),
            jax.ShapeDtypeStruct((8, hidden), F32),
            jax.ShapeDtypeStruct((tokens, width), F32),
        ],
        scratch_shapes=[
            pltpu.VMEM((width, tokens), BF16),
            pltpu.VMEM((tokens, width), F32),
            pltpu.VMEM((tokens, chunk), BF16),
            pltpu.SemaphoreType.DMA,
        ],
        compiler_params=pltpu.CompilerParams(vmem_limit_bytes=VMEM_LIMIT),
        name="feed_backward",
    )(gffn, low, gsum, act, slope, win, wfin)


def project_back_kernel(
    ghid_ref, normed_ref, inverse_ref, context_ref, wout_ref, gain_ref,
    gsum_ref, gcon_ref, dwout_ref, gvec_ref, acc_ref,
):
    step = pl.program_id(0)

    @pl.when(step == 0)
    def _():
        gvec_ref[...] = jnp.zeros_like(gvec_ref)
        acc_ref[...] = jnp.zeros_like(acc_ref)

    ghid = ghid_ref[...]
    normed = normed_ref[...]
    gvec_ref[0:1] += column_sum(ghid * normed)
    gvec_ref[1:2] += column_sum(ghid)
    gsum = normalize_back(ghid * gain_ref[0:1], normed, inverse_ref[:, 0:1])
    gsum_ref[...] = gsum
    gattn = gsum.astype(BF16)
    gvec_ref[2:3] += column_sum(gattn.astype(F32))
    gcon_ref[...] = dot_nt(gattn, wout_ref[...]).astype(BF16)
    acc_ref[...] += dot_tn(context_ref[...], gattn)

    @pl.when(step == pl.num_programs(0) - 1)
    def _():
        dwout_ref[...] = acc_ref[...].astype(BF16)


def project_backward(ghid, normed, inverse, context, wout, gain, tile):
    tokens, width = ghid.shape
    rows = pl.BlockSpec((tile, width), lambda i: (i, 0))
    return pl.pallas_call(
        project_back_kernel,
        grid=(tokens // tile,),
        in_specs=[
            rows, rows, pl.BlockSpec((tile, BLOCK), lambda i: (i, 0)), rows,
            whole(wout.shape), whole(gain.shape),
        ],
        out_specs=[rows, rows, whole((width, width)), pl.BlockSpec((8, width), lambda i: (0, 0))],
        out_shape=[
            jax.ShapeDtypeStruct((tokens, width), F32),
            jax.ShapeDtypeStruct((tokens, width), BF16),
            jax.ShapeDtypeStruct((width, width), BF16),
            jax.ShapeDtypeStruct((8, width), F32),
        ],
        scratch_shapes=[pltpu.VMEM((width, width), F32)],
        compiler_params=pltpu.CompilerParams(vmem_limit_bytes=VMEM_LIMIT),
        name="project_backward",
    )(ghid, normed, inverse, context, wout, gain)


FEED_STEPS = ((0, 2, 4, 7, 8, 11), (0, 5, 8, 11, 12, 15), (1, 9, 12, 15, 16, 19), (5, 13, 16, 19, 20, 23))
OUT_STEPS = (0, 1, 3, 6, 7, 10)
PAIR_STEPS = (0, 1, 2, 3, 5, 7)


def attention_back_kernel(
    planes, pieces, devices,
    q_ref, k_ref, v_ref, gcon_ref, lse_ref, segment_ref, tokens_ref, wq_ref, wk_ref, wv_ref, gsum_hbm,
    gtwo_ref, gbin_ref, gone_ref, *refs,
):
    sources, refs = refs[: 3 if planes else 0], refs[3 if planes else 0 :]
    gtok_hbm, refs = refs[0], refs[1:]
    if planes:
        outs, refs = refs[:5], refs[5:]
    else:
        dw_ref, small_ref, refs = refs[0], refs[1], refs[2:]
    tokens_t_ref, acc_ref, mask_ref, grad_ref, dk_ref, dv_ref, gbqv_ref, sem, *refs = refs
    pair = pl.program_id(0)
    last = pl.num_programs(0) - 1
    count, length = segment_ref.shape[0], segment_ref.shape[2]
    total, width = tokens_ref.shape
    pairs = width // BLOCK
    blocks = length // BLOCK
    offsets, _ = mask_offsets(length)
    tile = 512
    due, late = {}, []

    if planes:
        place = Place(planes)
        sems, (pair_dw_ref, small_ref), refs = refs[:3], refs[3:5], refs[5:]
        scatters = []

        def scatter(source, load, store, steps, via=None):
            nonlocal refs
            size = 6 if load else 5
            bufs, refs = refs[:size], refs[size:]
            held, bufs = (bufs[0], bufs[1:]) if load else (None, bufs)
            one = Scatter(place, len(scatters), source, held, bufs, sems, store, via)
            scatters.append(one)
            for stage, number in zip(STAGES, steps):
                if number < count * pairs:
                    due.setdefault(number, []).append(getattr(one, stage))
                else:
                    late.append((number, len(scatters), getattr(one, stage)))

        dwin, dwfin, dwout = sources
        half, wide = dwfin.shape[4] // 2, dwin.shape[5] // 2
        lead = (slice(None),) * 4
        for i in range(2):
            rows = slice(i * half, (i + 1) * half)
            scatter(dwfin.at[lead + (rows,)], True, store_to(outs[3], rows=rows), FEED_STEPS[i])
        for i in range(2):
            cols = slice(i * wide, (i + 1) * wide)
            scatter(dwin.at[lead + (slice(None), cols)], True, store_to(outs[2], cols=cols), FEED_STEPS[2 + i])
        scatter(dwout, True, store_to(outs[1]), OUT_STEPS)
        for i in range(pairs):
            def store(value, more, i=i):
                for part in range(3):
                    cols = slice(part * BLOCK, (part + 1) * BLOCK)
                    here = slice(part * width + i * BLOCK, part * width + (i + 1) * BLOCK)
                    store_to(outs[0], cols=here)(value[:, cols], more)

            scatter(
                pair_dw_ref.at[i], False, store, [count * (i + 1) + n for n in PAIR_STEPS], via=i % 2
            )
        scatter(
            small_ref.reshape(planes, 2, 2, 2, 8, BLOCK), False, store_to(outs[4]),
            [count * pairs + n for n in PAIR_STEPS], via=0,
        )

    @pl.when(pair == 0)
    def _():
        copy = pltpu.make_async_copy(gsum_hbm, acc_ref, sem)
        copy.start()
        if planes:
            place.enter()
        tokens_t_ref[...] = jnp.transpose(tokens_ref[...])
        for seq in range(count):
            fill_masks(mask_ref, seq, segment_ref[seq])
        for index, row in (
            (1, gone_ref[2:3]), (2, gone_ref[0:1]), (3, gone_ref[1:2]), (4, gbin_ref[0:1]),
            (5, gtwo_ref[2:3]), (6, gtwo_ref[0:1]), (7, gtwo_ref[1:2]),
        ):
            small_ref[:, index, :] = collect_vector(row, pieces[index], devices)
        copy.wait()

    def one_seq(seq, _):
        for number, acts in due.items():
            @pl.when(pair * count + seq == number)
            def _():
                for act in acts:
                    act()

        base = pl.multiple_of(seq * length, length)
        dk_ref[...] = jnp.zeros_like(dk_ref)
        dv_ref[...] = jnp.zeros_like(dv_ref)
        for block, (low, high) in enumerate(windows(length)):
            here = pl.ds(base + block * BLOCK, BLOCK)
            reach = pl.ds(base + low, high - low)
            query = stacked(q_ref[here])
            grad = stacked(gcon_ref[here])
            keys = k_ref[reach]
            scores = dot_nt(keys, query) + twice(mask_ref[seq, pl.ds(offsets[block], high - low), :])
            probs = jnp.exp(scores - lse_ref[seq, pl.ds(pair * blocks + block, 1), :])
            gprobs = dot_nt(v_ref[reach], grad)
            dots = jnp.sum(probs * gprobs, axis=0, keepdims=True)
            gscores = (probs * (gprobs - dots)).astype(BF16)
            dv_ref[low:high] += dot_nn(probs.astype(BF16), grad)
            dk_ref[low:high] += dot_nn(gscores, query)
            gquery = unstacked_t(dot_tn(keys, gscores)) * HEAD_DIM ** (-0.5)
            grad_ref[here, 0:BLOCK] = gquery.astype(BF16)
        rows = pl.ds(base, length)
        grad_ref[rows, BLOCK : 2 * BLOCK] = dk_ref[...].astype(BF16)
        grad_ref[rows, 2 * BLOCK :] = dv_ref[...].astype(BF16)
        return 0

    lax.fori_loop(0, count, one_seq, 0)
    cols = pl.multiple_of(pair * BLOCK, BLOCK)
    gbqv_ref[:, pl.ds(cols, BLOCK)] = column_sum(grad_ref[:, :BLOCK].astype(F32))
    gbqv_ref[:, pl.ds(width + cols, BLOCK)] = column_sum(grad_ref[:, 2 * BLOCK :].astype(F32))
    dw = dot_nn(tokens_t_ref[...], grad_ref[...])
    if planes:
        for part in range(3):
            here = slice(part * BLOCK, (part + 1) * BLOCK)
            pair_dw_ref[pair, ..., here] = dw[:, here].reshape(planes, 2, 2, 2, -1, BLOCK).astype(BF16)
    else:
        dw_ref[...] = dw.astype(BF16)
    weights = jnp.concatenate([wq_ref[...], wk_ref[...], wv_ref[...]], axis=1)
    for start in range(0, total, tile):
        here = slice(start, start + tile)
        acc_ref[here] += dot_nt(grad_ref[here], weights)

    @pl.when(pair == last)
    def _():
        copy = pltpu.make_async_copy(acc_ref, gtok_hbm, sem)
        copy.start()
        small_ref[:, 0, :] = collect_vector(gbqv_ref[...], pieces[0], devices)
        for _, _, act in sorted(late, key=lambda entry: entry[:2]):
            act()
        copy.wait()


def attention_backward(planes, pieces, devices, qkv, gcon, lse, segments, tokens, wqkv, gsum, vectors, grads):
    count, length = segments.shape[0], segments.shape[2]
    total, width = tokens.shape
    pairs = width // BLOCK
    any_ = pl.BlockSpec(memory_space=pl.ANY)

    def part(rows, index):
        return pl.BlockSpec((rows, BLOCK), lambda i: (0, index * pairs + i))

    scratch = [
        pltpu.VMEM((width, total), BF16),
        pltpu.VMEM((total, width), F32),
        pltpu.VMEM((count, mask_offsets(length)[1], BLOCK), F32),
        pltpu.VMEM((total, 3 * BLOCK), BF16),
        pltpu.VMEM((length, BLOCK), F32),
        pltpu.VMEM((length, BLOCK), F32),
        pltpu.VMEM((1, 2 * width), F32),
        pltpu.SemaphoreType.DMA,
    ]
    small = (devices, 8, BLOCK)
    if planes:
        grads = [g.reshape((planes, 2, 2, 2, -1) + g.shape[1:]) for g in grads]
        rows = width // devices
        shards = [(rows, 3 * width)] + [grads[i].shape[4:] for i in (2, 0, 1)] + [(8, BLOCK)]
        outs = [whole(shape) for shape in shards]
        out_shape = [jax.ShapeDtypeStruct(shape, F32) for shape in shards]
        number = 6 + pairs
        scratch += [
            pltpu.SemaphoreType.DMA((number, 5 + 2 * planes)),
            pltpu.SemaphoreType.DMA((number, 5 + 2 * planes)),
            pltpu.SemaphoreType.DMA((number,)),
            pltpu.VMEM((pairs, planes, 2, 2, 2, rows, 3 * BLOCK), BF16),
            pltpu.VMEM(small, F32),
        ]
        for shape in [(grads[1].shape[4] // 2, width)] * 2 + [(rows, grads[0].shape[5] // 2)] * 2 + [(rows, width)]:
            scratch += scatter_scratch(planes, *shape, BF16, True, None)
        for _ in range(pairs):
            scratch += scatter_scratch(planes, rows, 3 * BLOCK, BF16, False, 0)
        scratch += scatter_scratch(planes, 8, BLOCK, F32, False, 0)
    else:
        grads = []
        outs = [pl.BlockSpec((width, 3 * BLOCK), lambda i: (0, i)), whole(small)]
        out_shape = [jax.ShapeDtypeStruct((width, 3 * width), BF16), jax.ShapeDtypeStruct(small, F32)]
    return pl.pallas_call(
        functools.partial(attention_back_kernel, planes, pieces, devices),
        grid=(pairs,),
        in_specs=[
            part(total, 0), part(total, 1), part(total, 2), part(total, 0),
            whole(lse.shape), whole(segments.shape), whole(tokens.shape),
            part(width, 0), part(width, 1), part(width, 2), any_,
        ] + [whole(v.shape) for v in vectors] + [any_] * len(grads),
        out_specs=[any_] + outs,
        out_shape=[jax.ShapeDtypeStruct((total, width), F32)] + out_shape,
        scratch_shapes=scratch,
        compiler_params=pltpu.CompilerParams(
            vmem_limit_bytes=VMEM_LIMIT,
            **(dict(collective_id=1, has_side_effects=True) if planes else {}),
        ),
        name="attention_backward",
    )(qkv, qkv, qkv, gcon, lse, segments, tokens, wqkv, wqkv, wqkv, gsum, *vectors, *grads)


def shards(
    planes,
    tokens, weight_qkv, bias_qv, weight_out, bias_out, gain_one, shift_one,
    weight_in, bias_in, weight_fin, bias_fin, gain_two, shift_two, segments, cotangent,
):
    small = (bias_qv, bias_out, gain_one, shift_one, bias_in, bias_fin, gain_two, shift_two)
    pieces = tuple(v.shape[0] for v in small)
    joined = jnp.stack([jnp.pad(v, (0, BLOCK - v.shape[0])) for v in small])
    weights = [weight_qkv, joined, weight_out, weight_in, weight_fin]
    if not planes:
        weights = [lax.all_gather(w, AXES, axis=0, tiled=True) for w in weights]
    devices = planes * 8 if planes else weights[1].shape[0] // 8
    segments = segments.reshape(segments.shape[0], 1, segments.shape[1])
    fulls, rest = attention_forward(planes, tokens, segments, weights, pieces)
    wqkv, _, wout, win, wfin = fulls
    qkv, context, lse, normed, inverse, vectors, bin_ = rest
    tile = min(512, tokens.shape[0])
    output, act, slope, gsum_two, gffn, low, gvec_two = feed_forward(
        normed, cotangent, win, wfin, vectors, bin_, tile
    )
    dwin, dwfin, gbin, ghid = feed_backward(gffn, low, gsum_two, act, slope, win, wfin, 512)
    gsum_one, gcon, dwout, gvec_one = project_backward(ghid, normed, inverse, context, wout, vectors, tile)
    gtok, *sums = attention_backward(
        planes, pieces, devices, qkv, gcon, lse, segments, tokens, wqkv, gsum_one,
        (gvec_two, gbin, gvec_one), [dwin, dwfin, dwout],
    )
    if not planes:
        sums = [
            lax.psum_scatter(g.reshape((devices, -1) + g.shape[-1:]), AXES, scatter_dimension=0).astype(F32)
            for g in (sums[0], dwout, dwin, dwfin, sums[1])
        ]
        sums[0] = sums[0].reshape(sums[0].shape[0], -1, 3, BLOCK).swapaxes(1, 2).reshape(sums[0].shape)
    parts = [sums[4][i, :piece] for i, piece in enumerate(pieces)]
    return (
        output, gtok, sums[0], parts[0], sums[1], parts[1], parts[2], parts[3],
        sums[2], parts[4], sums[3], parts[5], parts[6], parts[7],
    )


AXES = ("dp", "inner")


def solution(mesh):
    row, vec = P(AXES, None), P(AXES)
    in_specs = (row, row, vec, row, vec, vec, vec, row, vec, row, vec, vec, vec, row, row)
    out_specs = (row, row, row, vec, row, vec, vec, vec, row, vec, row, vec, vec, vec)
    planes = mesh.shape["dp"] // 4 if mesh.shape["inner"] == 2 and mesh.shape["dp"] == 16 else 0
    return jax.shard_map(
        functools.partial(shards, planes),
        mesh=mesh, in_specs=in_specs, out_specs=out_specs, check_vma=False,
    )
```

```python
import functools

import jax
import jax.numpy as jnp
from jax import lax
from jax.experimental import pallas as pl
from jax.experimental.pallas import tpu as pltpu
from jax.sharding import PartitionSpec as P

HEAD_DIM = 64
BLOCK = 128
EPSILON = 1e-06
NEG_FILL = -1e30
F32 = jnp.float32
BF16 = jnp.bfloat16
VMEM_LIMIT = 60 << 20


def dot(left, right, dims):
    return lax.dot_general(left, right, ((dims[:1], dims[1:]), ((), ())), preferred_element_type=F32)


def dot_nn(left, right):
    return dot(left, right, (1, 0))


def dot_nt(left, right):
    return dot(left, right, (1, 1))


def dot_tn(left, right):
    return dot(left, right, (0, 0))


def windows(length):
    return [
        (max(0, start - BLOCK), min(length, start + 2 * BLOCK))
        for start in range(0, length, BLOCK)
    ]


def mask_offsets(length):
    offsets, total = [], 0
    for low, high in windows(length):
        offsets.append(total)
        total += high - low
    return offsets, total


def fill_masks(mask_ref, seq, segment_row):
    length = segment_row.shape[1]
    columns = jnp.transpose(jnp.broadcast_to(segment_row, (BLOCK, length)))
    offsets, _ = mask_offsets(length)
    for block, (low, high) in enumerate(windows(length)):
        rows = jnp.broadcast_to(
            segment_row[:, block * BLOCK : (block + 1) * BLOCK], (high - low, BLOCK)
        )
        mask_ref[seq, pl.ds(offsets[block], high - low), :] = jnp.where(
            columns[low:high] == rows, 0.0, NEG_FILL
        )


def stacked(pair):
    lane = lax.broadcasted_iota(jnp.int32, pair.shape, 1)
    zero = jnp.zeros_like(pair)
    return jnp.concatenate(
        [jnp.where(lane < HEAD_DIM, pair, zero), jnp.where(lane < HEAD_DIM, zero, pair)], axis=0
    )


def unstacked_t(joined):
    row = lax.broadcasted_iota(jnp.int32, (2 * HEAD_DIM, BLOCK), 0)
    return jnp.transpose(jnp.where(row < HEAD_DIM, joined[:, :BLOCK], joined[:, BLOCK:]))


def twice(mask):
    return jnp.concatenate([mask, mask], axis=1)


def normalize(summed):
    center = summed - jnp.mean(summed, axis=-1, keepdims=True)
    inverse = lax.rsqrt(jnp.mean(center * center, axis=-1, keepdims=True) + EPSILON)
    return (center * inverse, inverse)


def normalize_back(grad_normed, normed, inverse):
    mean_grad = jnp.mean(grad_normed, axis=-1, keepdims=True)
    mean_cross = jnp.mean(grad_normed * normed, axis=-1, keepdims=True)
    return inverse * (grad_normed - mean_grad - normed * mean_cross)


def column_sum(rows):
    return jnp.sum(rows, axis=0, keepdims=True)


def gelu_parts(pre):
    size = jnp.abs(pre)
    t = 1.0 / (1.0 + 0.3275911 * 0.7071067811865476 * size)
    bell = jnp.exp(-0.5 * pre * pre)
    series = t * (
        0.127414796
        + t * (-0.142248368 + t * (0.7107068705 + t * (-0.7265760135 + t * 0.5307027145)))
    )
    tail = series * bell
    cdf = jnp.where(pre >= 0.0, 1.0 - tail, tail)
    return (pre * cdf, cdf + pre * (bell * 0.3989422804014327))


MESH = pl.DeviceIdType.MESH


def when(condition, body):
    if condition is True:
        body()
    else:
        pl.when(condition)(body)


class Place:
    def __init__(self, planes):
        along = lax.axis_index("dp")
        self.planes = planes
        self.y = lax.axis_index("inner")
        self.c = lax.rem(along, 2)
        self.x = lax.rem(lax.div(along, 2), 2)
        self.z = lax.div(along, 4)

    def device(self, z=None, x=None, c=None, y=None):
        z = self.z if z is None else z
        x = self.x if x is None else x
        c = self.c if c is None else c
        return ((z * 2 + x) * 2 + c, self.y if y is None else y)

    @property
    def above(self):
        return self.device(z=jnp.minimum(self.z + 1, self.planes - 1))

    @property
    def below(self):
        return self.device(z=jnp.maximum(self.z - 1, 0))

    @property
    def across(self):
        return self.device(x=1 - self.x)

    @property
    def beside(self):
        return self.device(y=1 - self.y)

    @property
    def partner(self):
        return self.device(c=1 - self.c)

    @property
    def has_above(self):
        return self.z < self.planes - 1

    @property
    def has_below(self):
        return self.z > 0

    @property
    def diagonal(self):
        return self.device(x=1 - self.x, y=1 - self.y)

    def enter(self):
        barrier = pltpu.get_barrier_semaphore()
        planes = [self.device(z=lax.rem(self.z + i, self.planes)) for i in range(1, self.planes)]
        devices = [self.across, self.beside, self.diagonal, self.partner] + planes
        for device in devices:
            pl.semaphore_signal(barrier, inc=1, device_id=device, device_id_type=MESH)
        pl.semaphore_wait(barrier, len(devices))


def half_of(ref, half):
    if half == 2:
        return ref
    width = ref.shape[-1] // 2
    lead = (slice(None),) * (len(ref.shape) - 1)
    return ref.at[lead + (slice(half * width, (half + 1) * width),)]


SENDS = 64


class Gather:
    def __init__(self, place, index, shard, full, send, recv, local):
        self.place, self.index, self.shard, self.full = place, index, shard, full
        self.send, self.recv, self.local = send, recv, local
        self.rows = shard.shape[0]
        self.halves = (0, 1) if full.shape[-1] % (2 * BLOCK) == 0 else (2, None)
        self.slot = 0
        self.draining = False
        self.log = []

    def entry(self, z, x, c, y):
        device = ((z * 2 + x) * 2 + c) * 2 + y
        return self.full.at[pl.ds(pl.multiple_of(device * self.rows, 8), self.rows)]

    def run(self, name, *args):
        self.log.append((name, args))
        getattr(self, name)(*args)

    def push(self, condition, item, half, device, source=None):
        slot = self.slot
        self.slot += 1
        assert slot < SENDS

        def make():
            return pltpu.make_async_remote_copy(
                src_ref=half_of(self.entry(*item) if source is None else source, half),
                dst_ref=half_of(self.entry(*item), half),
                send_sem=self.send.at[self.index, slot],
                recv_sem=self.recv.at[(self.index,) + item + (min(half, 1),)],
                device_id=device,
                device_id_type=MESH,
            )

        if self.draining:
            when(condition, lambda: make().wait_send())
        else:
            when(condition, lambda: make().start())

    def await_item(self, item, half):
        if self.draining:
            return
        ref = half_of(self.entry(*item), half)
        pltpu.make_async_remote_copy(
            src_ref=ref, dst_ref=ref, send_sem=self.send.at[self.index, 0],
            recv_sem=self.recv.at[(self.index,) + item + (min(half, 1),)],
            device_id=self.place.partner, device_id_type=MESH,
        ).wait_recv()

    def own_copy(self):
        p = self.place
        return pltpu.make_async_copy(
            self.shard, self.entry(p.z, p.x, p.c, p.y), self.local.at[self.index]
        )

    def first_z(self):
        p = self.place
        item = (p.z, p.x, p.c, p.y)
        self.push(p.has_above, item, 2, p.above, self.shard)
        self.push(p.has_below, item, 2, p.below, self.shard)
        if not self.draining:
            self.own_copy().start()

    def first_xy(self):
        p = self.place
        item = (p.z, p.x, p.c, p.y)
        for device in (p.across, p.beside, p.partner):
            self.push(True, item, 2, device, self.shard)

    def planes_at(self, distance):
        p = self.place
        if distance == 0:
            return [(True, p.z, None, None)]
        return [
            (p.z >= distance, p.z - distance, p.has_above, p.above),
            (p.z + distance < p.planes, p.z + distance, p.has_below, p.below),
        ]

    def along_z(self, distance):
        p = self.place
        for there, z, more, onward in self.planes_at(distance):
            item = (jnp.clip(z, 0, p.planes - 1), p.x, p.c, p.y)
            if not self.draining:
                when(there, lambda: self.await_item(item, 2))
            self.push(jnp.logical_and(there, more), item, 2, onward)
            for device in (p.across, p.beside, p.partner):
                self.push(there, item, 2, device)

    def across_xy(self, distance):
        p = self.place
        for there, z, _, _ in self.planes_at(distance):
            z = jnp.clip(z, 0, p.planes - 1)
            for half, item, onward in (
                (self.halves[0], (z, 1 - p.x, p.c, p.y), p.beside),
                (self.halves[1], (z, p.x, p.c, 1 - p.y), p.across),
            ):
                if not self.draining:
                    when(there, lambda: self.await_item(item, 2))
                if half is not None:
                    self.push(there, item, half, onward)
                self.push(there, item, 2, p.partner)

    def diagonal(self, distance):
        p = self.place
        for there, z, _, _ in self.planes_at(distance):
            item = (jnp.clip(z, 0, p.planes - 1), 1 - p.x, p.c, 1 - p.y)

            def arrive():
                for half in self.halves:
                    if half is not None:
                        self.await_item(item, half)

            if not self.draining:
                when(there, arrive)
            self.push(there, item, 2, p.partner)

    def finish(self):
        p = self.place
        for z in range(p.planes):
            for x in range(2):
                for y in range(2):
                    self.await_item((z, x, 1 - p.c, y), 2)
        self.own_copy().wait()
        self.draining, self.slot = True, 0
        for name, args in self.log:
            getattr(self, name)(*args)


class Scatter:
    def __init__(self, place, index, source, held, bufs, sems, store):
        self.place, self.index, self.source, self.store = place, index, source, store
        self.held = source.at[:, :, place.c] if held is None else held
        self.loads = held is not None
        self.from_partner, self.from_square, self.spare, self.from_z = bufs
        self.send, self.recv, self.local = sems
        self.dtype = source.dtype

    def copy(self, slot, src, dst, device, arrival=None):
        return pltpu.make_async_remote_copy(
            src_ref=src, dst_ref=dst, send_sem=self.send.at[self.index, slot],
            recv_sem=self.recv.at[self.index, slot if arrival is None else arrival],
            device_id=device, device_id_type=MESH,
        )

    def own_copy(self):
        return pltpu.make_async_copy(
            self.source.at[:, :, self.place.c], self.held, self.local.at[self.index]
        )

    def partner_copy(self):
        p = self.place
        return self.copy(0, self.source.at[:, :, 1 - p.c], self.from_partner, p.partner)

    def square(self):
        p = self.place
        return ((1 - p.x, 1 - p.y, p.diagonal), (1 - p.x, p.y, p.across), (p.x, 1 - p.y, p.beside))

    def square_copies(self):
        return [
            self.copy(1 + i, self.held.at[:, x, y], self.from_square.at[i], device)
            for i, (x, y, device) in enumerate(self.square())
        ]

    def z_copy(self, z):
        p = self.place
        return self.copy(4 + z, self.spare.at[z], self.from_z.at[p.z], p.device(z=z), 4 + p.z)

    def z_arrival(self, z):
        p = self.place
        return self.copy(4 + z, self.spare.at[z], self.from_z.at[z], p.device(z=z), 4 + z)

    def start(self):
        if self.loads:
            self.own_copy().start()
        self.partner_copy().start()

    def after_partner(self):
        p = self.place
        if self.loads:
            self.own_copy().wait()
        self.partner_copy().wait_recv()

        def add(x, y):
            def one(z, _):
                total = self.held[z, x, y].astype(F32) + self.from_partner[z, x, y].astype(F32)
                self.held[z, x, y] = total.astype(self.dtype)
                return 0

            lax.fori_loop(0, p.planes, one, 0)

        for (x, y, _), copy in zip(self.square(), self.square_copies()):
            add(x, y)
            copy.start()
        add(p.x, p.y)

    def after_square(self):
        p = self.place
        for copy in self.square_copies():
            copy.wait_recv()

        def one(z, _):
            total = self.held[z, p.x, p.y].astype(F32)
            for i in range(3):
                total = total + self.from_square[i, z].astype(F32)
            self.spare[z] = total.astype(self.dtype)
            return 0

        lax.fori_loop(0, p.planes, one, 0)
        for z in range(p.planes):
            when(z != p.z, lambda: self.z_copy(z).start())

    def finish(self):
        p = self.place
        self.store(self.spare[p.z].astype(F32), False)
        for z in range(p.planes):
            def arrive(z=z):
                self.z_arrival(z).wait_recv()
                self.store(self.from_z[z].astype(F32), True)

            when(z != p.z, arrive)
        self.partner_copy().wait_send()
        for copy in self.square_copies():
            copy.wait_send()
        for z in range(p.planes):
            when(z != p.z, lambda: self.z_copy(z).wait_send())


STAGES = ("start", "after_partner", "after_square", "finish")


def scatter_scratch(planes, rows, width, dtype, held):
    return ([pltpu.VMEM((planes, 2, 2, rows, width), dtype)] if held else []) + [
        pltpu.VMEM((planes, 2, 2, rows, width), dtype),
        pltpu.VMEM((3, planes, rows, width), dtype),
        pltpu.VMEM((planes, rows, width), dtype),
        pltpu.VMEM((planes, rows, width), dtype),
    ]


def scatter_sems(planes, number):
    return [
        pltpu.SemaphoreType.DMA((number, 4 + planes)),
        pltpu.SemaphoreType.DMA((number, 4 + planes)),
        pltpu.SemaphoreType.DMA((number,)),
    ]


class Schedule:
    def __init__(self, place, sems, scratch, ticks):
        self.place, self.sems, self.scratch, self.ticks = place, sems, scratch, ticks
        self.count, self.due, self.late = 0, {}, []

    def add(self, source, load, store, steps):
        size = 5 if load else 4
        bufs, self.scratch = self.scratch[:size], self.scratch[size:]
        held, bufs = (bufs[0], bufs[1:]) if load else (None, bufs)
        one = Scatter(self.place, self.count, source, held, bufs, self.sems, store)
        self.count += 1
        for stage, number in zip(STAGES, steps):
            if number < self.ticks:
                self.due.setdefault(number, []).append(getattr(one, stage))
            else:
                self.late.append((number, self.count, getattr(one, stage)))

    def tick(self, now):
        for number, acts in self.due.items():
            @pl.when(now == number)
            def _():
                for act in acts:
                    act()

    def rest(self):
        for _, _, act in sorted(self.late, key=lambda entry: entry[:2]):
            act()


def store_to(out, cols=None, rows=None):
    def store(value, more):
        index = (slice(None) if rows is None else rows, slice(None) if cols is None else cols)
        out[index] = out[index] + value if more else value

    return store


def spread_masks(devices, piece):
    size = devices * piece
    column = lax.broadcasted_iota(jnp.int32, (devices, size), 1)
    start = lax.broadcasted_iota(jnp.int32, (devices, size), 0) * piece
    owner = jnp.logical_and(column >= start, column < start + piece)
    column = lax.broadcasted_iota(jnp.int32, (BLOCK, size), 1)
    number = jnp.floor((column.astype(F32) + 0.5) * (1.0 / piece)).astype(jnp.int32)
    place = column - number * piece == lax.broadcasted_iota(jnp.int32, (BLOCK, size), 0)
    return owner, place.astype(F32)


def spread_vectors(gathered, pieces):
    masks = {piece: spread_masks(gathered.shape[0], piece) for piece in set(pieces)}
    rows = []
    for index, piece in enumerate(pieces):
        owner, place = masks[piece]
        wide = dot_nn(gathered[:, index, :], place.astype(BF16))
        rows.append(jnp.sum(jnp.where(owner, wide, 0.0), axis=0, keepdims=True))
    return rows


def collect_vector(row, piece, devices):
    owner, place = spread_masks(devices, piece)
    wide = jnp.where(owner, row, 0.0)
    high = wide.astype(BF16)
    low = (wide - high.astype(F32)).astype(BF16)
    place = place.astype(BF16)
    return dot_nt(high, place) + dot_nt(low, place)


OUT_TICKS = (
    (0, "along_z", 1), (0, "across_xy", 0), (0, "along_z", 2), (1, "across_xy", 1), (1, "diagonal", 0),
    (1, "along_z", 3), (2, "across_xy", 2), (2, "diagonal", 1), (3, "across_xy", 3), (3, "diagonal", 2),
    (4, "diagonal", 3),
)
FEED_TICKS = (
    (0, "first_xy"), (0, "along_z", 1), (2, "along_z", 2), (4, "across_xy", 0), (5, "along_z", 3),
    (8, "diagonal", 0), (9, "across_xy", 1), (13, "diagonal", 1), (14, "across_xy", 2),
    (18, "diagonal", 2), (18, "across_xy", 3), (22, "diagonal", 3),
)


def attention_kernel(planes, pieces, tokens_ref, segment_ref, *refs):
    shards, refs = refs[:5], refs[5:]
    if planes:
        fulls, refs = refs[:5], refs[5:]
    else:
        fulls = shards
    (
        qkv_ref, context_ref, lse_ref, normed_ref, inverse_ref, vectors_ref, bin_ref,
        wqkv_ref, wout_ref, small_ref, bias_ref, mask_ref, load_sem, *sems,
    ) = refs
    length, width = tokens_ref.shape
    count = pl.num_programs(0)
    step = pl.program_id(0)
    pairs = width // BLOCK
    offsets, _ = mask_offsets(length)
    gathers = []
    if planes:
        place = Place(planes)
        gathers = [Gather(place, i, shards[i], fulls[i], *sems) for i in range(5)]
    attn, out, feed = gathers[:2], gathers[2:3], gathers[3:]

    def load(index, ref):
        return pltpu.make_async_copy(fulls[index], ref, load_sem.at[index])

    @pl.when(step == 0)
    def _():
        if planes:
            place.enter()
            for gather in attn + out:
                gather.run("first_z")
                gather.run("first_xy")
            for gather in feed:
                gather.run("first_z")
        for seq in range(segment_ref.shape[0]):
            fill_masks(mask_ref, seq, segment_ref[seq])
        for distance in range(1, planes + 2 if planes else 0):
            for gather in attn:
                if distance < planes:
                    gather.run("along_z", distance)
                if distance - 1 < planes:
                    gather.run("across_xy", distance - 1)
                if distance >= 2:
                    gather.run("diagonal", distance - 2)
        for gather in attn:
            gather.finish()
        load(0, wqkv_ref).start()
        load(1, small_ref).start()
        load(1, small_ref).wait()
        small = small_ref[...].astype(F32).reshape(-1, 8, BLOCK)
        bqv, bout, gain_one, shift_one, bin_, bfin, gain_two, shift_two = spread_vectors(small, pieces)
        bias_ref[:, :width] = bqv[:, :width]
        bias_ref[:, width : 2 * width] = jnp.zeros_like(bout)
        bias_ref[:, 2 * width : 3 * width] = bqv[:, width:]
        bias_ref[:, 3 * width :] = bout
        bin_ref[...] = bin_
        for row, vector in enumerate((gain_one, shift_one, bfin, gain_two, shift_two)):
            vectors_ref[row : row + 1] = vector
        vectors_ref[5:8] = jnp.zeros((3, width), F32)
        load(0, wqkv_ref).wait()

    due = {}
    for group, ticks in ((out, OUT_TICKS), (feed, FEED_TICKS)):
        for number, name, *args in ticks:
            for gather in group:
                due.setdefault(number, []).append(functools.partial(gather.run, name, *args))

    for part in range(3):
        cols = slice(part * width, (part + 1) * width)
        joined = dot_nn(tokens_ref[...], wqkv_ref[:, cols]) + bias_ref[:, cols]
        if part == 0:
            joined = joined * HEAD_DIM ** (-0.5)
        qkv_ref[:, cols] = joined.astype(BF16)

    def one_pair(pair, _):
        for number, acts in due.items():
            @pl.when(step * pairs + pair == number)
            def _():
                for act in acts:
                    act()

        def cols(part):
            return pl.ds(pl.multiple_of(part * width + pair * BLOCK, BLOCK), BLOCK)

        for block, (low, high) in enumerate(windows(length)):
            here = slice(block * BLOCK, (block + 1) * BLOCK)
            query = stacked(qkv_ref[here, cols(0)])
            scores = dot_nt(qkv_ref[low:high, cols(1)], query)
            scores = scores + twice(mask_ref[step, pl.ds(offsets[block], high - low), :])
            maxima = jnp.max(scores, axis=0, keepdims=True)
            exponent = jnp.exp(scores - maxima)
            totals = jnp.sum(exponent, axis=0, keepdims=True)
            context = dot_tn(qkv_ref[low:high, cols(2)], exponent.astype(BF16)) * (1.0 / totals)
            context_ref[here, cols(0)] = unstacked_t(context).astype(BF16)
            lse_ref[0, pl.ds(pair * (length // BLOCK) + block, 1), :] = maxima + jnp.log(totals)
        return 0

    lax.fori_loop(0, pairs, one_pair, 0)

    @pl.when(step == 0)
    def _():
        for gather in out:
            gather.finish()
        load(2, wout_ref).start()
        load(2, wout_ref).wait()

    branch = dot_nn(context_ref[...], wout_ref[...]) + bias_ref[:, 3 * width :]
    normed, inverse = normalize(tokens_ref[...].astype(F32) + branch)
    normed_ref[...] = normed
    inverse_ref[...] = jnp.broadcast_to(inverse, inverse_ref.shape)

    @pl.when(step == count - 1)
    def _():
        for gather in feed:
            gather.finish()


def whole(shape):
    return pl.BlockSpec(shape, lambda *_: (0,) * len(shape), pipeline_mode=pl.Buffered(1))


def attention_forward(planes, tokens, segments, weights, pieces):
    count, length = segments.shape[0], segments.shape[2]
    width = tokens.shape[1]
    rows = pl.BlockSpec((length, width), lambda i: (i, 0))
    any_ = pl.BlockSpec(memory_space=pl.ANY)
    lse_rows = (width // BLOCK) * (length // BLOCK)
    hidden = weights[3].shape[-1]
    devices = planes * 8 if planes else weights[1].shape[0] // 8
    gathered = [(devices * w.shape[0], w.shape[1]) for w in weights] if planes else []
    sems = []
    if planes:
        sems = [
            pltpu.SemaphoreType.DMA((5, SENDS)),
            pltpu.SemaphoreType.DMA((5, planes, 2, 2, 2, 2)),
            pltpu.SemaphoreType.DMA((5,)),
        ]
    out = pl.pallas_call(
        functools.partial(attention_kernel, planes, pieces),
        grid=(count,),
        in_specs=[rows, whole(segments.shape)] + [whole(w.shape) if planes else any_ for w in weights],
        out_specs=[any_] * len(gathered) + [
            pl.BlockSpec((length, 3 * width), lambda i: (i, 0)),
            rows,
            pl.BlockSpec((1, lse_rows, 2 * BLOCK), lambda i: (i, 0, 0)),
            rows,
            pl.BlockSpec((length, BLOCK), lambda i: (i, 0)),
            whole((8, width)),
            whole((1, hidden)),
        ],
        out_shape=[jax.ShapeDtypeStruct(s, w.dtype) for s, w in zip(gathered, weights)] + [
            jax.ShapeDtypeStruct((count * length, 3 * width), BF16),
            jax.ShapeDtypeStruct((count * length, width), BF16),
            jax.ShapeDtypeStruct((count, lse_rows, 2 * BLOCK), F32),
            jax.ShapeDtypeStruct((count * length, width), F32),
            jax.ShapeDtypeStruct((count * length, BLOCK), F32),
            jax.ShapeDtypeStruct((8, width), F32),
            jax.ShapeDtypeStruct((1, hidden), F32),
        ],
        scratch_shapes=[
            pltpu.VMEM((width, 3 * width), BF16),
            pltpu.VMEM((width, width), BF16),
            pltpu.VMEM((devices * 8, BLOCK), BF16),
            pltpu.VMEM((1, 4 * width), F32),
            pltpu.VMEM((count, mask_offsets(length)[1], BLOCK), F32),
            pltpu.SemaphoreType.DMA((3,)),
        ] + sems,
        compiler_params=pltpu.CompilerParams(
            vmem_limit_bytes=VMEM_LIMIT,
            **(dict(collective_id=0, has_side_effects=True) if planes else {}),
        ),
        name="attention_forward",
    )(tokens, segments, *weights)
    fulls = out[: len(gathered)] if planes else weights
    return fulls, out[len(gathered) :]


def feed_kernel(
    normed_ref, cot_ref, win_ref, wfin_ref, vec_ref, bin_ref,
    out_ref, act_ref, slope_ref, gsum_ref, gffn_ref, low_ref, gvec_ref,
    hidden_ref,
):
    hidden = normed_ref[...] * vec_ref[0:1] + vec_ref[1:2]
    hidden_ref[...] = hidden
    low_ref[...] = hidden.astype(BF16)
    width = win_ref.shape[0]

    def one_chunk(chunk, _):
        cols = pl.ds(pl.multiple_of(chunk * width, width), width)
        pre = dot_nn(low_ref[...], win_ref[:, cols]) + bin_ref[:, cols]
        active, slope = gelu_parts(pre)
        act_ref[:, cols] = active.astype(BF16)
        slope_ref[:, cols] = slope.astype(BF16)
        return 0

    lax.fori_loop(0, win_ref.shape[1] // width, one_chunk, 0)
    branch = dot_nn(act_ref[...], wfin_ref[...]) + vec_ref[2:3]
    normed, inverse = normalize(hidden_ref[...] + branch)
    gain = vec_ref[3:4]
    out_ref[...] = (normed * gain + vec_ref[4:5]).astype(BF16)
    cot = cot_ref[...].astype(F32)
    gsum = normalize_back(cot * gain, normed, inverse)
    gsum_ref[...] = gsum
    gffn = gsum.astype(BF16)
    gffn_ref[...] = gffn

    @pl.when(pl.program_id(0) == 0)
    def _():
        gvec_ref[...] = jnp.zeros_like(gvec_ref)

    gvec_ref[0:1] += column_sum(cot * normed)
    gvec_ref[1:2] += column_sum(cot)
    gvec_ref[2:3] += column_sum(gffn.astype(F32))


def feed_forward(normed, cotangent, win, wfin, vectors, bin_, tile):
    tokens, width = normed.shape
    hidden = win.shape[1]
    rows = pl.BlockSpec((tile, width), lambda i: (i, 0))
    wide = pl.BlockSpec((tile, hidden), lambda i: (i, 0))
    return pl.pallas_call(
        feed_kernel,
        grid=(tokens // tile,),
        in_specs=[rows, rows, whole(win.shape), whole(wfin.shape), whole(vectors.shape), whole(bin_.shape)],
        out_specs=[rows, wide, wide, rows, rows, rows, pl.BlockSpec((8, width), lambda i: (0, 0))],
        out_shape=[
            jax.ShapeDtypeStruct((tokens, width), BF16),
            jax.ShapeDtypeStruct((tokens, hidden), BF16),
            jax.ShapeDtypeStruct((tokens, hidden), BF16),
            jax.ShapeDtypeStruct((tokens, width), F32),
            jax.ShapeDtypeStruct((tokens, width), BF16),
            jax.ShapeDtypeStruct((tokens, width), BF16),
            jax.ShapeDtypeStruct((8, width), F32),
        ],
        scratch_shapes=[pltpu.VMEM((tile, width), F32)],
        compiler_params=pltpu.CompilerParams(vmem_limit_bytes=VMEM_LIMIT),
        name="feed_forward",
    )(normed, cotangent, win, wfin, vectors, bin_)


def fin_grad_kernel(act_ref, gffn_ref, dwfin_ref):
    dwfin_ref[...] = dot_tn(act_ref[...], gffn_ref[...]).astype(BF16)


def fin_grad(act, gffn, chunk):
    tokens, hidden = act.shape
    width = gffn.shape[1]
    return pl.pallas_call(
        fin_grad_kernel,
        grid=(hidden // chunk,),
        in_specs=[pl.BlockSpec((tokens, chunk), lambda i: (0, i)), whole(gffn.shape)],
        out_specs=pl.BlockSpec((chunk, width), lambda i: (i, 0)),
        out_shape=jax.ShapeDtypeStruct((hidden, width), BF16),
        compiler_params=pltpu.CompilerParams(vmem_limit_bytes=VMEM_LIMIT),
        name="fin_grad",
    )(act, gffn)


FIN_STEPS = ((0, 3, 9, 14), (0, 6, 13, 18), (1, 9, 17, 22), (2, 12, 21, 26))
FEED_CHUNKS = 6


def feed_back_kernel(
    planes, gffn_ref, low_ref, gsum_hbm, slope_ref, win_ref, wfin_ref,
    normed_ref, inverse_ref, context_ref, wout_ref, vec_ref, *refs,
):
    sources, refs = refs[: 1 if planes else 0], refs[1 if planes else 0 :]
    (
        dwin_ref, gbin_ref, gsum_ref, gcon_ref, dwout_ref, gvec_ref, *outs,
    ), refs = refs[: 7 if planes else 6], refs[7 if planes else 6 :]
    low_t_ref, acc_ref, gpre_ref, dwout_acc_ref, sem, *refs = refs
    step = pl.program_id(0)
    tokens = gffn_ref.shape[0]
    tile = normed_ref.shape[0]
    tiles = tokens // tile
    if planes:
        place = Place(planes)
        schedule = Schedule(place, refs[:3], refs[3:], tiles * (FEED_CHUNKS + 1))
        rows = sources[0].shape[4] // 4
        for i in range(4):
            here = slice(i * rows, (i + 1) * rows)
            schedule.add(
                sources[0].at[(slice(None),) * 4 + (here,)], True, store_to(outs[0], rows=here), FIN_STEPS[i]
            )

    @pl.when(step == 0)
    def _():
        copy = pltpu.make_async_copy(gsum_hbm, acc_ref, sem)
        copy.start()
        if planes:
            place.enter()
        low_t_ref[...] = jnp.transpose(low_ref[...])
        gvec_ref[...] = jnp.zeros_like(gvec_ref)
        dwout_acc_ref[...] = jnp.zeros_like(dwout_acc_ref)
        copy.wait()

    @pl.when(step < FEED_CHUNKS)
    def _():
        gbin_ref[...] = jnp.zeros_like(gbin_ref)

        def one_tile(index, _):
            if planes:
                schedule.tick(step * tiles + index)
            here = pl.ds(pl.multiple_of(index * tile, tile), tile)
            gpre = (dot_nt(gffn_ref[here], wfin_ref[...]) * slope_ref[here].astype(F32)).astype(BF16)
            gpre_ref[here] = gpre
            gbin_ref[0:1] += column_sum(gpre.astype(F32))
            acc_ref[here] += dot_nt(gpre, win_ref[...])
            return 0

        lax.fori_loop(0, tiles, one_tile, 0)
        dwin_ref[...] = dot_nn(low_t_ref[...], gpre_ref[...]).astype(BF16)

    @pl.when(step >= FEED_CHUNKS)
    def _():
        index = step - FEED_CHUNKS
        if planes:
            schedule.tick(tiles * FEED_CHUNKS + index)
        ghid = acc_ref[pl.ds(pl.multiple_of(index * tile, tile), tile)]
        normed = normed_ref[...]
        gvec_ref[0:1] += column_sum(ghid * normed)
        gvec_ref[1:2] += column_sum(ghid)
        gsum = normalize_back(ghid * vec_ref[0:1], normed, inverse_ref[:, 0:1])
        gsum_ref[...] = gsum
        gattn = gsum.astype(BF16)
        gvec_ref[2:3] += column_sum(gattn.astype(F32))
        gcon_ref[...] = dot_nt(gattn, wout_ref[...]).astype(BF16)
        dwout_acc_ref[...] += dot_tn(context_ref[...], gattn)

    @pl.when(step == pl.num_programs(0) - 1)
    def _():
        dwout_ref[...] = dwout_acc_ref[...].astype(BF16)
        if planes:
            schedule.rest()


def feed_backward(planes, gffn, low, gsum, slope, win, wfin, normed, inverse, context, wout, vectors, dwfin, tile):
    tokens, width = low.shape
    hidden = win.shape[1]
    chunk = hidden // FEED_CHUNKS
    any_ = pl.BlockSpec(memory_space=pl.ANY)
    sources, outs, out_shape, scratch = [], [], [], []
    if planes:
        source = dwfin.reshape(planes, 2, 2, 2, -1, width)
        sources = [source]
        outs = [whole(source.shape[4:])]
        out_shape = [jax.ShapeDtypeStruct(source.shape[4:], F32)]
        scratch = scatter_sems(planes, 4)
        for _ in range(4):
            scratch += scatter_scratch(planes, source.shape[4] // 4, width, BF16, True)

    def first(step):
        return jnp.minimum(step, FEED_CHUNKS - 1)

    def then(columns):
        return pl.BlockSpec((tile, columns), lambda i: (jnp.maximum(i - FEED_CHUNKS, 0), 0))

    return pl.pallas_call(
        functools.partial(feed_back_kernel, planes),
        grid=(FEED_CHUNKS + tokens // tile,),
        in_specs=[
            whole(gffn.shape), whole(low.shape), any_,
            pl.BlockSpec((tokens, chunk), lambda i: (0, first(i))),
            pl.BlockSpec((width, chunk), lambda i: (0, first(i))),
            pl.BlockSpec((chunk, width), lambda i: (first(i), 0)),
            then(width), then(BLOCK), then(width), whole(wout.shape), whole(vectors.shape),
        ] + [any_] * len(sources),
        out_specs=[
            pl.BlockSpec((width, chunk), lambda i: (0, first(i))),
            pl.BlockSpec((8, chunk), lambda i: (0, first(i))),
            then(width), then(width), whole((width, width)), whole((8, width)),
        ] + outs,
        out_shape=[
            jax.ShapeDtypeStruct((width, hidden), BF16),
            jax.ShapeDtypeStruct((8, hidden), F32),
            jax.ShapeDtypeStruct((tokens, width), F32),
            jax.ShapeDtypeStruct((tokens, width), BF16),
            jax.ShapeDtypeStruct((width, width), BF16),
            jax.ShapeDtypeStruct((8, width), F32),
        ] + out_shape,
        scratch_shapes=[
            pltpu.VMEM((width, tokens), BF16),
            pltpu.VMEM((tokens, width), F32),
            pltpu.VMEM((tokens, chunk), BF16),
            pltpu.VMEM((width, width), F32),
            pltpu.SemaphoreType.DMA,
        ] + scratch,
        compiler_params=pltpu.CompilerParams(
            vmem_limit_bytes=VMEM_LIMIT,
            **(dict(collective_id=2, has_side_effects=True) if planes else {}),
        ),
        name="feed_backward",
    )(gffn, low, gsum, slope, win, wfin, normed, inverse, context, wout, vectors, *sources)


IN_STEPS = ((0, 2, 6, 9), (0, 4, 9, 12), (1, 6, 12, 15), (2, 8, 15, 18))
OUT_STEPS = (3, 10, 17, 20)
PAIR_STEPS = (0, 1, 5, 9)


def attention_back_kernel(
    planes, pieces, devices,
    q_ref, k_ref, v_ref, gcon_ref, lse_ref, segment_ref, tokens_ref, wq_ref, wk_ref, wv_ref, gsum_hbm,
    gtwo_ref, gbin_ref, gone_ref, *refs,
):
    sources, refs = refs[: 2 if planes else 0], refs[2 if planes else 0 :]
    gtok_hbm, refs = refs[0], refs[1:]
    if planes:
        outs, refs = refs[:4], refs[4:]
    else:
        dw_ref, small_ref, refs = refs[0], refs[1], refs[2:]
    tokens_t_ref, acc_ref, mask_ref, grad_ref, dk_ref, dv_ref, gbqv_ref, sem, *refs = refs
    pair = pl.program_id(0)
    last = pl.num_programs(0) - 1
    count, length = segment_ref.shape[0], segment_ref.shape[2]
    total, width = tokens_ref.shape
    pairs = width // BLOCK
    blocks = length // BLOCK
    offsets, _ = mask_offsets(length)
    tile = 512

    if planes:
        place = Place(planes)
        pair_dw_ref, small_ref = refs[3:5]
        schedule = Schedule(place, refs[:3], refs[5:], count * pairs)
        dwin, dwout = sources
        wide = dwin.shape[5] // 4
        for i in range(4):
            cols = slice(i * wide, (i + 1) * wide)
            schedule.add(
                dwin.at[(slice(None),) * 5 + (cols,)], True, store_to(outs[2], cols=cols), IN_STEPS[i]
            )
        schedule.add(dwout, True, store_to(outs[1]), OUT_STEPS)
        for i in range(pairs):
            def store(value, more, i=i):
                for part in range(3):
                    cols = slice(part * BLOCK, (part + 1) * BLOCK)
                    here = slice(part * width + i * BLOCK, part * width + (i + 1) * BLOCK)
                    store_to(outs[0], cols=here)(value[:, cols], more)

            schedule.add(pair_dw_ref.at[i], False, store, [count * (i + 1) + n for n in PAIR_STEPS])
        schedule.add(
            small_ref.reshape(planes, 2, 2, 2, 8, BLOCK), False, store_to(outs[3]),
            [count * pairs + n for n in PAIR_STEPS],
        )

    @pl.when(pair == 0)
    def _():
        copy = pltpu.make_async_copy(gsum_hbm, acc_ref, sem)
        copy.start()
        if planes:
            place.enter()
        tokens_t_ref[...] = jnp.transpose(tokens_ref[...])
        for seq in range(count):
            fill_masks(mask_ref, seq, segment_ref[seq])
        for index, row in (
            (1, gone_ref[2:3]), (2, gone_ref[0:1]), (3, gone_ref[1:2]), (4, gbin_ref[0:1]),
            (5, gtwo_ref[2:3]), (6, gtwo_ref[0:1]), (7, gtwo_ref[1:2]),
        ):
            small_ref[:, index, :] = collect_vector(row, pieces[index], devices)
        copy.wait()

    def one_seq(seq, _):
        if planes:
            schedule.tick(pair * count + seq)
        base = pl.multiple_of(seq * length, length)
        dk_ref[...] = jnp.zeros_like(dk_ref)
        dv_ref[...] = jnp.zeros_like(dv_ref)
        for block, (low, high) in enumerate(windows(length)):
            here = pl.ds(base + block * BLOCK, BLOCK)
            reach = pl.ds(base + low, high - low)
            query = stacked(q_ref[here])
            grad = stacked(gcon_ref[here])
            keys = k_ref[reach]
            scores = dot_nt(keys, query) + twice(mask_ref[seq, pl.ds(offsets[block], high - low), :])
            probs = jnp.exp(scores - lse_ref[seq, pl.ds(pair * blocks + block, 1), :])
            gprobs = dot_nt(v_ref[reach], grad)
            dots = jnp.sum(probs * gprobs, axis=0, keepdims=True)
            gscores = (probs * (gprobs - dots)).astype(BF16)
            dv_ref[low:high] += dot_nn(probs.astype(BF16), grad)
            dk_ref[low:high] += dot_nn(gscores, query)
            gquery = unstacked_t(dot_tn(keys, gscores)) * HEAD_DIM ** (-0.5)
            grad_ref[here, 0:BLOCK] = gquery.astype(BF16)
        rows = pl.ds(base, length)
        grad_ref[rows, BLOCK : 2 * BLOCK] = dk_ref[...].astype(BF16)
        grad_ref[rows, 2 * BLOCK :] = dv_ref[...].astype(BF16)
        return 0

    lax.fori_loop(0, count, one_seq, 0)
    cols = pl.multiple_of(pair * BLOCK, BLOCK)
    gbqv_ref[:, pl.ds(cols, BLOCK)] = column_sum(grad_ref[:, :BLOCK].astype(F32))
    gbqv_ref[:, pl.ds(width + cols, BLOCK)] = column_sum(grad_ref[:, 2 * BLOCK :].astype(F32))
    dw = dot_nn(tokens_t_ref[...], grad_ref[...])
    if planes:
        for part in range(3):
            here = slice(part * BLOCK, (part + 1) * BLOCK)
            pair_dw_ref[pair, ..., here] = dw[:, here].reshape(planes, 2, 2, 2, -1, BLOCK).astype(BF16)
    else:
        dw_ref[...] = dw.astype(BF16)
    weights = jnp.concatenate([wq_ref[...], wk_ref[...], wv_ref[...]], axis=1)
    for start in range(0, total, tile):
        here = slice(start, start + tile)
        acc_ref[here] += dot_nt(grad_ref[here], weights)

    @pl.when(pair == last)
    def _():
        copy = pltpu.make_async_copy(acc_ref, gtok_hbm, sem)
        copy.start()
        small_ref[:, 0, :] = collect_vector(gbqv_ref[...], pieces[0], devices)
        if planes:
            schedule.rest()
        copy.wait()


def attention_backward(planes, pieces, devices, qkv, gcon, lse, segments, tokens, wqkv, gsum, vectors, grads):
    count, length = segments.shape[0], segments.shape[2]
    total, width = tokens.shape
    pairs = width // BLOCK
    any_ = pl.BlockSpec(memory_space=pl.ANY)

    def part(rows, index):
        return pl.BlockSpec((rows, BLOCK), lambda i: (0, index * pairs + i))

    scratch = [
        pltpu.VMEM((width, total), BF16),
        pltpu.VMEM((total, width), F32),
        pltpu.VMEM((count, mask_offsets(length)[1], BLOCK), F32),
        pltpu.VMEM((total, 3 * BLOCK), BF16),
        pltpu.VMEM((length, BLOCK), F32),
        pltpu.VMEM((length, BLOCK), F32),
        pltpu.VMEM((1, 2 * width), F32),
        pltpu.SemaphoreType.DMA,
    ]
    small = (devices, 8, BLOCK)
    if planes:
        grads = [g.reshape((planes, 2, 2, 2, -1) + g.shape[1:]) for g in grads]
        rows = width // devices
        shards = [(rows, 3 * width), (rows, width), grads[0].shape[4:], (8, BLOCK)]
        outs = [whole(shape) for shape in shards]
        out_shape = [jax.ShapeDtypeStruct(shape, F32) for shape in shards]
        scratch += scatter_sems(planes, 6 + pairs) + [
            pltpu.VMEM((pairs, planes, 2, 2, 2, rows, 3 * BLOCK), BF16),
            pltpu.VMEM(small, F32),
        ]
        for shape in [(rows, grads[0].shape[5] // 4)] * 4 + [(rows, width)]:
            scratch += scatter_scratch(planes, *shape, BF16, True)
        for _ in range(pairs):
            scratch += scatter_scratch(planes, rows, 3 * BLOCK, BF16, False)
        scratch += scatter_scratch(planes, 8, BLOCK, F32, False)
    else:
        grads = []
        outs = [pl.BlockSpec((width, 3 * BLOCK), lambda i: (0, i)), whole(small)]
        out_shape = [jax.ShapeDtypeStruct((width, 3 * width), BF16), jax.ShapeDtypeStruct(small, F32)]
    return pl.pallas_call(
        functools.partial(attention_back_kernel, planes, pieces, devices),
        grid=(pairs,),
        in_specs=[
            part(total, 0), part(total, 1), part(total, 2), part(total, 0),
            whole(lse.shape), whole(segments.shape), whole(tokens.shape),
            part(width, 0), part(width, 1), part(width, 2), any_,
        ] + [whole(v.shape) for v in vectors] + [any_] * len(grads),
        out_specs=[any_] + outs,
        out_shape=[jax.ShapeDtypeStruct((total, width), F32)] + out_shape,
        scratch_shapes=scratch,
        compiler_params=pltpu.CompilerParams(
            vmem_limit_bytes=VMEM_LIMIT,
            **(dict(collective_id=1, has_side_effects=True) if planes else {}),
        ),
        name="attention_backward",
    )(qkv, qkv, qkv, gcon, lse, segments, tokens, wqkv, wqkv, wqkv, gsum, *vectors, *grads)


def shards(
    planes,
    tokens, weight_qkv, bias_qv, weight_out, bias_out, gain_one, shift_one,
    weight_in, bias_in, weight_fin, bias_fin, gain_two, shift_two, segments, cotangent,
):
    small = (bias_qv, bias_out, gain_one, shift_one, bias_in, bias_fin, gain_two, shift_two)
    pieces = tuple(v.shape[0] for v in small)
    joined = jnp.stack([jnp.pad(v, (0, BLOCK - v.shape[0])) for v in small])
    weights = [weight_qkv, joined, weight_out, weight_in, weight_fin]
    if not planes:
        weights = [lax.all_gather(w, AXES, axis=0, tiled=True) for w in weights]
    devices = planes * 8 if planes else weights[1].shape[0] // 8
    segments = segments.reshape(segments.shape[0], 1, segments.shape[1])
    fulls, rest = attention_forward(planes, tokens, segments, weights, pieces)
    wqkv, _, wout, win, wfin = fulls
    qkv, context, lse, normed, inverse, vectors, bin_ = rest
    tile, width = min(512, tokens.shape[0]), tokens.shape[1]
    output, act, slope, gsum_two, gffn, low, gvec_two = feed_forward(
        normed, cotangent, win, wfin, vectors, bin_, tile
    )
    dwfin = fin_grad(act, gffn, width)
    dwin, gbin, gsum_one, gcon, dwout, gvec_one, *fin = feed_backward(
        planes, gffn, low, gsum_two, slope, win, wfin, normed, inverse, context, wout, vectors, dwfin, tile
    )
    gtok, *sums = attention_backward(
        planes, pieces, devices, qkv, gcon, lse, segments, tokens, wqkv, gsum_one,
        (gvec_two, gbin, gvec_one), [dwin, dwout],
    )
    if not planes:
        sums = [
            lax.psum_scatter(g.reshape((devices, -1) + g.shape[-1:]), AXES, scatter_dimension=0).astype(F32)
            for g in (sums[0], dwout, dwin, sums[1], dwfin)
        ]
        sums[0] = sums[0].reshape(sums[0].shape[0], -1, 3, BLOCK).swapaxes(1, 2).reshape(sums[0].shape)
        fin = sums[4:]
    parts = [sums[3][i, :piece] for i, piece in enumerate(pieces)]
    return (
        output, gtok, sums[0], parts[0], sums[1], parts[1], parts[2], parts[3],
        sums[2], parts[4], fin[0], parts[5], parts[6], parts[7],
    )


AXES = ("dp", "inner")


def solution(mesh):
    row, vec = P(AXES, None), P(AXES)
    in_specs = (row, row, vec, row, vec, vec, vec, row, vec, row, vec, vec, vec, row, row)
    out_specs = (row, row, row, vec, row, vec, vec, vec, row, vec, row, vec, vec, vec)
    planes = mesh.shape["dp"] // 4 if mesh.shape["inner"] == 2 and mesh.shape["dp"] == 16 else 0
    return jax.shard_map(
        functools.partial(shards, planes),
        mesh=mesh, in_specs=in_specs, out_specs=out_specs, check_vma=False,
    )
```

```python
import functools

import jax
import jax.numpy as jnp
from jax import lax
from jax.experimental import pallas as pl
from jax.experimental.pallas import tpu as pltpu
from jax.sharding import PartitionSpec as P

HEAD_DIM = 64
BLOCK = 128
EPSILON = 1e-06
NEG_FILL = -1e30
F32 = jnp.float32
BF16 = jnp.bfloat16
VMEM_LIMIT = 60 << 20


def dot(left, right, dims):
    return lax.dot_general(left, right, ((dims[:1], dims[1:]), ((), ())), preferred_element_type=F32)


def dot_nn(left, right):
    return dot(left, right, (1, 0))


def dot_nt(left, right):
    return dot(left, right, (1, 1))


def dot_tn(left, right):
    return dot(left, right, (0, 0))


def windows(length):
    return [
        (max(0, start - BLOCK), min(length, start + 2 * BLOCK))
        for start in range(0, length, BLOCK)
    ]


def mask_offsets(length):
    offsets, total = [], 0
    for low, high in windows(length):
        offsets.append(total)
        total += high - low
    return offsets, total


def fill_masks(mask_ref, seq, segment_row):
    length = segment_row.shape[1]
    columns = jnp.transpose(jnp.broadcast_to(segment_row, (BLOCK, length)))
    offsets, _ = mask_offsets(length)
    for block, (low, high) in enumerate(windows(length)):
        rows = jnp.broadcast_to(
            segment_row[:, block * BLOCK : (block + 1) * BLOCK], (high - low, BLOCK)
        )
        mask_ref[seq, pl.ds(offsets[block], high - low), :] = jnp.where(
            columns[low:high] == rows, 0.0, NEG_FILL
        )


def stacked(pair):
    lane = lax.broadcasted_iota(jnp.int32, pair.shape, 1)
    zero = jnp.zeros_like(pair)
    return jnp.concatenate(
        [jnp.where(lane < HEAD_DIM, pair, zero), jnp.where(lane < HEAD_DIM, zero, pair)], axis=0
    )


def unstacked_t(joined):
    row = lax.broadcasted_iota(jnp.int32, (2 * HEAD_DIM, BLOCK), 0)
    return jnp.transpose(jnp.where(row < HEAD_DIM, joined[:, :BLOCK], joined[:, BLOCK:]))


def twice(mask):
    return jnp.concatenate([mask, mask], axis=1)


def normalize(summed):
    center = summed - jnp.mean(summed, axis=-1, keepdims=True)
    inverse = lax.rsqrt(jnp.mean(center * center, axis=-1, keepdims=True) + EPSILON)
    return (center * inverse, inverse)


def normalize_back(grad_normed, normed, inverse):
    mean_grad = jnp.mean(grad_normed, axis=-1, keepdims=True)
    mean_cross = jnp.mean(grad_normed * normed, axis=-1, keepdims=True)
    return inverse * (grad_normed - mean_grad - normed * mean_cross)


def column_sum(rows):
    return jnp.sum(rows, axis=0, keepdims=True)


def gelu_parts(pre):
    cdf = 0.5 + 0.5 * lax.erf(pre * 0.7071067811865476)
    bell = jnp.exp2((-0.7213475204444817 * pre) * pre)
    return (pre * cdf, cdf + pre * (bell * 0.3989422804014327))


MESH = pl.DeviceIdType.MESH


def when(condition, body):
    if condition is True:
        body()
    else:
        pl.when(condition)(body)


class Place:
    def __init__(self, planes):
        along = lax.axis_index("dp")
        self.planes = planes
        self.y = lax.axis_index("inner")
        self.c = lax.rem(along, 2)
        self.x = lax.rem(lax.div(along, 2), 2)
        self.z = lax.div(along, 4)

    def device(self, z=None, x=None, c=None, y=None):
        z = self.z if z is None else z
        x = self.x if x is None else x
        c = self.c if c is None else c
        return ((z * 2 + x) * 2 + c, self.y if y is None else y)

    @property
    def above(self):
        return self.device(z=jnp.minimum(self.z + 1, self.planes - 1))

    @property
    def below(self):
        return self.device(z=jnp.maximum(self.z - 1, 0))

    @property
    def across(self):
        return self.device(x=1 - self.x)

    @property
    def beside(self):
        return self.device(y=1 - self.y)

    @property
    def partner(self):
        return self.device(c=1 - self.c)

    @property
    def has_above(self):
        return self.z < self.planes - 1

    @property
    def has_below(self):
        return self.z > 0

    @property
    def diagonal(self):
        return self.device(x=1 - self.x, y=1 - self.y)

    def enter(self):
        barrier = pltpu.get_barrier_semaphore()
        planes = [self.device(z=lax.rem(self.z + i, self.planes)) for i in range(1, self.planes)]
        devices = [self.across, self.beside, self.diagonal, self.partner] + planes
        for device in devices:
            pl.semaphore_signal(barrier, inc=1, device_id=device, device_id_type=MESH)
        pl.semaphore_wait(barrier, len(devices))


def half_of(ref, half):
    if half == 2:
        return ref
    width = ref.shape[-1] // 2
    lead = (slice(None),) * (len(ref.shape) - 1)
    return ref.at[lead + (slice(half * width, (half + 1) * width),)]


SENDS = 64


class Gather:
    def __init__(self, place, index, shard, full, send, recv, local):
        self.place, self.index, self.shard, self.full = place, index, shard, full
        self.send, self.recv, self.local = send, recv, local
        self.rows = shard.shape[0]
        self.halves = (0, 1) if full.shape[-1] % (2 * BLOCK) == 0 else (2, None)
        self.slot = 0
        self.draining = False
        self.log = []

    def entry(self, z, x, c, y):
        device = ((z * 2 + x) * 2 + c) * 2 + y
        return self.full.at[pl.ds(pl.multiple_of(device * self.rows, 8), self.rows)]

    def run(self, name, *args):
        self.log.append((name, args))
        getattr(self, name)(*args)

    def push(self, condition, item, half, device, source=None):
        slot = self.slot
        self.slot += 1
        assert slot < SENDS

        def make():
            return pltpu.make_async_remote_copy(
                src_ref=half_of(self.entry(*item) if source is None else source, half),
                dst_ref=half_of(self.entry(*item), half),
                send_sem=self.send.at[self.index, slot],
                recv_sem=self.recv.at[(self.index,) + item + (min(half, 1),)],
                device_id=device,
                device_id_type=MESH,
            )

        if self.draining:
            when(condition, lambda: make().wait_send())
        else:
            when(condition, lambda: make().start())

    def await_item(self, item, half):
        if self.draining:
            return
        ref = half_of(self.entry(*item), half)
        pltpu.make_async_remote_copy(
            src_ref=ref, dst_ref=ref, send_sem=self.send.at[self.index, 0],
            recv_sem=self.recv.at[(self.index,) + item + (min(half, 1),)],
            device_id=self.place.partner, device_id_type=MESH,
        ).wait_recv()

    def own_copy(self):
        p = self.place
        return pltpu.make_async_copy(
            self.shard, self.entry(p.z, p.x, p.c, p.y), self.local.at[self.index]
        )

    def first_z(self):
        p = self.place
        item = (p.z, p.x, p.c, p.y)
        self.push(p.has_above, item, 2, p.above, self.shard)
        self.push(p.has_below, item, 2, p.below, self.shard)
        if not self.draining:
            self.own_copy().start()

    def first_xy(self):
        p = self.place
        item = (p.z, p.x, p.c, p.y)
        for device in (p.across, p.beside, p.partner):
            self.push(True, item, 2, device, self.shard)

    def planes_at(self, distance):
        p = self.place
        if distance == 0:
            return [(True, p.z, None, None)]
        return [
            (p.z >= distance, p.z - distance, p.has_above, p.above),
            (p.z + distance < p.planes, p.z + distance, p.has_below, p.below),
        ]

    def along_z(self, distance):
        p = self.place
        for there, z, more, onward in self.planes_at(distance):
            item = (jnp.clip(z, 0, p.planes - 1), p.x, p.c, p.y)
            if not self.draining:
                when(there, lambda: self.await_item(item, 2))
            self.push(jnp.logical_and(there, more), item, 2, onward)
            for device in (p.across, p.beside, p.partner):
                self.push(there, item, 2, device)

    def across_xy(self, distance):
        p = self.place
        for there, z, _, _ in self.planes_at(distance):
            z = jnp.clip(z, 0, p.planes - 1)
            for half, item, onward in (
                (self.halves[0], (z, 1 - p.x, p.c, p.y), p.beside),
                (self.halves[1], (z, p.x, p.c, 1 - p.y), p.across),
            ):
                if not self.draining:
                    when(there, lambda: self.await_item(item, 2))
                if half is not None:
                    self.push(there, item, half, onward)
                self.push(there, item, 2, p.partner)

    def diagonal(self, distance):
        p = self.place
        for there, z, _, _ in self.planes_at(distance):
            item = (jnp.clip(z, 0, p.planes - 1), 1 - p.x, p.c, 1 - p.y)

            def arrive():
                for half in self.halves:
                    if half is not None:
                        self.await_item(item, half)

            if not self.draining:
                when(there, arrive)
            self.push(there, item, 2, p.partner)

    def finish(self):
        p = self.place
        for z in range(p.planes):
            for x in range(2):
                for y in range(2):
                    self.await_item((z, x, 1 - p.c, y), 2)
        self.own_copy().wait()
        self.draining, self.slot = True, 0
        for name, args in self.log:
            getattr(self, name)(*args)


class Bundles:
    def __init__(self, place, index, shard, full, send, recv, local):
        self.place, self.index, self.shard, self.full = place, index, shard, full
        self.send, self.recv, self.local = send, recv, local

    def copy(self, slot, src, dst, device, arrival=None):
        return pltpu.make_async_remote_copy(
            src_ref=src, dst_ref=dst, send_sem=self.send.at[self.index, slot],
            recv_sem=self.recv.at[self.index, slot if arrival is None else arrival],
            device_id=device, device_id_type=MESH,
        )

    def own_copy(self):
        p = self.place
        return pltpu.make_async_copy(
            self.shard, self.full.at[p.z, p.x, p.c, p.y], self.local.at[self.index]
        )

    def z_copy(self, z):
        p = self.place
        return self.copy(z, self.shard, self.full.at[p.z, p.x, p.c, p.y], p.device(z=z), p.z)

    def z_arrival(self, z):
        p = self.place
        return self.copy(z, self.shard, self.full.at[z, p.x, p.c, p.y], p.device(z=z))

    def bundle(self, step, here):
        p = self.place
        full = self.full
        other = {"across": p.across, "beside": p.beside, "partner": p.partner}
        to, x, y, half = (
            ("across", 0, 0, 2), ("beside", 0, 0, 2), ("partner", 0, 0, 2),
            ("beside", 1, 0, 0), ("across", 0, 1, 1), ("partner", 1, 0, 2), ("partner", 0, 1, 2),
            ("partner", 1, 1, 2),
        )[step]
        c = p.c
        if not here:
            x = 1 - x if to == "across" else x
            y = 1 - y if to == "beside" else y
            c = 1 - c if to == "partner" else c
        ref = half_of(full.at[:, 1 - p.x if x else p.x, c, 1 - p.y if y else p.y], half)
        return self.copy(p.planes + step, ref, ref, other[to])

    def first(self):
        for z in range(self.place.planes):
            when(z != self.place.z, lambda: self.z_copy(z).start())
        self.own_copy().start()

    def move(self, arrived, onward):
        for step in arrived:
            self.bundle(step, False).wait_recv()
        for step in onward:
            self.bundle(step, True).start()

    def after_z(self):
        for z in range(self.place.planes):
            when(z != self.place.z, lambda: self.z_arrival(z).wait_recv())
        self.own_copy().wait()
        self.move((), (0, 1, 2))

    def after_side(self):
        self.move((0, 1), (3, 4, 5, 6))

    def after_diagonal(self):
        self.move((3, 4), (7,))

    def finish(self):
        self.move((2, 5, 6, 7), ())
        for z in range(self.place.planes):
            when(z != self.place.z, lambda: self.z_copy(z).wait_send())
        for step in range(8):
            self.bundle(step, True).wait_send()


class Scatter:
    def __init__(self, place, index, source, held, bufs, sems, store):
        self.place, self.index, self.source, self.store = place, index, source, store
        self.held = source.at[:, :, place.c] if held is None else held
        self.loads = held is not None
        self.from_partner, self.from_square, self.spare, self.from_z = bufs
        self.send, self.recv, self.local = sems
        self.dtype = source.dtype

    def copy(self, slot, src, dst, device, arrival=None):
        return pltpu.make_async_remote_copy(
            src_ref=src, dst_ref=dst, send_sem=self.send.at[self.index, slot],
            recv_sem=self.recv.at[self.index, slot if arrival is None else arrival],
            device_id=device, device_id_type=MESH,
        )

    def own_copy(self):
        return pltpu.make_async_copy(
            self.source.at[:, :, self.place.c], self.held, self.local.at[self.index]
        )

    def partner_copy(self):
        p = self.place
        return self.copy(0, self.source.at[:, :, 1 - p.c], self.from_partner, p.partner)

    def square(self):
        p = self.place
        return ((1 - p.x, 1 - p.y, p.diagonal), (1 - p.x, p.y, p.across), (p.x, 1 - p.y, p.beside))

    def square_copies(self):
        return [
            self.copy(1 + i, self.held.at[:, x, y], self.from_square.at[i], device)
            for i, (x, y, device) in enumerate(self.square())
        ]

    def z_copy(self, z):
        p = self.place
        return self.copy(4 + z, self.spare.at[z], self.from_z.at[p.z], p.device(z=z), 4 + p.z)

    def z_arrival(self, z):
        p = self.place
        return self.copy(4 + z, self.spare.at[z], self.from_z.at[z], p.device(z=z), 4 + z)

    def start(self):
        if self.loads:
            self.own_copy().start()
        self.partner_copy().start()

    def after_partner(self):
        p = self.place
        if self.loads:
            self.own_copy().wait()
        self.partner_copy().wait_recv()

        def add(x, y):
            def one(z, _):
                total = self.held[z, x, y].astype(F32) + self.from_partner[z, x, y].astype(F32)
                self.held[z, x, y] = total.astype(self.dtype)
                return 0

            lax.fori_loop(0, p.planes, one, 0)

        for (x, y, _), copy in zip(self.square(), self.square_copies()):
            add(x, y)
            copy.start()
        add(p.x, p.y)

    def after_square(self):
        p = self.place
        for copy in self.square_copies():
            copy.wait_recv()

        def one(z, _):
            total = self.held[z, p.x, p.y].astype(F32)
            for i in range(3):
                total = total + self.from_square[i, z].astype(F32)
            self.spare[z] = total.astype(self.dtype)
            return 0

        lax.fori_loop(0, p.planes, one, 0)
        for z in range(p.planes):
            when(z != p.z, lambda: self.z_copy(z).start())

    def finish(self):
        p = self.place
        self.store(self.spare[p.z].astype(F32), False)
        for z in range(p.planes):
            def arrive(z=z):
                self.z_arrival(z).wait_recv()
                self.store(self.from_z[z].astype(F32), True)

            when(z != p.z, arrive)
        self.partner_copy().wait_send()
        for copy in self.square_copies():
            copy.wait_send()
        for z in range(p.planes):
            when(z != p.z, lambda: self.z_copy(z).wait_send())


STAGES = ("start", "after_partner", "after_square", "finish")


def scatter_scratch(planes, rows, width, dtype, held):
    return ([pltpu.VMEM((planes, 2, 2, rows, width), dtype)] if held else []) + [
        pltpu.VMEM((planes, 2, 2, rows, width), dtype),
        pltpu.VMEM((3, planes, rows, width), dtype),
        pltpu.VMEM((planes, rows, width), dtype),
        pltpu.VMEM((planes, rows, width), dtype),
    ]


def scatter_sems(planes, number):
    return [
        pltpu.SemaphoreType.DMA((number, 4 + planes)),
        pltpu.SemaphoreType.DMA((number, 4 + planes)),
        pltpu.SemaphoreType.DMA((number,)),
    ]


class Schedule:
    def __init__(self, place, sems, scratch, ticks):
        self.place, self.sems, self.scratch, self.ticks = place, sems, scratch, ticks
        self.count, self.due, self.late = 0, {}, []

    def add(self, source, load, store, steps):
        size = 5 if load else 4
        bufs, self.scratch = self.scratch[:size], self.scratch[size:]
        held, bufs = (bufs[0], bufs[1:]) if load else (None, bufs)
        one = Scatter(self.place, self.count, source, held, bufs, self.sems, store)
        self.count += 1
        for stage, number in zip(STAGES, steps):
            if number < self.ticks:
                self.due.setdefault(number, []).append(getattr(one, stage))
            else:
                self.late.append((number, self.count, getattr(one, stage)))

    def tick(self, now):
        for number, acts in self.due.items():
            @pl.when(now == number)
            def _():
                for act in acts:
                    act()

    def rest(self):
        for _, _, act in sorted(self.late, key=lambda entry: entry[:2]):
            act()


def store_to(out, cols=None, rows=None):
    def store(value, more):
        index = (slice(None) if rows is None else rows, slice(None) if cols is None else cols)
        out[index] = out[index] + value if more else value

    return store


def spread_masks(devices, piece):
    size = devices * piece
    column = lax.broadcasted_iota(jnp.int32, (devices, size), 1)
    start = lax.broadcasted_iota(jnp.int32, (devices, size), 0) * piece
    owner = jnp.logical_and(column >= start, column < start + piece)
    column = lax.broadcasted_iota(jnp.int32, (BLOCK, size), 1)
    number = jnp.floor((column.astype(F32) + 0.5) * (1.0 / piece)).astype(jnp.int32)
    place = column - number * piece == lax.broadcasted_iota(jnp.int32, (BLOCK, size), 0)
    return owner, place.astype(F32)


def spread_vectors(gathered, pieces):
    masks = {piece: spread_masks(gathered.shape[0], piece) for piece in set(pieces)}
    rows = []
    for index, piece in enumerate(pieces):
        owner, place = masks[piece]
        wide = dot_nn(gathered[:, index, :], place.astype(BF16))
        rows.append(jnp.sum(jnp.where(owner, wide, 0.0), axis=0, keepdims=True))
    return rows


def collect_vector(row, piece, devices):
    owner, place = spread_masks(devices, piece)
    wide = jnp.where(owner, row, 0.0)
    high = wide.astype(BF16)
    low = (wide - high.astype(F32)).astype(BF16)
    place = place.astype(BF16)
    return dot_nt(high, place) + dot_nt(low, place)


GATHER_STEPS = (
    (11, 17, 21, 23), (-2, 2, 7, 11), (-1, 4, 11, 15), (0, 8, 15, 19), (4, 12, 19, 22),
)


def attention_kernel(planes, pieces, tokens_ref, segment_ref, *refs):
    shards, refs = refs[:5], refs[5:]
    if planes:
        fulls, refs = refs[:5], refs[5:]
    else:
        fulls = shards
    (
        qkv_ref, context_ref, lse_ref, vectors_ref, bin_ref,
        wqkv_ref, small_ref, bias_ref, mask_ref, load_sem, *sems,
    ) = refs
    length, width = tokens_ref.shape
    count = pl.num_programs(0)
    step = pl.program_id(0)
    pairs = width // BLOCK
    offsets, _ = mask_offsets(length)
    gathers = []
    if planes:
        place = Place(planes)
        gathers = [Gather(place, i, shards[i], fulls[i], *sems[:3]) for i in range(2)]
        cuts = [(2, ()), (3, (slice(None), 0)), (3, (slice(None), 1)), (4, (0,)), (4, (1,))]
        for i, (array, cut) in enumerate(cuts):
            shard, full = shards[array], fulls[array]
            if cut:
                size = shard.shape[len(cut) - 1] // 2
                cut = cut[:-1] + (slice(cut[-1] * size, (cut[-1] + 1) * size),)
                shard, full = shard.at[cut], full.at[(slice(None),) * 4 + cut]
            gathers.append(Bundles(place, i, shard, full, *sems[3:]))
    attn, later = gathers[:2], gathers[2:]
    due = {}
    for gather, steps in zip(later, GATHER_STEPS):
        for number, act in zip(steps, (gather.first, gather.after_z, gather.after_side, gather.after_diagonal)):
            due.setdefault(number, []).append(act)

    def load(index, ref):
        return pltpu.make_async_copy(fulls[index], ref, load_sem.at[index])

    @pl.when(step == 0)
    def _():
        if planes:
            place.enter()
            for gather in attn:
                gather.run("first_z")
                gather.run("first_xy")
            for act in due.get(-4, []):
                act()
        for seq in range(segment_ref.shape[0]):
            fill_masks(mask_ref, seq, segment_ref[seq])
        for distance in range(1, planes + 2 if planes else 0):
            for gather in attn:
                if distance < planes:
                    gather.run("along_z", distance)
            for act in due.get(distance - 4, []) if distance < 4 else ():
                act()
            for gather in attn:
                if distance - 1 < planes:
                    gather.run("across_xy", distance - 1)
                if distance >= 2:
                    gather.run("diagonal", distance - 2)
        for gather in attn:
            gather.finish()
        load(0, wqkv_ref).start()
        load(1, small_ref).start()
        load(1, small_ref).wait()
        small = small_ref[...].astype(F32).reshape(-1, 8, BLOCK)
        bqv, bout, gain_one, shift_one, bin_, bfin, gain_two, shift_two = spread_vectors(small, pieces)
        bias_ref[:, :width] = bqv[:, :width]
        bias_ref[:, width : 2 * width] = jnp.zeros_like(bout)
        bias_ref[:, 2 * width :] = bqv[:, width:]
        bin_ref[...] = bin_
        for row, vector in enumerate((gain_one, shift_one, bfin, gain_two, shift_two, bout)):
            vectors_ref[row : row + 1] = vector
        vectors_ref[6:8] = jnp.zeros((2, width), F32)
        load(0, wqkv_ref).wait()

    for part in range(3):
        cols = slice(part * width, (part + 1) * width)
        joined = dot_nn(tokens_ref[...], wqkv_ref[:, cols]) + bias_ref[:, cols]
        if part == 0:
            joined = joined * HEAD_DIM ** (-0.5)
        qkv_ref[:, cols] = joined.astype(BF16)

    def one_pair(pair, _):
        for number, acts in due.items():
            if number < 0:
                continue

            @pl.when(step * pairs + pair == number)
            def _():
                for act in acts:
                    act()

        def cols(part):
            return pl.ds(pl.multiple_of(part * width + pair * BLOCK, BLOCK), BLOCK)

        reach = windows(length)
        here = [slice(block * BLOCK, (block + 1) * BLOCK) for block in range(len(reach))]
        scores = [
            dot_nt(qkv_ref[low:high, cols(1)], stacked(qkv_ref[rows, cols(0)]))
            + twice(mask_ref[step, pl.ds(offsets[block], high - low), :])
            for block, (rows, (low, high)) in enumerate(zip(here, reach))
        ]
        maxima = [jnp.max(score, axis=0, keepdims=True) for score in scores]
        exponents = [jnp.exp(score - peak) for score, peak in zip(scores, maxima)]
        totals = [jnp.sum(exponent, axis=0, keepdims=True) for exponent in exponents]
        contexts = [
            dot_tn(qkv_ref[low:high, cols(2)], exponent.astype(BF16)) * (1.0 / total)
            for exponent, total, (low, high) in zip(exponents, totals, reach)
        ]
        for block, context in enumerate(contexts):
            context_ref[here[block], cols(0)] = unstacked_t(context).astype(BF16)
            lse_ref[0, pl.ds(pair * len(reach) + block, 1), :] = maxima[block] + jnp.log(totals[block])
        return 0

    lax.fori_loop(0, pairs, one_pair, 0)

    @pl.when(step == count - 1)
    def _():
        for gather in later:
            gather.finish()


def whole(shape):
    return pl.BlockSpec(shape, lambda *_: (0,) * len(shape), pipeline_mode=pl.Buffered(1))


def attention_forward(planes, tokens, segments, weights, pieces):
    count, length = segments.shape[0], segments.shape[2]
    width = tokens.shape[1]
    rows = pl.BlockSpec((length, width), lambda i: (i, 0))
    any_ = pl.BlockSpec(memory_space=pl.ANY)
    lse_rows = (width // BLOCK) * (length // BLOCK)
    hidden = weights[3].shape[-1]
    devices = planes * 8 if planes else weights[1].shape[0] // 8
    gathered = []
    if planes:
        gathered = [(devices * w.shape[0], w.shape[1]) for w in weights[:2]]
        gathered += [(planes, 2, 2, 2) + w.shape for w in weights[2:]]
    sems = []
    if planes:
        sems = [
            pltpu.SemaphoreType.DMA((2, SENDS)),
            pltpu.SemaphoreType.DMA((2, planes, 2, 2, 2, 2)),
            pltpu.SemaphoreType.DMA((2,)),
            pltpu.SemaphoreType.DMA((5, planes + 8)),
            pltpu.SemaphoreType.DMA((5, planes + 8)),
            pltpu.SemaphoreType.DMA((5,)),
        ]
    out = pl.pallas_call(
        functools.partial(attention_kernel, planes, pieces),
        grid=(count,),
        in_specs=[rows, whole(segments.shape)] + [whole(w.shape) if planes else any_ for w in weights],
        out_specs=[any_] * len(gathered) + [
            pl.BlockSpec((length, 3 * width), lambda i: (i, 0)),
            rows,
            pl.BlockSpec((1, lse_rows, 2 * BLOCK), lambda i: (i, 0, 0)),
            whole((8, width)),
            whole((1, hidden)),
        ],
        out_shape=[jax.ShapeDtypeStruct(s, w.dtype) for s, w in zip(gathered, weights)] + [
            jax.ShapeDtypeStruct((count * length, 3 * width), BF16),
            jax.ShapeDtypeStruct((count * length, width), BF16),
            jax.ShapeDtypeStruct((count, lse_rows, 2 * BLOCK), F32),
            jax.ShapeDtypeStruct((8, width), F32),
            jax.ShapeDtypeStruct((1, hidden), F32),
        ],
        scratch_shapes=[
            pltpu.VMEM((width, 3 * width), BF16),
            pltpu.VMEM((devices * 8, BLOCK), BF16),
            pltpu.VMEM((1, 3 * width), F32),
            pltpu.VMEM((count, mask_offsets(length)[1], BLOCK), F32),
            pltpu.SemaphoreType.DMA((2,)),
        ] + sems,
        compiler_params=pltpu.CompilerParams(
            vmem_limit_bytes=VMEM_LIMIT,
            **(dict(collective_id=0, has_side_effects=True) if planes else {}),
        ),
        name="attention_forward",
    )(tokens, segments, *weights)
    fulls = out[: len(gathered)] if planes else weights
    return [f.reshape(-1, f.shape[-1]) for f in fulls], out[len(gathered) :]


def feed_kernel(
    tokens_ref, context_ref, cot_ref, wout_ref, win_ref, wfin_ref, vec_ref, bin_ref,
    normed_ref, inverse_ref, out_ref, act_ref, slope_ref, gsum_ref, gffn_ref, low_ref, gvec_ref,
    hidden_ref,
):
    branch = dot_nn(context_ref[...], wout_ref[...]) + vec_ref[5:6]
    normed, inverse = normalize(tokens_ref[...].astype(F32) + branch)
    normed_ref[...] = normed
    inverse_ref[...] = jnp.broadcast_to(inverse, inverse_ref.shape)
    hidden = normed * vec_ref[0:1] + vec_ref[1:2]
    hidden_ref[...] = hidden
    low_ref[...] = hidden.astype(BF16)
    width = 2 * BLOCK

    def one_chunk(chunk, _):
        cols = pl.ds(pl.multiple_of(chunk * width, width), width)
        pre = dot_nn(low_ref[...], win_ref[:, cols]) + bin_ref[:, cols]
        active, slope = gelu_parts(pre)
        act_ref[:, cols] = active.astype(BF16)
        slope_ref[:, cols] = slope.astype(BF16)
        return 0

    lax.fori_loop(0, win_ref.shape[1] // width, one_chunk, 0, unroll=True)
    branch = dot_nn(act_ref[...], wfin_ref[...]) + vec_ref[2:3]
    normed, inverse = normalize(hidden_ref[...] + branch)
    gain = vec_ref[3:4]
    out_ref[...] = (normed * gain + vec_ref[4:5]).astype(BF16)
    cot = cot_ref[...].astype(F32)
    gsum = normalize_back(cot * gain, normed, inverse)
    gsum_ref[...] = gsum
    gffn = gsum.astype(BF16)
    gffn_ref[...] = gffn

    @pl.when(pl.program_id(0) == 0)
    def _():
        gvec_ref[...] = jnp.zeros_like(gvec_ref)

    gvec_ref[0:1] += column_sum(cot * normed)
    gvec_ref[1:2] += column_sum(cot)
    gvec_ref[2:3] += column_sum(gffn.astype(F32))


def feed_forward(tokens, context, cotangent, wout, win, wfin, vectors, bin_, tile):
    total, width = tokens.shape
    hidden = win.shape[1]
    rows = pl.BlockSpec((tile, width), lambda i: (i, 0))
    wide = pl.BlockSpec((tile, hidden), lambda i: (i, 0))
    return pl.pallas_call(
        feed_kernel,
        grid=(total // tile,),
        in_specs=[rows, rows, rows] + [whole(w.shape) for w in (wout, win, wfin, vectors, bin_)],
        out_specs=[
            rows, pl.BlockSpec((tile, BLOCK), lambda i: (i, 0)), rows, wide, wide, rows, rows, rows,
            pl.BlockSpec((8, width), lambda i: (0, 0)),
        ],
        out_shape=[
            jax.ShapeDtypeStruct((total, width), F32),
            jax.ShapeDtypeStruct((total, BLOCK), F32),
            jax.ShapeDtypeStruct((total, width), BF16),
            jax.ShapeDtypeStruct((total, hidden), BF16),
            jax.ShapeDtypeStruct((total, hidden), BF16),
            jax.ShapeDtypeStruct((total, width), F32),
            jax.ShapeDtypeStruct((total, width), BF16),
            jax.ShapeDtypeStruct((total, width), BF16),
            jax.ShapeDtypeStruct((8, width), F32),
        ],
        scratch_shapes=[pltpu.VMEM((tile, width), F32)],
        compiler_params=pltpu.CompilerParams(vmem_limit_bytes=VMEM_LIMIT),
        name="feed_forward",
    )(tokens, context, cotangent, wout, win, wfin, vectors, bin_)


def fin_grad_kernel(act_ref, gffn_ref, dwfin_ref):
    dwfin_ref[...] = dot_tn(act_ref[...], gffn_ref[...]).astype(BF16)


def fin_grad(act, gffn, chunk):
    tokens, hidden = act.shape
    width = gffn.shape[1]
    return pl.pallas_call(
        fin_grad_kernel,
        grid=(hidden // chunk,),
        in_specs=[pl.BlockSpec((tokens, chunk), lambda i: (0, i)), whole(gffn.shape)],
        out_specs=pl.BlockSpec((chunk, width), lambda i: (i, 0)),
        out_shape=jax.ShapeDtypeStruct((hidden, width), BF16),
        compiler_params=pltpu.CompilerParams(vmem_limit_bytes=VMEM_LIMIT),
        name="fin_grad",
    )(act, gffn)


FIN_STEPS = ((0, 3, 9, 14), (0, 6, 13, 18), (1, 9, 17, 22), (2, 12, 21, 26))
FEED_CHUNKS = 6


def feed_back_kernel(
    planes, gffn_ref, low_ref, gsum_hbm, slope_ref, win_ref, wfin_ref,
    normed_ref, inverse_ref, context_ref, wout_ref, vec_ref, *refs,
):
    sources, refs = refs[: 1 if planes else 0], refs[1 if planes else 0 :]
    (
        dwin_ref, gbin_ref, gsum_ref, gcon_ref, dwout_ref, gvec_ref, *outs,
    ), refs = refs[: 7 if planes else 6], refs[7 if planes else 6 :]
    low_t_ref, acc_ref, gpre_ref, dwout_acc_ref, sem, *refs = refs
    step = pl.program_id(0)
    tokens = gffn_ref.shape[0]
    tile = normed_ref.shape[0]
    tiles = tokens // tile
    if planes:
        place = Place(planes)
        schedule = Schedule(place, refs[:3], refs[3:], tiles * (FEED_CHUNKS + 1))
        rows = sources[0].shape[4] // 4
        for i in range(4):
            here = slice(i * rows, (i + 1) * rows)
            schedule.add(
                sources[0].at[(slice(None),) * 4 + (here,)], True, store_to(outs[0], rows=here), FIN_STEPS[i]
            )

    @pl.when(step == 0)
    def _():
        copy = pltpu.make_async_copy(gsum_hbm, acc_ref, sem)
        copy.start()
        if planes:
            place.enter()
        low_t_ref[...] = jnp.transpose(low_ref[...])
        gvec_ref[...] = jnp.zeros_like(gvec_ref)
        dwout_acc_ref[...] = jnp.zeros_like(dwout_acc_ref)
        copy.wait()

    @pl.when(step < FEED_CHUNKS)
    def _():
        gbin_ref[...] = jnp.zeros_like(gbin_ref)

        def one_tile(index, _):
            if planes:
                schedule.tick(step * tiles + index)
            here = pl.ds(pl.multiple_of(index * tile, tile), tile)
            gpre = (dot_nt(gffn_ref[here], wfin_ref[...]) * slope_ref[here].astype(F32)).astype(BF16)
            gpre_ref[here] = gpre
            gbin_ref[0:1] += column_sum(gpre.astype(F32))
            acc_ref[here] += dot_nt(gpre, win_ref[...])
            return 0

        lax.fori_loop(0, tiles, one_tile, 0)
        dwin_ref[...] = dot_nn(low_t_ref[...], gpre_ref[...]).astype(BF16)

    @pl.when(step >= FEED_CHUNKS)
    def _():
        index = step - FEED_CHUNKS
        if planes:
            schedule.tick(tiles * FEED_CHUNKS + index)
        ghid = acc_ref[pl.ds(pl.multiple_of(index * tile, tile), tile)]
        normed = normed_ref[...]
        gvec_ref[0:1] += column_sum(ghid * normed)
        gvec_ref[1:2] += column_sum(ghid)
        gsum = normalize_back(ghid * vec_ref[0:1], normed, inverse_ref[:, 0:1])
        gsum_ref[...] = gsum
        gattn = gsum.astype(BF16)
        gvec_ref[2:3] += column_sum(gattn.astype(F32))
        gcon_ref[...] = dot_nt(gattn, wout_ref[...]).astype(BF16)
        dwout_acc_ref[...] += dot_tn(context_ref[...], gattn)

    @pl.when(step == pl.num_programs(0) - 1)
    def _():
        dwout_ref[...] = dwout_acc_ref[...].astype(BF16)
        if planes:
            schedule.rest()


def feed_backward(planes, gffn, low, gsum, slope, win, wfin, normed, inverse, context, wout, vectors, dwfin, tile):
    tokens, width = low.shape
    hidden = win.shape[1]
    chunk = hidden // FEED_CHUNKS
    any_ = pl.BlockSpec(memory_space=pl.ANY)
    sources, outs, out_shape, scratch = [], [], [], []
    if planes:
        source = dwfin.reshape(planes, 2, 2, 2, -1, width)
        sources = [source]
        outs = [whole(source.shape[4:])]
        out_shape = [jax.ShapeDtypeStruct(source.shape[4:], F32)]
        scratch = scatter_sems(planes, 4)
        for _ in range(4):
            scratch += scatter_scratch(planes, source.shape[4] // 4, width, BF16, True)

    def first(step):
        return jnp.minimum(step, FEED_CHUNKS - 1)

    def then(columns):
        return pl.BlockSpec((tile, columns), lambda i: (jnp.maximum(i - FEED_CHUNKS, 0), 0))

    return pl.pallas_call(
        functools.partial(feed_back_kernel, planes),
        grid=(FEED_CHUNKS + tokens // tile,),
        in_specs=[
            whole(gffn.shape), whole(low.shape), any_,
            pl.BlockSpec((tokens, chunk), lambda i: (0, first(i))),
            pl.BlockSpec((width, chunk), lambda i: (0, first(i))),
            pl.BlockSpec((chunk, width), lambda i: (first(i), 0)),
            then(width), then(BLOCK), then(width), whole(wout.shape), whole(vectors.shape),
        ] + [any_] * len(sources),
        out_specs=[
            pl.BlockSpec((width, chunk), lambda i: (0, first(i))),
            pl.BlockSpec((8, chunk), lambda i: (0, first(i))),
            then(width), then(width), whole((width, width)), whole((8, width)),
        ] + outs,
        out_shape=[
            jax.ShapeDtypeStruct((width, hidden), BF16),
            jax.ShapeDtypeStruct((8, hidden), F32),
            jax.ShapeDtypeStruct((tokens, width), F32),
            jax.ShapeDtypeStruct((tokens, width), BF16),
            jax.ShapeDtypeStruct((width, width), BF16),
            jax.ShapeDtypeStruct((8, width), F32),
        ] + out_shape,
        scratch_shapes=[
            pltpu.VMEM((width, tokens), BF16),
            pltpu.VMEM((tokens, width), F32),
            pltpu.VMEM((tokens, chunk), BF16),
            pltpu.VMEM((width, width), F32),
            pltpu.SemaphoreType.DMA,
        ] + scratch,
        compiler_params=pltpu.CompilerParams(
            vmem_limit_bytes=VMEM_LIMIT,
            **(dict(collective_id=2, has_side_effects=True) if planes else {}),
        ),
        name="feed_backward",
    )(gffn, low, gsum, slope, win, wfin, normed, inverse, context, wout, vectors, *sources)


IN_STEPS = ((0, 2, 8, 12), (0, 5, 12, 16), (1, 8, 16, 20), (2, 12, 20, 23))
OUT_STEPS = (4, 14, 22, 24)
PAIR_STEPS = (0, 1, 6, 10)


def attention_back_kernel(
    planes, pieces, devices,
    q_ref, k_ref, v_ref, gcon_ref, lse_ref, segment_ref, tokens_ref, wq_ref, wk_ref, wv_ref, gsum_hbm,
    gtwo_ref, gbin_ref, gone_ref, *refs,
):
    sources, refs = refs[: 2 if planes else 0], refs[2 if planes else 0 :]
    gtok_hbm, refs = refs[0], refs[1:]
    if planes:
        outs, refs = refs[:4], refs[4:]
    else:
        dw_ref, small_ref, refs = refs[0], refs[1], refs[2:]
    tokens_t_ref, acc_ref, mask_ref, grad_ref, dk_ref, dv_ref, gbqv_ref, sem, *refs = refs
    pair = pl.program_id(0)
    last = pl.num_programs(0) - 1
    count, length = segment_ref.shape[0], segment_ref.shape[2]
    total, width = tokens_ref.shape
    pairs = width // BLOCK
    blocks = length // BLOCK
    offsets, _ = mask_offsets(length)
    tile = 512

    if planes:
        place = Place(planes)
        pair_dw_ref, small_ref = refs[3:5]
        schedule = Schedule(place, refs[:3], refs[5:], count * pairs)
        dwin, dwout = sources
        wide = dwin.shape[5] // 4
        for i in range(4):
            cols = slice(i * wide, (i + 1) * wide)
            schedule.add(
                dwin.at[(slice(None),) * 5 + (cols,)], True, store_to(outs[2], cols=cols), IN_STEPS[i]
            )
        schedule.add(dwout, True, store_to(outs[1]), OUT_STEPS)
        for i in range(pairs):
            def store(value, more, i=i):
                for part in range(3):
                    cols = slice(part * BLOCK, (part + 1) * BLOCK)
                    here = slice(part * width + i * BLOCK, part * width + (i + 1) * BLOCK)
                    store_to(outs[0], cols=here)(value[:, cols], more)

            schedule.add(pair_dw_ref.at[i], False, store, [count * (i + 1) + n for n in PAIR_STEPS])
        schedule.add(
            small_ref.reshape(planes, 2, 2, 2, 8, BLOCK), False, store_to(outs[3]),
            [count * pairs + n for n in PAIR_STEPS],
        )

    @pl.when(pair == 0)
    def _():
        copy = pltpu.make_async_copy(gsum_hbm, acc_ref, sem)
        copy.start()
        if planes:
            place.enter()
        tokens_t_ref[...] = jnp.transpose(tokens_ref[...])
        for seq in range(count):
            fill_masks(mask_ref, seq, segment_ref[seq])
        for index, row in (
            (1, gone_ref[2:3]), (2, gone_ref[0:1]), (3, gone_ref[1:2]), (4, gbin_ref[0:1]),
            (5, gtwo_ref[2:3]), (6, gtwo_ref[0:1]), (7, gtwo_ref[1:2]),
        ):
            small_ref[:, index, :] = collect_vector(row, pieces[index], devices)
        copy.wait()

    def one_seq(seq, _):
        if planes:
            schedule.tick(pair * count + seq)
        base = pl.multiple_of(seq * length, length)
        dk_ref[...] = jnp.zeros_like(dk_ref)
        dv_ref[...] = jnp.zeros_like(dv_ref)
        span = windows(length)
        here = [pl.ds(base + block * BLOCK, BLOCK) for block in range(len(span))]
        reach = [pl.ds(base + low, high - low) for low, high in span]
        queries = [stacked(q_ref[rows]) for rows in here]
        grads = [stacked(gcon_ref[rows]) for rows in here]
        scores = [dot_nt(k_ref[keys], query) for keys, query in zip(reach, queries)]
        gprobs = [dot_nt(v_ref[keys], grad) for keys, grad in zip(reach, grads)]
        probs = [
            jnp.exp(
                score + twice(mask_ref[seq, pl.ds(offsets[block], score.shape[0]), :])
                - lse_ref[seq, pl.ds(pair * blocks + block, 1), :]
            )
            for block, score in enumerate(scores)
        ]
        dots = [jnp.sum(prob * gprob, axis=0, keepdims=True) for prob, gprob in zip(probs, gprobs)]
        gscores = [
            (prob * (gprob - dot_)).astype(BF16) for prob, gprob, dot_ in zip(probs, gprobs, dots)
        ]
        for block, (low, high) in enumerate(span):
            dv_ref[low:high] += dot_nn(probs[block].astype(BF16), grads[block])
            dk_ref[low:high] += dot_nn(gscores[block], queries[block])
            gquery = unstacked_t(dot_tn(k_ref[reach[block]], gscores[block])) * HEAD_DIM ** (-0.5)
            grad_ref[here[block], 0:BLOCK] = gquery.astype(BF16)
        rows = pl.ds(base, length)
        grad_ref[rows, BLOCK : 2 * BLOCK] = dk_ref[...].astype(BF16)
        grad_ref[rows, 2 * BLOCK :] = dv_ref[...].astype(BF16)
        return 0

    lax.fori_loop(0, count, one_seq, 0)
    cols = pl.multiple_of(pair * BLOCK, BLOCK)
    gbqv_ref[:, pl.ds(cols, BLOCK)] = column_sum(grad_ref[:, :BLOCK].astype(F32))
    gbqv_ref[:, pl.ds(width + cols, BLOCK)] = column_sum(grad_ref[:, 2 * BLOCK :].astype(F32))
    dw = dot_nn(tokens_t_ref[...], grad_ref[...])
    if planes:
        for part in range(3):
            here = slice(part * BLOCK, (part + 1) * BLOCK)
            pair_dw_ref[pair, ..., here] = dw[:, here].reshape(planes, 2, 2, 2, -1, BLOCK).astype(BF16)
    else:
        dw_ref[...] = dw.astype(BF16)
    weights = jnp.concatenate([wq_ref[...], wk_ref[...], wv_ref[...]], axis=1)
    for start in range(0, total, tile):
        here = slice(start, start + tile)
        acc_ref[here] += dot_nt(grad_ref[here], weights)

    @pl.when(pair == last)
    def _():
        copy = pltpu.make_async_copy(acc_ref, gtok_hbm, sem)
        copy.start()
        small_ref[:, 0, :] = collect_vector(gbqv_ref[...], pieces[0], devices)
        if planes:
            schedule.rest()
        copy.wait()


def attention_backward(planes, pieces, devices, qkv, gcon, lse, segments, tokens, wqkv, gsum, vectors, grads):
    count, length = segments.shape[0], segments.shape[2]
    total, width = tokens.shape
    pairs = width // BLOCK
    any_ = pl.BlockSpec(memory_space=pl.ANY)

    def part(rows, index):
        return pl.BlockSpec((rows, BLOCK), lambda i: (0, index * pairs + i))

    scratch = [
        pltpu.VMEM((width, total), BF16),
        pltpu.VMEM((total, width), F32),
        pltpu.VMEM((count, mask_offsets(length)[1], BLOCK), F32),
        pltpu.VMEM((total, 3 * BLOCK), BF16),
        pltpu.VMEM((length, BLOCK), F32),
        pltpu.VMEM((length, BLOCK), F32),
        pltpu.VMEM((1, 2 * width), F32),
        pltpu.SemaphoreType.DMA,
    ]
    small = (devices, 8, BLOCK)
    if planes:
        grads = [g.reshape((planes, 2, 2, 2, -1) + g.shape[1:]) for g in grads]
        rows = width // devices
        shards = [(rows, 3 * width), (rows, width), grads[0].shape[4:], (8, BLOCK)]
        outs = [whole(shape) for shape in shards]
        out_shape = [jax.ShapeDtypeStruct(shape, F32) for shape in shards]
        scratch += scatter_sems(planes, 6 + pairs) + [
            pltpu.VMEM((pairs, planes, 2, 2, 2, rows, 3 * BLOCK), BF16),
            pltpu.VMEM(small, F32),
        ]
        for shape in [(rows, grads[0].shape[5] // 4)] * 4 + [(rows, width)]:
            scratch += scatter_scratch(planes, *shape, BF16, True)
        for _ in range(pairs):
            scratch += scatter_scratch(planes, rows, 3 * BLOCK, BF16, False)
        scratch += scatter_scratch(planes, 8, BLOCK, F32, False)
    else:
        grads = []
        outs = [pl.BlockSpec((width, 3 * BLOCK), lambda i: (0, i)), whole(small)]
        out_shape = [jax.ShapeDtypeStruct((width, 3 * width), BF16), jax.ShapeDtypeStruct(small, F32)]
    return pl.pallas_call(
        functools.partial(attention_back_kernel, planes, pieces, devices),
        grid=(pairs,),
        in_specs=[
            part(total, 0), part(total, 1), part(total, 2), part(total, 0),
            whole(lse.shape), whole(segments.shape), whole(tokens.shape),
            part(width, 0), part(width, 1), part(width, 2), any_,
        ] + [whole(v.shape) for v in vectors] + [any_] * len(grads),
        out_specs=[any_] + outs,
        out_shape=[jax.ShapeDtypeStruct((total, width), F32)] + out_shape,
        scratch_shapes=scratch,
        compiler_params=pltpu.CompilerParams(
            vmem_limit_bytes=VMEM_LIMIT,
            **(dict(collective_id=1, has_side_effects=True) if planes else {}),
        ),
        name="attention_backward",
    )(qkv, qkv, qkv, gcon, lse, segments, tokens, wqkv, wqkv, wqkv, gsum, *vectors, *grads)


def shards(
    planes,
    tokens, weight_qkv, bias_qv, weight_out, bias_out, gain_one, shift_one,
    weight_in, bias_in, weight_fin, bias_fin, gain_two, shift_two, segments, cotangent,
):
    small = (bias_qv, bias_out, gain_one, shift_one, bias_in, bias_fin, gain_two, shift_two)
    pieces = tuple(v.shape[0] for v in small)
    joined = jnp.stack([jnp.pad(v, (0, BLOCK - v.shape[0])) for v in small])
    weights = [weight_qkv, joined, weight_out, weight_in, weight_fin]
    if not planes:
        weights = [lax.all_gather(w, AXES, axis=0, tiled=True) for w in weights]
    devices = planes * 8 if planes else weights[1].shape[0] // 8
    segments = segments.reshape(segments.shape[0], 1, segments.shape[1])
    fulls, rest = attention_forward(planes, tokens, segments, weights, pieces)
    wqkv, _, wout, win, wfin = fulls
    qkv, context, lse, vectors, bin_ = rest
    tile, width = min(512, tokens.shape[0]), tokens.shape[1]
    normed, inverse, output, act, slope, gsum_two, gffn, low, gvec_two = feed_forward(
        tokens, context, cotangent, wout, win, wfin, vectors, bin_, tile
    )
    dwfin = fin_grad(act, gffn, width)
    dwin, gbin, gsum_one, gcon, dwout, gvec_one, *fin = feed_backward(
        planes, gffn, low, gsum_two, slope, win, wfin, normed, inverse, context, wout, vectors, dwfin, tile
    )
    gtok, *sums = attention_backward(
        planes, pieces, devices, qkv, gcon, lse, segments, tokens, wqkv, gsum_one,
        (gvec_two, gbin, gvec_one), [dwin, dwout],
    )
    if not planes:
        sums = [
            lax.psum_scatter(g.reshape((devices, -1) + g.shape[-1:]), AXES, scatter_dimension=0).astype(F32)
            for g in (sums[0], dwout, dwin, sums[1], dwfin)
        ]
        sums[0] = sums[0].reshape(sums[0].shape[0], -1, 3, BLOCK).swapaxes(1, 2).reshape(sums[0].shape)
        fin = sums[4:]
    parts = [sums[3][i, :piece] for i, piece in enumerate(pieces)]
    return (
        output, gtok, sums[0], parts[0], sums[1], parts[1], parts[2], parts[3],
        sums[2], parts[4], fin[0], parts[5], parts[6], parts[7],
    )


AXES = ("dp", "inner")


def solution(mesh):
    row, vec = P(AXES, None), P(AXES)
    in_specs = (row, row, vec, row, vec, vec, vec, row, vec, row, vec, vec, vec, row, row)
    out_specs = (row, row, row, vec, row, vec, vec, vec, row, vec, row, vec, vec, vec)
    planes = mesh.shape["dp"] // 4 if mesh.shape["inner"] == 2 and mesh.shape["dp"] == 16 else 0
    return jax.shard_map(
        functools.partial(shards, planes),
        mesh=mesh, in_specs=in_specs, out_specs=out_specs, check_vma=False,
    )
```

```python
import functools

import jax
import jax.numpy as jnp
from jax import lax
from jax.experimental import pallas as pl
from jax.experimental.pallas import tpu as pltpu
from jax.sharding import PartitionSpec as P

HEAD_DIM = 64
BLOCK = 128
EPSILON = 1e-06
NEG_FILL = -1e30
F32 = jnp.float32
BF16 = jnp.bfloat16
VMEM_LIMIT = 60 << 20


def dot(left, right, dims):
    return lax.dot_general(left, right, ((dims[:1], dims[1:]), ((), ())), preferred_element_type=F32)


def dot_nn(left, right):
    return dot(left, right, (1, 0))


def dot_nt(left, right):
    return dot(left, right, (1, 1))


def dot_tn(left, right):
    return dot(left, right, (0, 0))


def windows(length):
    return [
        (max(0, start - BLOCK), min(length, start + 2 * BLOCK))
        for start in range(0, length, BLOCK)
    ]


def mask_offsets(length):
    offsets, total = [], 0
    for low, high in windows(length):
        offsets.append(total)
        total += high - low
    return offsets, total


def fill_masks(mask_ref, seq, segment_row):
    length = segment_row.shape[1]
    columns = jnp.transpose(jnp.broadcast_to(segment_row, (BLOCK, length)))
    offsets, _ = mask_offsets(length)
    for block, (low, high) in enumerate(windows(length)):
        rows = jnp.broadcast_to(
            segment_row[:, block * BLOCK : (block + 1) * BLOCK], (high - low, BLOCK)
        )
        mask_ref[seq, pl.ds(offsets[block], high - low), :] = jnp.where(
            columns[low:high] == rows, 0.0, NEG_FILL
        )


def stacked(pair):
    lane = lax.broadcasted_iota(jnp.int32, pair.shape, 1)
    zero = jnp.zeros_like(pair)
    return jnp.concatenate(
        [jnp.where(lane < HEAD_DIM, pair, zero), jnp.where(lane < HEAD_DIM, zero, pair)], axis=0
    )


def unstacked_t(joined):
    row = lax.broadcasted_iota(jnp.int32, (2 * HEAD_DIM, BLOCK), 0)
    return jnp.transpose(jnp.where(row < HEAD_DIM, joined[:, :BLOCK], joined[:, BLOCK:]))


def twice(mask):
    return jnp.concatenate([mask, mask], axis=1)


def normalize(summed):
    center = summed - jnp.mean(summed, axis=-1, keepdims=True)
    inverse = lax.rsqrt(jnp.mean(center * center, axis=-1, keepdims=True) + EPSILON)
    return (center * inverse, inverse)


def normalize_back(grad_normed, normed, inverse):
    mean_grad = jnp.mean(grad_normed, axis=-1, keepdims=True)
    mean_cross = jnp.mean(grad_normed * normed, axis=-1, keepdims=True)
    return inverse * (grad_normed - mean_grad - normed * mean_cross)


def column_sum(rows):
    return jnp.sum(rows, axis=0, keepdims=True)


def gelu_parts(pre):
    cdf = 0.5 + 0.5 * lax.erf(pre * 0.7071067811865476)
    bell = jnp.exp2((-0.7213475204444817 * pre) * pre)
    return (pre * cdf, cdf + pre * (bell * 0.3989422804014327))


MESH = pl.DeviceIdType.MESH


def when(condition, body):
    if condition is True:
        body()
    else:
        pl.when(condition)(body)


class Place:
    def __init__(self, planes):
        along = lax.axis_index("dp")
        self.planes = planes
        self.y = lax.axis_index("inner")
        self.c = lax.rem(along, 2)
        self.x = lax.rem(lax.div(along, 2), 2)
        self.z = lax.div(along, 4)

    def device(self, z=None, x=None, c=None, y=None):
        z = self.z if z is None else z
        x = self.x if x is None else x
        c = self.c if c is None else c
        return ((z * 2 + x) * 2 + c, self.y if y is None else y)

    @property
    def above(self):
        return self.device(z=jnp.minimum(self.z + 1, self.planes - 1))

    @property
    def below(self):
        return self.device(z=jnp.maximum(self.z - 1, 0))

    @property
    def across(self):
        return self.device(x=1 - self.x)

    @property
    def beside(self):
        return self.device(y=1 - self.y)

    @property
    def partner(self):
        return self.device(c=1 - self.c)

    @property
    def has_above(self):
        return self.z < self.planes - 1

    @property
    def has_below(self):
        return self.z > 0

    @property
    def diagonal(self):
        return self.device(x=1 - self.x, y=1 - self.y)

    def enter(self):
        barrier = pltpu.get_barrier_semaphore()
        planes = [self.device(z=lax.rem(self.z + i, self.planes)) for i in range(1, self.planes)]
        devices = [self.across, self.beside, self.diagonal, self.partner] + planes
        for device in devices:
            pl.semaphore_signal(barrier, inc=1, device_id=device, device_id_type=MESH)
        pl.semaphore_wait(barrier, len(devices))


def half_of(ref, half):
    if half == 2:
        return ref
    width = ref.shape[-1] // 2
    lead = (slice(None),) * (len(ref.shape) - 1)
    return ref.at[lead + (slice(half * width, (half + 1) * width),)]


SENDS = 64


class Gather:
    def __init__(self, place, index, shard, full, send, recv, local):
        self.place, self.index, self.shard, self.full = place, index, shard, full
        self.send, self.recv, self.local = send, recv, local
        self.rows = shard.shape[0]
        self.halves = (0, 1) if full.shape[-1] % (2 * BLOCK) == 0 else (2, None)
        self.slot = 0
        self.draining = False
        self.log = []

    def entry(self, z, x, c, y):
        device = ((z * 2 + x) * 2 + c) * 2 + y
        return self.full.at[pl.ds(pl.multiple_of(device * self.rows, 8), self.rows)]

    def run(self, name, *args):
        self.log.append((name, args))
        getattr(self, name)(*args)

    def push(self, condition, item, half, device, source=None):
        slot = self.slot
        self.slot += 1
        assert slot < SENDS

        def make():
            return pltpu.make_async_remote_copy(
                src_ref=half_of(self.entry(*item) if source is None else source, half),
                dst_ref=half_of(self.entry(*item), half),
                send_sem=self.send.at[self.index, slot],
                recv_sem=self.recv.at[(self.index,) + item + (min(half, 1),)],
                device_id=device,
                device_id_type=MESH,
            )

        if self.draining:
            when(condition, lambda: make().wait_send())
        else:
            when(condition, lambda: make().start())

    def await_item(self, item, half):
        if self.draining:
            return
        ref = half_of(self.entry(*item), half)
        pltpu.make_async_remote_copy(
            src_ref=ref, dst_ref=ref, send_sem=self.send.at[self.index, 0],
            recv_sem=self.recv.at[(self.index,) + item + (min(half, 1),)],
            device_id=self.place.partner, device_id_type=MESH,
        ).wait_recv()

    def own_copy(self):
        p = self.place
        return pltpu.make_async_copy(
            self.shard, self.entry(p.z, p.x, p.c, p.y), self.local.at[self.index]
        )

    def first_z(self):
        p = self.place
        item = (p.z, p.x, p.c, p.y)
        self.push(p.has_above, item, 2, p.above, self.shard)
        self.push(p.has_below, item, 2, p.below, self.shard)
        if not self.draining:
            self.own_copy().start()

    def first_xy(self):
        p = self.place
        item = (p.z, p.x, p.c, p.y)
        for device in (p.across, p.beside, p.partner):
            self.push(True, item, 2, device, self.shard)

    def planes_at(self, distance):
        p = self.place
        if distance == 0:
            return [(True, p.z, None, None)]
        return [
            (p.z >= distance, p.z - distance, p.has_above, p.above),
            (p.z + distance < p.planes, p.z + distance, p.has_below, p.below),
        ]

    def along_z(self, distance):
        p = self.place
        for there, z, more, onward in self.planes_at(distance):
            item = (jnp.clip(z, 0, p.planes - 1), p.x, p.c, p.y)
            if not self.draining:
                when(there, lambda: self.await_item(item, 2))
            self.push(jnp.logical_and(there, more), item, 2, onward)
            for device in (p.across, p.beside, p.partner):
                self.push(there, item, 2, device)

    def across_xy(self, distance):
        p = self.place
        for there, z, _, _ in self.planes_at(distance):
            z = jnp.clip(z, 0, p.planes - 1)
            for half, item, onward in (
                (self.halves[0], (z, 1 - p.x, p.c, p.y), p.beside),
                (self.halves[1], (z, p.x, p.c, 1 - p.y), p.across),
            ):
                if not self.draining:
                    when(there, lambda: self.await_item(item, 2))
                if half is not None:
                    self.push(there, item, half, onward)
                self.push(there, item, 2, p.partner)

    def diagonal(self, distance):
        p = self.place
        for there, z, _, _ in self.planes_at(distance):
            item = (jnp.clip(z, 0, p.planes - 1), 1 - p.x, p.c, 1 - p.y)

            def arrive():
                for half in self.halves:
                    if half is not None:
                        self.await_item(item, half)

            if not self.draining:
                when(there, arrive)
            self.push(there, item, 2, p.partner)

    def finish(self):
        p = self.place
        for z in range(p.planes):
            for x in range(2):
                for y in range(2):
                    self.await_item((z, x, 1 - p.c, y), 2)
        self.own_copy().wait()
        self.draining, self.slot = True, 0
        for name, args in self.log:
            getattr(self, name)(*args)


class Bundles:
    def __init__(self, place, index, shard, full, send, recv, local):
        self.place, self.index, self.shard, self.full = place, index, shard, full
        self.send, self.recv, self.local = send, recv, local

    def copy(self, slot, src, dst, device, arrival=None):
        return pltpu.make_async_remote_copy(
            src_ref=src, dst_ref=dst, send_sem=self.send.at[self.index, slot],
            recv_sem=self.recv.at[self.index, slot if arrival is None else arrival],
            device_id=device, device_id_type=MESH,
        )

    def own_copy(self):
        p = self.place
        return pltpu.make_async_copy(
            self.shard, self.full.at[p.z, p.x, p.c, p.y], self.local.at[self.index]
        )

    def z_copy(self, z):
        p = self.place
        return self.copy(z, self.shard, self.full.at[p.z, p.x, p.c, p.y], p.device(z=z), p.z)

    def z_arrival(self, z):
        p = self.place
        return self.copy(z, self.shard, self.full.at[z, p.x, p.c, p.y], p.device(z=z))

    def bundle(self, step, here):
        p = self.place
        full = self.full
        other = {"across": p.across, "beside": p.beside, "partner": p.partner}
        to, x, y, half = (
            ("across", 0, 0, 2), ("beside", 0, 0, 2), ("partner", 0, 0, 2),
            ("beside", 1, 0, 0), ("across", 0, 1, 1), ("partner", 1, 0, 2), ("partner", 0, 1, 2),
            ("partner", 1, 1, 2),
        )[step]
        c = p.c
        if not here:
            x = 1 - x if to == "across" else x
            y = 1 - y if to == "beside" else y
            c = 1 - c if to == "partner" else c
        ref = half_of(full.at[:, 1 - p.x if x else p.x, c, 1 - p.y if y else p.y], half)
        return self.copy(p.planes + step, ref, ref, other[to])

    def first(self):
        for z in range(self.place.planes):
            when(z != self.place.z, lambda: self.z_copy(z).start())
        self.own_copy().start()

    def move(self, arrived, onward):
        for step in arrived:
            self.bundle(step, False).wait_recv()
        for step in onward:
            self.bundle(step, True).start()

    def after_z(self):
        for z in range(self.place.planes):
            when(z != self.place.z, lambda: self.z_arrival(z).wait_recv())
        self.own_copy().wait()
        self.move((), (0, 1, 2))

    def after_side(self):
        self.move((0, 1), (3, 4, 5, 6))

    def after_diagonal(self):
        self.move((3, 4), (7,))

    def finish(self):
        self.move((2, 5, 6, 7), ())
        for z in range(self.place.planes):
            when(z != self.place.z, lambda: self.z_copy(z).wait_send())
        for step in range(8):
            self.bundle(step, True).wait_send()


class Scatter:
    def __init__(self, place, index, source, held, bufs, sems, store):
        self.place, self.index, self.source, self.store = place, index, source, store
        self.held = source.at[:, :, place.c] if held is None else held
        self.loads = held is not None
        self.from_partner, self.from_square, self.spare, self.from_z = bufs
        self.send, self.recv, self.local = sems
        self.dtype = source.dtype

    def copy(self, slot, src, dst, device, arrival=None):
        return pltpu.make_async_remote_copy(
            src_ref=src, dst_ref=dst, send_sem=self.send.at[self.index, slot],
            recv_sem=self.recv.at[self.index, slot if arrival is None else arrival],
            device_id=device, device_id_type=MESH,
        )

    def own_copy(self):
        return pltpu.make_async_copy(
            self.source.at[:, :, self.place.c], self.held, self.local.at[self.index]
        )

    def partner_copy(self):
        p = self.place
        return self.copy(0, self.source.at[:, :, 1 - p.c], self.from_partner, p.partner)

    def square(self):
        p = self.place
        return ((1 - p.x, 1 - p.y, p.diagonal), (1 - p.x, p.y, p.across), (p.x, 1 - p.y, p.beside))

    def square_copies(self):
        return [
            self.copy(1 + i, self.held.at[:, x, y], self.from_square.at[i], device)
            for i, (x, y, device) in enumerate(self.square())
        ]

    def z_copy(self, z):
        p = self.place
        return self.copy(4 + z, self.spare.at[z], self.from_z.at[p.z], p.device(z=z), 4 + p.z)

    def z_arrival(self, z):
        p = self.place
        return self.copy(4 + z, self.spare.at[z], self.from_z.at[z], p.device(z=z), 4 + z)

    def start(self):
        if self.loads:
            self.own_copy().start()
        self.partner_copy().start()

    def after_partner(self):
        p = self.place
        if self.loads:
            self.own_copy().wait()
        self.partner_copy().wait_recv()

        def add(x, y):
            def one(z, _):
                total = self.held[z, x, y].astype(F32) + self.from_partner[z, x, y].astype(F32)
                self.held[z, x, y] = total.astype(self.dtype)
                return 0

            lax.fori_loop(0, p.planes, one, 0)

        for (x, y, _), copy in zip(self.square(), self.square_copies()):
            add(x, y)
            copy.start()
        add(p.x, p.y)

    def after_square(self):
        p = self.place
        for copy in self.square_copies():
            copy.wait_recv()

        def one(z, _):
            total = self.held[z, p.x, p.y].astype(F32)
            for i in range(3):
                total = total + self.from_square[i, z].astype(F32)
            self.spare[z] = total.astype(self.dtype)
            return 0

        lax.fori_loop(0, p.planes, one, 0)
        for z in range(p.planes):
            when(z != p.z, lambda: self.z_copy(z).start())

    def finish(self):
        p = self.place
        self.store(self.spare[p.z].astype(F32), False)
        for z in range(p.planes):
            def arrive(z=z):
                self.z_arrival(z).wait_recv()
                self.store(self.from_z[z].astype(F32), True)

            when(z != p.z, arrive)
        self.partner_copy().wait_send()
        for copy in self.square_copies():
            copy.wait_send()
        for z in range(p.planes):
            when(z != p.z, lambda: self.z_copy(z).wait_send())


STAGES = ("start", "after_partner", "after_square", "finish")


def scatter_scratch(planes, rows, width, dtype, held):
    return ([pltpu.VMEM((planes, 2, 2, rows, width), dtype)] if held else []) + [
        pltpu.VMEM((planes, 2, 2, rows, width), dtype),
        pltpu.VMEM((3, planes, rows, width), dtype),
        pltpu.VMEM((planes, rows, width), dtype),
        pltpu.VMEM((planes, rows, width), dtype),
    ]


def scatter_sems(planes, number):
    return [
        pltpu.SemaphoreType.DMA((number, 4 + planes)),
        pltpu.SemaphoreType.DMA((number, 4 + planes)),
        pltpu.SemaphoreType.DMA((number,)),
    ]


class Schedule:
    def __init__(self, place, sems, scratch, ticks):
        self.place, self.sems, self.scratch, self.ticks = place, sems, scratch, ticks
        self.count, self.due, self.late = 0, {}, []

    def add(self, source, load, store, steps):
        size = 5 if load else 4
        bufs, self.scratch = self.scratch[:size], self.scratch[size:]
        held, bufs = (bufs[0], bufs[1:]) if load else (None, bufs)
        one = Scatter(self.place, self.count, source, held, bufs, self.sems, store)
        self.count += 1
        for stage, number in zip(STAGES, steps):
            if number < self.ticks:
                self.due.setdefault(number, []).append(getattr(one, stage))
            else:
                self.late.append((number, self.count, getattr(one, stage)))

    def tick(self, now):
        for number, acts in self.due.items():
            @pl.when(now == number)
            def _():
                for act in acts:
                    act()

    def tick_at(self, step, size, index):
        for number, acts in self.due.items():
            if number % size != index:
                continue

            @pl.when(step == number // size)
            def _():
                for act in acts:
                    act()

    def rest(self):
        for _, _, act in sorted(self.late, key=lambda entry: entry[:2]):
            act()


def store_to(out, cols=None, rows=None):
    def store(value, more):
        index = (slice(None) if rows is None else rows, slice(None) if cols is None else cols)
        out[index] = out[index] + value if more else value

    return store


def spread_masks(devices, piece):
    size = devices * piece
    column = lax.broadcasted_iota(jnp.int32, (devices, size), 1)
    start = lax.broadcasted_iota(jnp.int32, (devices, size), 0) * piece
    owner = jnp.logical_and(column >= start, column < start + piece)
    column = lax.broadcasted_iota(jnp.int32, (BLOCK, size), 1)
    number = jnp.floor((column.astype(F32) + 0.5) * (1.0 / piece)).astype(jnp.int32)
    place = column - number * piece == lax.broadcasted_iota(jnp.int32, (BLOCK, size), 0)
    return owner, place.astype(F32)


def spread_vectors(gathered, pieces):
    masks = {piece: spread_masks(gathered.shape[0], piece) for piece in set(pieces)}
    rows = []
    for index, piece in enumerate(pieces):
        owner, place = masks[piece]
        wide = dot_nn(gathered[:, index, :], place.astype(BF16))
        rows.append(jnp.sum(jnp.where(owner, wide, 0.0), axis=0, keepdims=True))
    return rows


def collect_vector(row, piece, devices):
    owner, place = spread_masks(devices, piece)
    wide = jnp.where(owner, row, 0.0)
    high = wide.astype(BF16)
    low = (wide - high.astype(F32)).astype(BF16)
    place = place.astype(BF16)
    return dot_nt(high, place) + dot_nt(low, place)


GATHER_STEPS = (
    (11, 17, 21, 23), (-2, 2, 7, 11), (-1, 4, 11, 15), (0, 8, 15, 19), (4, 12, 19, 22),
)


def attention_kernel(planes, pieces, tokens_ref, segment_ref, *refs):
    shards, refs = refs[:5], refs[5:]
    if planes:
        fulls, refs = refs[:5], refs[5:]
    else:
        fulls = shards
    (
        qkv_ref, context_ref, lse_ref, vectors_ref, bin_ref,
        wqkv_ref, small_ref, bias_ref, mask_ref, load_sem, *sems,
    ) = refs
    length, width = tokens_ref.shape
    count = pl.num_programs(0)
    step = pl.program_id(0)
    pairs = width // BLOCK
    offsets, _ = mask_offsets(length)
    gathers = []
    if planes:
        place = Place(planes)
        gathers = [Gather(place, i, shards[i], fulls[i], *sems[:3]) for i in range(2)]
        cuts = [(2, ()), (3, (slice(None), 0)), (3, (slice(None), 1)), (4, (0,)), (4, (1,))]
        for i, (array, cut) in enumerate(cuts):
            shard, full = shards[array], fulls[array]
            if cut:
                size = shard.shape[len(cut) - 1] // 2
                cut = cut[:-1] + (slice(cut[-1] * size, (cut[-1] + 1) * size),)
                shard, full = shard.at[cut], full.at[(slice(None),) * 4 + cut]
            gathers.append(Bundles(place, i, shard, full, *sems[3:]))
    attn, later = gathers[:2], gathers[2:]
    due = {}
    for gather, steps in zip(later, GATHER_STEPS):
        for number, act in zip(steps, (gather.first, gather.after_z, gather.after_side, gather.after_diagonal)):
            due.setdefault(number, []).append(act)

    def load(index, ref):
        return pltpu.make_async_copy(fulls[index], ref, load_sem.at[index])

    @pl.when(step == 0)
    def _():
        if planes:
            place.enter()
            for gather in attn:
                gather.run("first_z")
                gather.run("first_xy")
            for act in due.get(-4, []):
                act()
        for seq in range(segment_ref.shape[0]):
            fill_masks(mask_ref, seq, segment_ref[seq])
        for distance in range(1, planes + 2 if planes else 0):
            for gather in attn:
                if distance < planes:
                    gather.run("along_z", distance)
            for act in due.get(distance - 4, []) if distance < 4 else ():
                act()
            for gather in attn:
                if distance - 1 < planes:
                    gather.run("across_xy", distance - 1)
                if distance >= 2:
                    gather.run("diagonal", distance - 2)
        for gather in attn:
            gather.finish()
        load(0, wqkv_ref).start()
        load(1, small_ref).start()
        load(1, small_ref).wait()
        small = small_ref[...].astype(F32).reshape(-1, 8, BLOCK)
        bqv, bout, gain_one, shift_one, bin_, bfin, gain_two, shift_two = spread_vectors(small, pieces)
        bias_ref[:, :width] = bqv[:, :width]
        bias_ref[:, width : 2 * width] = jnp.zeros_like(bout)
        bias_ref[:, 2 * width :] = bqv[:, width:]
        bin_ref[...] = bin_
        for row, vector in enumerate((gain_one, shift_one, bfin, gain_two, shift_two, bout)):
            vectors_ref[row : row + 1] = vector
        vectors_ref[6:8] = jnp.zeros((2, width), F32)
        load(0, wqkv_ref).wait()

    for part in range(3):
        cols = slice(part * width, (part + 1) * width)
        joined = dot_nn(tokens_ref[...], wqkv_ref[:, cols]) + bias_ref[:, cols]
        if part == 0:
            joined = joined * HEAD_DIM ** (-0.5)
        qkv_ref[:, cols] = joined.astype(BF16)

    def one_pair(pair, _):
        for number, acts in due.items():
            if number < 0:
                continue

            @pl.when(step * pairs + pair == number)
            def _():
                for act in acts:
                    act()

        def cols(part):
            return pl.ds(pl.multiple_of(part * width + pair * BLOCK, BLOCK), BLOCK)

        reach = windows(length)
        here = [slice(block * BLOCK, (block + 1) * BLOCK) for block in range(len(reach))]
        scores = [
            dot_nt(qkv_ref[low:high, cols(1)], stacked(qkv_ref[rows, cols(0)]))
            + twice(mask_ref[step, pl.ds(offsets[block], high - low), :])
            for block, (rows, (low, high)) in enumerate(zip(here, reach))
        ]
        maxima = [jnp.max(score, axis=0, keepdims=True) for score in scores]
        exponents = [jnp.exp(score - peak) for score, peak in zip(scores, maxima)]
        totals = [jnp.sum(exponent, axis=0, keepdims=True) for exponent in exponents]
        contexts = [
            dot_tn(qkv_ref[low:high, cols(2)], exponent.astype(BF16)) * (1.0 / total)
            for exponent, total, (low, high) in zip(exponents, totals, reach)
        ]
        for block, context in enumerate(contexts):
            context_ref[here[block], cols(0)] = unstacked_t(context).astype(BF16)
            lse_ref[0, pl.ds(pair * len(reach) + block, 1), :] = maxima[block] + jnp.log(totals[block])
        return 0

    lax.fori_loop(0, pairs, one_pair, 0)

    @pl.when(step == count - 1)
    def _():
        for gather in later:
            gather.finish()


def whole(shape):
    return pl.BlockSpec(shape, lambda *_: (0,) * len(shape), pipeline_mode=pl.Buffered(1))


def attention_forward(planes, tokens, segments, weights, pieces):
    count, length = segments.shape[0], segments.shape[2]
    width = tokens.shape[1]
    rows = pl.BlockSpec((length, width), lambda i: (i, 0))
    any_ = pl.BlockSpec(memory_space=pl.ANY)
    lse_rows = (width // BLOCK) * (length // BLOCK)
    hidden = weights[3].shape[-1]
    devices = planes * 8 if planes else weights[1].shape[0] // 8
    gathered = []
    if planes:
        gathered = [(devices * w.shape[0], w.shape[1]) for w in weights[:2]]
        gathered += [(planes, 2, 2, 2) + w.shape for w in weights[2:]]
    sems = []
    if planes:
        sems = [
            pltpu.SemaphoreType.DMA((2, SENDS)),
            pltpu.SemaphoreType.DMA((2, planes, 2, 2, 2, 2)),
            pltpu.SemaphoreType.DMA((2,)),
            pltpu.SemaphoreType.DMA((5, planes + 8)),
            pltpu.SemaphoreType.DMA((5, planes + 8)),
            pltpu.SemaphoreType.DMA((5,)),
        ]
    out = pl.pallas_call(
        functools.partial(attention_kernel, planes, pieces),
        grid=(count,),
        in_specs=[rows, whole(segments.shape)] + [whole(w.shape) if planes else any_ for w in weights],
        out_specs=[any_] * len(gathered) + [
            pl.BlockSpec((length, 3 * width), lambda i: (i, 0)),
            rows,
            pl.BlockSpec((1, lse_rows, 2 * BLOCK), lambda i: (i, 0, 0)),
            whole((8, width)),
            whole((1, hidden)),
        ],
        out_shape=[jax.ShapeDtypeStruct(s, w.dtype) for s, w in zip(gathered, weights)] + [
            jax.ShapeDtypeStruct((count * length, 3 * width), BF16),
            jax.ShapeDtypeStruct((count * length, width), BF16),
            jax.ShapeDtypeStruct((count, lse_rows, 2 * BLOCK), F32),
            jax.ShapeDtypeStruct((8, width), F32),
            jax.ShapeDtypeStruct((1, hidden), F32),
        ],
        scratch_shapes=[
            pltpu.VMEM((width, 3 * width), BF16),
            pltpu.VMEM((devices * 8, BLOCK), BF16),
            pltpu.VMEM((1, 3 * width), F32),
            pltpu.VMEM((count, mask_offsets(length)[1], BLOCK), F32),
            pltpu.SemaphoreType.DMA((2,)),
        ] + sems,
        compiler_params=pltpu.CompilerParams(
            vmem_limit_bytes=VMEM_LIMIT,
            **(dict(collective_id=0, has_side_effects=True) if planes else {}),
        ),
        name="attention_forward",
    )(tokens, segments, *weights)
    fulls = out[: len(gathered)] if planes else weights
    return [f.reshape(-1, f.shape[-1]) for f in fulls], out[len(gathered) :]


def feed_kernel(
    tokens_ref, context_ref, cot_ref, wout_ref, win_ref, wfin_ref, vec_ref, bin_ref,
    normed_ref, inverse_ref, out_ref, act_ref, slope_ref, gsum_ref, gffn_ref, low_ref, gvec_ref,
    hidden_ref,
):
    branch = dot_nn(context_ref[...], wout_ref[...]) + vec_ref[5:6]
    normed, inverse = normalize(tokens_ref[...].astype(F32) + branch)
    normed_ref[...] = normed
    inverse_ref[...] = jnp.broadcast_to(inverse, inverse_ref.shape)
    hidden = normed * vec_ref[0:1] + vec_ref[1:2]
    hidden_ref[...] = hidden
    low_ref[...] = hidden.astype(BF16)
    width = 2 * BLOCK

    def one_chunk(chunk, _):
        cols = pl.ds(pl.multiple_of(chunk * width, width), width)
        pre = dot_nn(low_ref[...], win_ref[:, cols]) + bin_ref[:, cols]
        active, slope = gelu_parts(pre)
        act_ref[:, cols] = active.astype(BF16)
        slope_ref[:, cols] = slope.astype(BF16)
        return 0

    lax.fori_loop(0, win_ref.shape[1] // width, one_chunk, 0, unroll=True)
    branch = dot_nn(act_ref[...], wfin_ref[...]) + vec_ref[2:3]
    normed, inverse = normalize(hidden_ref[...] + branch)
    gain = vec_ref[3:4]
    out_ref[...] = (normed * gain + vec_ref[4:5]).astype(BF16)
    cot = cot_ref[...].astype(F32)
    gsum = normalize_back(cot * gain, normed, inverse)
    gsum_ref[...] = gsum
    gffn = gsum.astype(BF16)
    gffn_ref[...] = gffn

    @pl.when(pl.program_id(0) == 0)
    def _():
        gvec_ref[...] = jnp.zeros_like(gvec_ref)

    gvec_ref[0:1] += column_sum(cot * normed)
    gvec_ref[1:2] += column_sum(cot)
    gvec_ref[2:3] += column_sum(gffn.astype(F32))


def feed_forward(tokens, context, cotangent, wout, win, wfin, vectors, bin_, tile):
    total, width = tokens.shape
    hidden = win.shape[1]
    rows = pl.BlockSpec((tile, width), lambda i: (i, 0))
    wide = pl.BlockSpec((tile, hidden), lambda i: (i, 0))
    return pl.pallas_call(
        feed_kernel,
        grid=(total // tile,),
        in_specs=[rows, rows, rows] + [whole(w.shape) for w in (wout, win, wfin, vectors, bin_)],
        out_specs=[
            rows, pl.BlockSpec((tile, BLOCK), lambda i: (i, 0)), rows, wide, wide, rows, rows, rows,
            pl.BlockSpec((8, width), lambda i: (0, 0)),
        ],
        out_shape=[
            jax.ShapeDtypeStruct((total, width), F32),
            jax.ShapeDtypeStruct((total, BLOCK), F32),
            jax.ShapeDtypeStruct((total, width), BF16),
            jax.ShapeDtypeStruct((total, hidden), BF16),
            jax.ShapeDtypeStruct((total, hidden), BF16),
            jax.ShapeDtypeStruct((total, width), F32),
            jax.ShapeDtypeStruct((total, width), BF16),
            jax.ShapeDtypeStruct((total, width), BF16),
            jax.ShapeDtypeStruct((8, width), F32),
        ],
        scratch_shapes=[pltpu.VMEM((tile, width), F32)],
        compiler_params=pltpu.CompilerParams(vmem_limit_bytes=VMEM_LIMIT),
        name="feed_forward",
    )(tokens, context, cotangent, wout, win, wfin, vectors, bin_)


def fin_grad_kernel(act_ref, gffn_ref, dwfin_ref):
    dwfin_ref[...] = dot_tn(act_ref[...], gffn_ref[...]).astype(BF16)


def fin_grad(act, gffn, chunk):
    tokens, hidden = act.shape
    width = gffn.shape[1]
    return pl.pallas_call(
        fin_grad_kernel,
        grid=(hidden // chunk,),
        in_specs=[pl.BlockSpec((tokens, chunk), lambda i: (0, i)), whole(gffn.shape)],
        out_specs=pl.BlockSpec((chunk, width), lambda i: (i, 0)),
        out_shape=jax.ShapeDtypeStruct((hidden, width), BF16),
        compiler_params=pltpu.CompilerParams(vmem_limit_bytes=VMEM_LIMIT),
        name="fin_grad",
    )(act, gffn)


FIN_STEPS = ((0, 2, 9, 14), (0, 6, 13, 18), (1, 10, 18, 23), (2, 14, 23, 27))
FEED_CHUNKS = 6


def feed_back_kernel(
    planes, gffn_ref, low_ref, gsum_hbm, slope_ref, win_ref, wfin_ref,
    normed_ref, inverse_ref, context_ref, wout_ref, vec_ref, *refs,
):
    sources, refs = refs[: 1 if planes else 0], refs[1 if planes else 0 :]
    (
        dwin_ref, gbin_ref, gsum_ref, gcon_ref, dwout_ref, gvec_ref, *outs,
    ), refs = refs[: 7 if planes else 6], refs[7 if planes else 6 :]
    low_t_ref, acc_ref, gpre_ref, dwout_acc_ref, sem, *refs = refs
    step = pl.program_id(0)
    tokens = gffn_ref.shape[0]
    tile = normed_ref.shape[0]
    tiles = tokens // tile
    if planes:
        place = Place(planes)
        schedule = Schedule(place, refs[:3], refs[3:], tiles * (FEED_CHUNKS + 1))
        rows = sources[0].shape[4] // 4
        for i in range(4):
            here = slice(i * rows, (i + 1) * rows)
            schedule.add(
                sources[0].at[(slice(None),) * 4 + (here,)], True, store_to(outs[0], rows=here), FIN_STEPS[i]
            )

    @pl.when(step == 0)
    def _():
        copy = pltpu.make_async_copy(gsum_hbm, acc_ref, sem)
        copy.start()
        if planes:
            place.enter()
        low_t_ref[...] = jnp.transpose(low_ref[...])
        gvec_ref[...] = jnp.zeros_like(gvec_ref)
        dwout_acc_ref[...] = jnp.zeros_like(dwout_acc_ref)
        copy.wait()

    @pl.when(step < FEED_CHUNKS)
    def _():
        gbin_ref[...] = jnp.zeros_like(gbin_ref)

        for index in range(tiles):
            if planes:
                schedule.tick_at(step, tiles, index)
            here = slice(index * tile, (index + 1) * tile)
            gpre = (dot_nt(gffn_ref[here], wfin_ref[...]) * slope_ref[here].astype(F32)).astype(BF16)
            gpre_ref[here] = gpre
            gbin_ref[0:1] += column_sum(gpre.astype(F32))
            acc_ref[here] += dot_nt(gpre, win_ref[...])
        dwin_ref[...] = dot_nn(low_t_ref[...], gpre_ref[...]).astype(BF16)

    @pl.when(step >= FEED_CHUNKS)
    def _():
        index = step - FEED_CHUNKS
        if planes:
            schedule.tick(tiles * FEED_CHUNKS + index)
        ghid = acc_ref[pl.ds(pl.multiple_of(index * tile, tile), tile)]
        normed = normed_ref[...]
        gvec_ref[0:1] += column_sum(ghid * normed)
        gvec_ref[1:2] += column_sum(ghid)
        gsum = normalize_back(ghid * vec_ref[0:1], normed, inverse_ref[:, 0:1])
        gsum_ref[...] = gsum
        gattn = gsum.astype(BF16)
        gvec_ref[2:3] += column_sum(gattn.astype(F32))
        gcon_ref[...] = dot_nt(gattn, wout_ref[...]).astype(BF16)
        dwout_acc_ref[...] += dot_tn(context_ref[...], gattn)

    @pl.when(step == pl.num_programs(0) - 1)
    def _():
        dwout_ref[...] = dwout_acc_ref[...].astype(BF16)
        if planes:
            schedule.rest()


def feed_backward(planes, gffn, low, gsum, slope, win, wfin, normed, inverse, context, wout, vectors, dwfin, tile):
    tokens, width = low.shape
    hidden = win.shape[1]
    chunk = hidden // FEED_CHUNKS
    any_ = pl.BlockSpec(memory_space=pl.ANY)
    sources, outs, out_shape, scratch = [], [], [], []
    if planes:
        source = dwfin.reshape(planes, 2, 2, 2, -1, width)
        sources = [source]
        outs = [whole(source.shape[4:])]
        out_shape = [jax.ShapeDtypeStruct(source.shape[4:], F32)]
        scratch = scatter_sems(planes, 4)
        for _ in range(4):
            scratch += scatter_scratch(planes, source.shape[4] // 4, width, BF16, True)

    def first(step):
        return jnp.minimum(step, FEED_CHUNKS - 1)

    def then(columns):
        return pl.BlockSpec((tile, columns), lambda i: (jnp.maximum(i - FEED_CHUNKS, 0), 0))

    return pl.pallas_call(
        functools.partial(feed_back_kernel, planes),
        grid=(FEED_CHUNKS + tokens // tile,),
        in_specs=[
            whole(gffn.shape), whole(low.shape), any_,
            pl.BlockSpec((tokens, chunk), lambda i: (0, first(i))),
            pl.BlockSpec((width, chunk), lambda i: (0, first(i))),
            pl.BlockSpec((chunk, width), lambda i: (first(i), 0)),
            then(width), then(BLOCK), then(width), whole(wout.shape), whole(vectors.shape),
        ] + [any_] * len(sources),
        out_specs=[
            pl.BlockSpec((width, chunk), lambda i: (0, first(i))),
            pl.BlockSpec((8, chunk), lambda i: (0, first(i))),
            then(width), then(width), whole((width, width)), whole((8, width)),
        ] + outs,
        out_shape=[
            jax.ShapeDtypeStruct((width, hidden), BF16),
            jax.ShapeDtypeStruct((8, hidden), F32),
            jax.ShapeDtypeStruct((tokens, width), F32),
            jax.ShapeDtypeStruct((tokens, width), BF16),
            jax.ShapeDtypeStruct((width, width), BF16),
            jax.ShapeDtypeStruct((8, width), F32),
        ] + out_shape,
        scratch_shapes=[
            pltpu.VMEM((width, tokens), BF16),
            pltpu.VMEM((tokens, width), F32),
            pltpu.VMEM((tokens, chunk), BF16),
            pltpu.VMEM((width, width), F32),
            pltpu.SemaphoreType.DMA,
        ] + scratch,
        compiler_params=pltpu.CompilerParams(
            vmem_limit_bytes=VMEM_LIMIT,
            **(dict(collective_id=2, has_side_effects=True) if planes else {}),
        ),
        name="feed_backward",
    )(gffn, low, gsum, slope, win, wfin, normed, inverse, context, wout, vectors, *sources)


IN_STEPS = ((0, 2, 8, 12), (0, 5, 12, 16), (1, 8, 16, 20), (2, 12, 20, 23))
OUT_STEPS = (4, 14, 22, 24)
PAIR_STEPS = (0, 1, 6, 10)


def attention_back_kernel(
    planes, pieces, devices,
    q_ref, k_ref, v_ref, gcon_ref, lse_ref, segment_ref, tokens_ref, wq_ref, wk_ref, wv_ref, gsum_hbm,
    gtwo_ref, gbin_ref, gone_ref, *refs,
):
    sources, refs = refs[: 2 if planes else 0], refs[2 if planes else 0 :]
    gtok_hbm, refs = refs[0], refs[1:]
    if planes:
        outs, refs = refs[:4], refs[4:]
    else:
        dw_ref, small_ref, refs = refs[0], refs[1], refs[2:]
    tokens_t_ref, acc_ref, mask_ref, grad_ref, dk_ref, dv_ref, gbqv_ref, sem, *refs = refs
    pair = pl.program_id(0)
    last = pl.num_programs(0) - 1
    count, length = segment_ref.shape[0], segment_ref.shape[2]
    total, width = tokens_ref.shape
    pairs = width // BLOCK
    blocks = length // BLOCK
    offsets, _ = mask_offsets(length)
    tile = 512

    if planes:
        place = Place(planes)
        pair_dw_ref, small_ref = refs[3:5]
        schedule = Schedule(place, refs[:3], refs[5:], count * pairs)
        dwin, dwout = sources
        wide = dwin.shape[5] // 4
        for i in range(4):
            cols = slice(i * wide, (i + 1) * wide)
            schedule.add(
                dwin.at[(slice(None),) * 5 + (cols,)], True, store_to(outs[2], cols=cols), IN_STEPS[i]
            )
        schedule.add(dwout, True, store_to(outs[1]), OUT_STEPS)
        for i in range(pairs):
            def store(value, more, i=i):
                for part in range(3):
                    cols = slice(part * BLOCK, (part + 1) * BLOCK)
                    here = slice(part * width + i * BLOCK, part * width + (i + 1) * BLOCK)
                    store_to(outs[0], cols=here)(value[:, cols], more)

            schedule.add(pair_dw_ref.at[i], False, store, [count * (i + 1) + n for n in PAIR_STEPS])
        schedule.add(
            small_ref.reshape(planes, 2, 2, 2, 8, BLOCK), False, store_to(outs[3]),
            [count * pairs + n for n in PAIR_STEPS],
        )

    @pl.when(pair == 0)
    def _():
        copy = pltpu.make_async_copy(gsum_hbm, acc_ref, sem)
        copy.start()
        if planes:
            place.enter()
        tokens_t_ref[...] = jnp.transpose(tokens_ref[...])
        for seq in range(count):
            fill_masks(mask_ref, seq, segment_ref[seq])
        for index, row in (
            (1, gone_ref[2:3]), (2, gone_ref[0:1]), (3, gone_ref[1:2]), (4, gbin_ref[0:1]),
            (5, gtwo_ref[2:3]), (6, gtwo_ref[0:1]), (7, gtwo_ref[1:2]),
        ):
            small_ref[:, index, :] = collect_vector(row, pieces[index], devices)
        copy.wait()

    def one_seq(seq, _):
        if planes:
            schedule.tick(pair * count + seq)
        base = pl.multiple_of(seq * length, length)
        dk_ref[...] = jnp.zeros_like(dk_ref)
        dv_ref[...] = jnp.zeros_like(dv_ref)
        span = windows(length)
        here = [pl.ds(base + block * BLOCK, BLOCK) for block in range(len(span))]
        reach = [pl.ds(base + low, high - low) for low, high in span]
        queries = [stacked(q_ref[rows]) for rows in here]
        grads = [stacked(gcon_ref[rows]) for rows in here]
        scores = [dot_nt(k_ref[keys], query) for keys, query in zip(reach, queries)]
        gprobs = [dot_nt(v_ref[keys], grad) for keys, grad in zip(reach, grads)]
        probs = [
            jnp.exp(
                score + twice(mask_ref[seq, pl.ds(offsets[block], score.shape[0]), :])
                - lse_ref[seq, pl.ds(pair * blocks + block, 1), :]
            )
            for block, score in enumerate(scores)
        ]
        dots = [jnp.sum(prob * gprob, axis=0, keepdims=True) for prob, gprob in zip(probs, gprobs)]
        gscores = [
            (prob * (gprob - dot_)).astype(BF16) for prob, gprob, dot_ in zip(probs, gprobs, dots)
        ]
        for block, (low, high) in enumerate(span):
            dv_ref[low:high] += dot_nn(probs[block].astype(BF16), grads[block])
            dk_ref[low:high] += dot_nn(gscores[block], queries[block])
            gquery = unstacked_t(dot_tn(k_ref[reach[block]], gscores[block])) * HEAD_DIM ** (-0.5)
            grad_ref[here[block], 0:BLOCK] = gquery.astype(BF16)
        rows = pl.ds(base, length)
        grad_ref[rows, BLOCK : 2 * BLOCK] = dk_ref[...].astype(BF16)
        grad_ref[rows, 2 * BLOCK :] = dv_ref[...].astype(BF16)
        return 0

    lax.fori_loop(0, count, one_seq, 0)
    cols = pl.multiple_of(pair * BLOCK, BLOCK)
    gbqv_ref[:, pl.ds(cols, BLOCK)] = column_sum(grad_ref[:, :BLOCK].astype(F32))
    gbqv_ref[:, pl.ds(width + cols, BLOCK)] = column_sum(grad_ref[:, 2 * BLOCK :].astype(F32))
    dw = dot_nn(tokens_t_ref[...], grad_ref[...])
    if planes:
        for part in range(3):
            here = slice(part * BLOCK, (part + 1) * BLOCK)
            pair_dw_ref[pair, ..., here] = dw[:, here].reshape(planes, 2, 2, 2, -1, BLOCK).astype(BF16)
    else:
        dw_ref[...] = dw.astype(BF16)
    weights = jnp.concatenate([wq_ref[...], wk_ref[...], wv_ref[...]], axis=1)
    for start in range(0, total, tile):
        here = slice(start, start + tile)
        acc_ref[here] += dot_nt(grad_ref[here], weights)

    @pl.when(pair == last)
    def _():
        copy = pltpu.make_async_copy(acc_ref, gtok_hbm, sem)
        copy.start()
        small_ref[:, 0, :] = collect_vector(gbqv_ref[...], pieces[0], devices)
        if planes:
            schedule.rest()
        copy.wait()


def attention_backward(planes, pieces, devices, qkv, gcon, lse, segments, tokens, wqkv, gsum, vectors, grads):
    count, length = segments.shape[0], segments.shape[2]
    total, width = tokens.shape
    pairs = width // BLOCK
    any_ = pl.BlockSpec(memory_space=pl.ANY)

    def part(rows, index):
        return pl.BlockSpec((rows, BLOCK), lambda i: (0, index * pairs + i))

    scratch = [
        pltpu.VMEM((width, total), BF16),
        pltpu.VMEM((total, width), F32),
        pltpu.VMEM((count, mask_offsets(length)[1], BLOCK), F32),
        pltpu.VMEM((total, 3 * BLOCK), BF16),
        pltpu.VMEM((length, BLOCK), F32),
        pltpu.VMEM((length, BLOCK), F32),
        pltpu.VMEM((1, 2 * width), F32),
        pltpu.SemaphoreType.DMA,
    ]
    small = (devices, 8, BLOCK)
    if planes:
        grads = [g.reshape((planes, 2, 2, 2, -1) + g.shape[1:]) for g in grads]
        rows = width // devices
        shards = [(rows, 3 * width), (rows, width), grads[0].shape[4:], (8, BLOCK)]
        outs = [whole(shape) for shape in shards]
        out_shape = [jax.ShapeDtypeStruct(shape, F32) for shape in shards]
        scratch += scatter_sems(planes, 6 + pairs) + [
            pltpu.VMEM((pairs, planes, 2, 2, 2, rows, 3 * BLOCK), BF16),
            pltpu.VMEM(small, F32),
        ]
        for shape in [(rows, grads[0].shape[5] // 4)] * 4 + [(rows, width)]:
            scratch += scatter_scratch(planes, *shape, BF16, True)
        for _ in range(pairs):
            scratch += scatter_scratch(planes, rows, 3 * BLOCK, BF16, False)
        scratch += scatter_scratch(planes, 8, BLOCK, F32, False)
    else:
        grads = []
        outs = [pl.BlockSpec((width, 3 * BLOCK), lambda i: (0, i)), whole(small)]
        out_shape = [jax.ShapeDtypeStruct((width, 3 * width), BF16), jax.ShapeDtypeStruct(small, F32)]
    return pl.pallas_call(
        functools.partial(attention_back_kernel, planes, pieces, devices),
        grid=(pairs,),
        in_specs=[
            part(total, 0), part(total, 1), part(total, 2), part(total, 0),
            whole(lse.shape), whole(segments.shape), whole(tokens.shape),
            part(width, 0), part(width, 1), part(width, 2), any_,
        ] + [whole(v.shape) for v in vectors] + [any_] * len(grads),
        out_specs=[any_] + outs,
        out_shape=[jax.ShapeDtypeStruct((total, width), F32)] + out_shape,
        scratch_shapes=scratch,
        compiler_params=pltpu.CompilerParams(
            vmem_limit_bytes=VMEM_LIMIT,
            **(dict(collective_id=1, has_side_effects=True) if planes else {}),
        ),
        name="attention_backward",
    )(qkv, qkv, qkv, gcon, lse, segments, tokens, wqkv, wqkv, wqkv, gsum, *vectors, *grads)


def shards(
    planes,
    tokens, weight_qkv, bias_qv, weight_out, bias_out, gain_one, shift_one,
    weight_in, bias_in, weight_fin, bias_fin, gain_two, shift_two, segments, cotangent,
):
    small = (bias_qv, bias_out, gain_one, shift_one, bias_in, bias_fin, gain_two, shift_two)
    pieces = tuple(v.shape[0] for v in small)
    joined = jnp.stack([jnp.pad(v, (0, BLOCK - v.shape[0])) for v in small])
    weights = [weight_qkv, joined, weight_out, weight_in, weight_fin]
    if not planes:
        weights = [lax.all_gather(w, AXES, axis=0, tiled=True) for w in weights]
    devices = planes * 8 if planes else weights[1].shape[0] // 8
    segments = segments.reshape(segments.shape[0], 1, segments.shape[1])
    fulls, rest = attention_forward(planes, tokens, segments, weights, pieces)
    wqkv, _, wout, win, wfin = fulls
    qkv, context, lse, vectors, bin_ = rest
    tile, width = min(512, tokens.shape[0]), tokens.shape[1]
    normed, inverse, output, act, slope, gsum_two, gffn, low, gvec_two = feed_forward(
        tokens, context, cotangent, wout, win, wfin, vectors, bin_, tile
    )
    dwfin = fin_grad(act, gffn, width)
    dwin, gbin, gsum_one, gcon, dwout, gvec_one, *fin = feed_backward(
        planes, gffn, low, gsum_two, slope, win, wfin, normed, inverse, context, wout, vectors, dwfin, tile
    )
    gtok, *sums = attention_backward(
        planes, pieces, devices, qkv, gcon, lse, segments, tokens, wqkv, gsum_one,
        (gvec_two, gbin, gvec_one), [dwin, dwout],
    )
    if not planes:
        sums = [
            lax.psum_scatter(g.reshape((devices, -1) + g.shape[-1:]), AXES, scatter_dimension=0).astype(F32)
            for g in (sums[0], dwout, dwin, sums[1], dwfin)
        ]
        sums[0] = sums[0].reshape(sums[0].shape[0], -1, 3, BLOCK).swapaxes(1, 2).reshape(sums[0].shape)
        fin = sums[4:]
    parts = [sums[3][i, :piece] for i, piece in enumerate(pieces)]
    return (
        output, gtok, sums[0], parts[0], sums[1], parts[1], parts[2], parts[3],
        sums[2], parts[4], fin[0], parts[5], parts[6], parts[7],
    )


AXES = ("dp", "inner")


def solution(mesh):
    row, vec = P(AXES, None), P(AXES)
    in_specs = (row, row, vec, row, vec, vec, vec, row, vec, row, vec, vec, vec, row, row)
    out_specs = (row, row, row, vec, row, vec, vec, vec, row, vec, row, vec, vec, vec)
    planes = mesh.shape["dp"] // 4 if mesh.shape["inner"] == 2 and mesh.shape["dp"] == 16 else 0
    return jax.shard_map(
        functools.partial(shards, planes),
        mesh=mesh, in_specs=in_specs, out_specs=out_specs, check_vma=False,
    )
```
